32 devices in a mesh: dp: 8 (over y, x, core), tensor: 4 (over z).
Axes of the slice: x: 2, y: 2, z: 4, core: 2. Of those that a mesh axis runs over, the one named last changes fastest.
Arguments:
- tokens: bfloat16 [4096, 1024], P(('dp', 'tensor')), may hold values from -6 to 6
- attn_gain: bfloat16 [1024], replicated, may hold values from 0.099609375 to 1.8984375
- ffn_gain: bfloat16 [1024], replicated, may hold values from 0.099609375 to 1.8984375
- w_qkv: bfloat16 [3, 1024, 1024], P(None, None, 'tensor'), may hold values from -0.1875 to 0.1875
- w_out: bfloat16 [1024, 1024], P('tensor'), may hold values from -0.1875 to 0.1875
- w_gateup: bfloat16 [2, 1024, 4096], P(None, None, 'tensor'), may hold values from -0.1875 to 0.1875
- w_down: bfloat16 [4096, 1024], P('tensor'), may hold values from -0.09375 to 0.09375
- variate_bias: float32 [2, 16], P(None, 'tensor'), may hold values from -4 to 4
- adapter_down: bfloat16 [16, 2, 16, 1024], P('dp'), may hold values from -0.1875 to 0.1875
- adapter_up: bfloat16 [16, 2, 16, 1024], P('dp', None, None, 'tensor'), may hold values from -1.5 to 1.5
- owner_table: int32 [16], replicated, may hold values from 0 to 15, each once
- lengths: int32 [8, 4], P('dp'), may hold values from 1 to 256, 512 in all within a row
- adapter_ids: int32 [8, 4], P('dp'), may hold values from 0 to 15
- page_counts: int32 [8, 4], P('dp'), may hold values from 1 to 8, 20 in all within a row
- page_table: int32 [8, 32], P('dp'), may hold values from 0 to 255, as said below
- cache_pool: bfloat16 [256, 128, 2, 1024], P('dp', None, None, 'tensor'), may hold values from -500 to 500
Outputs:
- output: bfloat16 [4096, 1024], P(('dp', 'tensor'))
The draws below stay inside these ranges and needn't reach their ends.
Inputs may be any that keep to these rules, and one draw needn't show every extreme that they name: owner_table is a permutation: adapter a is row owner_table[a] of adapter_down and adapter_up. `page_table`: every pool page is named exactly once; page p lies on home p // 32; the 32 pages of one row lie 4 to a home on 8 distinct homes.
All inputs are finite; a program needn't handle non-finite values.
Results may differ from the reference program's by a relative error of at most 0.0085.
The reference program's roundings to bfloat16 on the way (of `normed`, `low_rank`, `query`, `weights`, `attn_mix`, `ffn_in` and `hidden`) count: a program that leaves them out, or rounds other values in their place, can miss the bound.
Values may be sent and summed in bfloat16 or wider, within the bound.
No kernel may reach another device: no remote copies, remote signals or barrier semaphores. Data moves between devices by JAX's collectives and lax.ppermute only.
A program may use at most 192 MiB of HBM per device.

```python
import math
import jax
import jax.numpy as jnp
import numpy as np
from jax import lax

D = 1024
H = 16
HD = 64
FF = 4096
R = 16
ADAPTERS = 16
TOK_DEV = 512
REQ_DEV = 4
MOSTLEN = 256
PAGE = 128
PAGES_REQ = 8
PAGES_DEV = 32
LIVE_DEV = 20
POOL_DEV = 32
POOL = 256
TOKENS = 4096
VARLEN = 160
N_DP = 8


def draw_page_table(key, part):
    slot_cap = max(1, PAGES_DEV // N_DP)
    home_count = PAGES_DEV // slot_cap
    key_offsets, key_slots = jax.random.split(key)
    offsets = jax.random.permutation(key_offsets, N_DP)[:home_count].astype(jnp.int32)
    device_ids = jnp.arange(N_DP, dtype=jnp.int32)[:, None]
    page_slots = jnp.arange(PAGES_DEV, dtype=jnp.int32)[None, :]
    home_ids = (device_ids + offsets[page_slots // slot_cap]) % N_DP
    slot_perms = jax.vmap(lambda sub_key: jax.random.permutation(sub_key, POOL_DEV).astype(jnp.int32))(jax.random.split(key_slots, N_DP))
    local_ids = slot_perms[home_ids, jnp.broadcast_to(page_slots, home_ids.shape)]
    return (home_ids * POOL_DEV + local_ids).astype(jnp.int32)


def draw_cache_pool(key, part):
    shape = (POOL, PAGE, 2, H * HD)
    key_base = jax.random.fold_in(key, 0)
    base = jnp.clip(jax.random.normal(key_base, shape, jnp.float32), -4.0, 4.0)
    return base.astype(jnp.bfloat16)


def touch_ends(values, rng, least, high):
    longest = values.shape.index(max(values.shape))
    spots = []
    for shift in (0, 1):
        where = [jax.random.randint(jax.random.fold_in(rng, axis), (), 0, length) for axis, length in enumerate(values.shape)]
        where[longest] = (where[longest] + shift) % values.shape[longest]
        spots.append(tuple(where))
    return values.at[spots[0]].set(least).at[spots[1]].set(high)


def levels(stream_key, dims, pieces, low, largest):
    def one(dim, blocks):
        heights = jax.random.uniform(jax.random.fold_in(jax.random.fold_in(stream_key, 6), dim), (blocks,), jnp.float32, low / len(pieces), largest / len(pieces))
        return jnp.repeat(jnp.exp(heights), dims[dim] // blocks).reshape((-1,) + (1,) * (len(dims) - dim - 1))

    level = one(*pieces[0])
    for cut in pieces[1:]:
        level = level * one(*cut)
    return level


def rank_bounds(amount, slope):
    loads = [(1 << 20) // math.isqrt(grade ** slope) + 1 for grade in range(1, amount + 1)]
    scale = 1 + sum(loads) // (1 << 30)
    return np.cumsum(np.array([max(1, weight // scale) for weight in loads]))


def ranked_ids(stream_key, shape, number_of, slope):
    grid = rank_bounds(number_of, slope)
    pick = jax.random.randint(jax.random.fold_in(stream_key, 1), shape, 0, int(grid[number_of - 1]))
    rank = jnp.searchsorted(jnp.asarray(grid, jnp.int32), pick, side="right")
    return jax.random.permutation(jax.random.fold_in(stream_key, 2), number_of)[rank].astype(jnp.int32)


def profile(number_of, total, most, skew):
    weights = [(1 << 20) // math.isqrt(grade ** skew) + 1 for grade in range(2, number_of + 1)]
    spare, given = total - most - (number_of - 1), [1] * (number_of - 1)
    while spare > 0:
        free = [i for i in range(number_of - 1) if given[i] < most]
        pool, left = sum([weights[i] for i in free]), spare
        for i in free:
            addition = min(most - given[i], max(1, left * weights[i] // pool), spare)
            given[i] = given[i] + addition
            spare = spare - addition
    return np.array([most] + given)


def ragged(own_key, amount, total, most, skew):
    if amount == 2:
        one = jax.random.randint(own_key, (), max(1, total - most), min(most, total - 1) + 1)
        return jnp.stack([one, total - one])
    sizes = jnp.asarray(profile(amount, total, most, skew), jnp.int32)
    twos = (amount - 1) // 2
    source_of, receiver = sizes[1:1 + 2 * twos:2], sizes[2:2 + 2 * twos:2]
    slack = jnp.minimum(source_of - 1, most - receiver)
    passed = jax.random.randint(jax.random.fold_in(own_key, 1), (twos,), 0, 1 << 20) % (slack + 1)
    sizes = sizes.at[1:1 + 2 * twos:2].set(source_of - passed).at[2:2 + 2 * twos:2].set(receiver + passed)
    return sizes[jax.random.permutation(jax.random.fold_in(own_key, 2), amount)]


def scatter_about(own_key, shape, width, most, cuts=(), held_as=jnp.bfloat16):
    values = width * jax.random.normal(own_key, shape, jnp.float32)
    if cuts:
        values = values * levels(own_key, shape, cuts, -0.22, 0.18)
    return jnp.clip(values, -most, most).astype(held_as)


def setup_inputs(seed: int = 0) -> dict:
    arg_keys = jax.random.split(jax.random.key(seed), 17)
    tokens = scatter_about(arg_keys[0], (TOKENS, D), 1.0, 6.0, ((0, 32),))
    attn_gain = jnp.clip(1.0 + 0.18 * jax.random.normal(arg_keys[1], (D,), jnp.float32), 0.099609375, 1.8984375).astype(jnp.bfloat16)
    ffn_gain = jnp.clip(1.0 + 0.18 * jax.random.normal(arg_keys[2], (D,), jnp.float32), 0.099609375, 1.8984375).astype(jnp.bfloat16)
    w_qkv = scatter_about(arg_keys[3], (3, D, H * HD), D ** -0.5, 0.1875, ((2, 4),))
    w_out = scatter_about(arg_keys[4], (H * HD, D), (H * HD) ** -0.5, 0.1875, ((0, 4),))
    w_gateup = scatter_about(arg_keys[5], (2, D, FF), D ** -0.5, 0.1875, ((2, 4),))
    w_down = scatter_about(arg_keys[6], (FF, D), FF ** -0.5, 0.09375, ((0, 4),))
    variate_bias = scatter_about(arg_keys[7], (2, H), 1.5, 4.0, ((1, 4),), jnp.float32)
    adapter_down = scatter_about(arg_keys[8], (ADAPTERS, 2, R, D), D ** -0.5, 0.1875, ((0, 8),))
    adapter_up = scatter_about(arg_keys[9], (ADAPTERS, 2, R, H * HD), R ** -0.5, 1.5, ((0, 8), (3, 4)))
    owner_table = jax.random.permutation(arg_keys[10], ADAPTERS).astype(jnp.int32)
    lengths = jax.vmap(lambda own: ragged(own, REQ_DEV, TOK_DEV, MOSTLEN, 2))(jax.random.split(arg_keys[11], N_DP)).reshape((N_DP, REQ_DEV)).astype(jnp.int32)
    adapter_ids = touch_ends(ranked_ids(arg_keys[12], (N_DP, REQ_DEV), ADAPTERS, 2), jax.random.fold_in(arg_keys[12], 3), 0, ADAPTERS - 1).astype(jnp.int32)
    page_counts = jax.vmap(lambda own: ragged(own, REQ_DEV, LIVE_DEV, PAGES_REQ, 1))(jax.random.split(arg_keys[13], N_DP)).reshape((N_DP, REQ_DEV)).astype(jnp.int32)
    page_table = draw_page_table(jax.random.fold_in(arg_keys[16], 71), 0)
    cache_pool = draw_cache_pool(jax.random.fold_in(arg_keys[16], 71), 0)
    return {"tokens": tokens, "attn_gain": attn_gain, "ffn_gain": ffn_gain, "w_qkv": w_qkv, "w_out": w_out, "w_gateup": w_gateup, "w_down": w_down, "variate_bias": variate_bias, "adapter_down": adapter_down, "adapter_up": adapter_up, "owner_table": owner_table, "lengths": lengths, "adapter_ids": adapter_ids, "page_counts": page_counts, "page_table": page_table, "cache_pool": cache_pool}


def normalize(values, gain):
    values = values.astype(jnp.float32)
    inv_scale = lax.rsqrt(lax.optimization_barrier(jnp.mean(values * values, axis=-1, keepdims=True)) + 1e-05)
    return values * inv_scale * gain.astype(jnp.float32)

def rotary(values, time_pos):
    half_dim = values.shape[-1] // 2
    frequency = 10000.0 ** (-2.0 * jnp.arange(half_dim, dtype=jnp.float32) / values.shape[-1])
    angles = time_pos.astype(jnp.float32)[:, None] * frequency[None, :]
    cosine = jnp.cos(angles)[:, None, :]
    sine_part = jnp.sin(angles)[:, None, :]
    first_half = values[..., :half_dim]
    second_half = values[..., half_dim:]
    return jnp.concatenate([first_half * cosine - second_half * sine_part, first_half * sine_part + second_half * cosine], axis=-1)

def token_layout(req_lens, live_counts, page_len, tok_total):
    end_pos = jnp.cumsum(req_lens, dtype=jnp.int32)
    starts = end_pos - req_lens
    tok_index = jnp.arange(tok_total, dtype=jnp.int32)
    request = lax.optimization_barrier(jnp.sum((tok_index[:, None] >= end_pos[None, :]).astype(jnp.int32), axis=1, dtype=jnp.int32))
    onehot = request[:, None] == jnp.arange(req_lens.shape[0], dtype=jnp.int32)[None, :]
    first_pos = lax.optimization_barrier(jnp.sum(jnp.where(onehot, starts[None, :], 0), axis=1, dtype=jnp.int32))
    cached = lax.optimization_barrier(jnp.sum(jnp.where(onehot, live_counts[None, :], 0), axis=1, dtype=jnp.int32))
    return (request, onehot, cached * page_len + tok_index - first_pos)

def cache_layout(live_counts, page_len, pages_req):
    slot_index = jnp.arange(live_counts.shape[0] * pages_req * page_len, dtype=jnp.int32)
    page_no = slot_index // page_len
    request = page_no // pages_req
    within = page_no % pages_req
    onehot = request[:, None] == jnp.arange(live_counts.shape[0], dtype=jnp.int32)[None, :]
    limit = lax.optimization_barrier(jnp.sum(jnp.where(onehot, live_counts[None, :], 0), axis=1, dtype=jnp.int32))
    return (request, within * page_len + slot_index % page_len, within < limit)

def attend(query, all_keys, all_values, query_req, query_pos, key_req, key_pos, key_live, var_bias):
    scores = jnp.einsum('thd,khd->htk', query.astype(jnp.float32), all_keys.astype(jnp.float32)) * query.shape[-1] ** (-0.5)
    same_var = query_pos[:, None] // VARLEN == key_pos[None, :] // VARLEN
    scores = scores + jnp.where(same_var[None], var_bias[0][:, None, None], var_bias[1][:, None, None])
    allowed = key_live[None, :] & (key_req[None, :] == query_req[:, None]) & (key_pos[None, :] <= query_pos[:, None])
    scores = jnp.where(allowed[None], scores, -jnp.inf)
    row_max = lax.optimization_barrier(jnp.max(scores, axis=-1, keepdims=True))
    weights = jnp.exp(scores - row_max)
    weights = (weights / lax.optimization_barrier(jnp.sum(weights, axis=-1, keepdims=True))).astype(jnp.bfloat16)
    return jnp.einsum('htk,khd->thd', weights.astype(jnp.float32), all_values.astype(jnp.float32))

def reference(tokens, attn_gain, ffn_gain, w_qkv, w_out, w_gateup, w_down, variate_bias, adapter_down, adapter_up, owner_table, lengths, adapter_ids, page_counts, page_table, cache_pool):

    def one_group(group_idx):
        rows_in = lax.dynamic_slice_in_dim(tokens, group_idx * TOK_DEV, TOK_DEV, 0)
        live_counts = page_counts[group_idx]
        request, onehot, position = token_layout(lengths[group_idx], live_counts, PAGE, TOK_DEV)
        normed = normalize(rows_in, attn_gain).astype(jnp.bfloat16)
        projected = jnp.einsum('td,kde->kte', normed.astype(jnp.float32), w_qkv.astype(jnp.float32))
        slot_ids = owner_table[adapter_ids[group_idx]]
        down_sel = adapter_down[slot_ids].astype(jnp.float32)
        up_sel = adapter_up[slot_ids].astype(jnp.float32)
        member = onehot.astype(jnp.float32)
        lowall = jnp.einsum('td,rkcd->rtkc', normed.astype(jnp.float32), down_sel)
        low_rank = jnp.einsum('rtkc,tr->tkc', lowall, member).astype(jnp.bfloat16)
        spread = jnp.transpose(member)[:, :, None, None] * low_rank.astype(jnp.float32)
        delta_proj = jnp.einsum('rtkc,rkce->kte', spread, up_sel)
        time_pos = position % VARLEN
        query = rotary((projected[0] + delta_proj[0]).reshape(TOK_DEV, H, HD), time_pos).astype(jnp.bfloat16)
        new_keys = rotary(projected[1].reshape(TOK_DEV, H, HD), time_pos).astype(jnp.bfloat16)
        new_values = (projected[2] + delta_proj[1]).reshape(TOK_DEV, H, HD).astype(jnp.bfloat16)
        cached = cache_pool[page_table[group_idx]]
        all_keys = jnp.concatenate([cached[:, :, 0].reshape(PAGES_DEV * PAGE, H, HD), new_keys], axis=0)
        all_values = jnp.concatenate([cached[:, :, 1].reshape(PAGES_DEV * PAGE, H, HD), new_values], axis=0)
        cache_req, cache_pos, cache_live = cache_layout(live_counts, PAGE, PAGES_REQ)
        key_req = jnp.concatenate([cache_req, request])
        key_pos = jnp.concatenate([cache_pos, position])
        key_live = jnp.concatenate([cache_live, jnp.ones((TOK_DEV,), dtype=bool)])
        attn_mix = attend(query, all_keys, all_values, request, position, key_req, key_pos, key_live, variate_bias).reshape(TOK_DEV, H * HD).astype(jnp.bfloat16)
        residual = rows_in.astype(jnp.float32) + jnp.dot(attn_mix, w_out, preferred_element_type=jnp.float32)
        ffn_in = normalize(residual, ffn_gain).astype(jnp.bfloat16)
        gate_up = jnp.einsum('td,kdf->ktf', ffn_in.astype(jnp.float32), w_gateup.astype(jnp.float32))
        hidden = (jax.nn.silu(gate_up[0]) * gate_up[1]).astype(jnp.bfloat16)
        return (residual + jnp.dot(hidden, w_down, preferred_element_type=jnp.float32)).astype(jnp.bfloat16)
    result = lax.map(one_group, jnp.arange(N_DP, dtype=jnp.int32))
    return result.reshape(N_DP * TOK_DEV, D)
```

```python
import functools

import jax
import jax.numpy as jnp
from jax import lax
from jax.experimental import pallas as pl
from jax.experimental.pallas import tpu as pltpu
from jax.sharding import PartitionSpec as P

HD = 64
PAGES_REQ = 8
VARLEN = 160
TILE = 64
KCH = 128
BF = jnp.bfloat16
F32 = jnp.float32
NEG = -1e30


def normalize(values, gain):
    values = values.astype(F32)
    inv_scale = lax.rsqrt(jnp.mean(values * values, axis=-1, keepdims=True) + 1e-05)
    return values * inv_scale * gain.astype(F32)


def rotary(values, time_pos):
    half_dim = values.shape[-1] // 2
    frequency = 10000.0 ** (-2.0 * jnp.arange(half_dim, dtype=F32) / values.shape[-1])
    angles = time_pos.astype(F32)[:, None] * frequency[None, :]
    cosine = jnp.cos(angles)[:, None, :]
    sine_part = jnp.sin(angles)[:, None, :]
    first_half = values[..., :half_dim]
    second_half = values[..., half_dim:]
    return jnp.concatenate(
        [
            first_half * cosine - second_half * sine_part,
            first_half * sine_part + second_half * cosine,
        ],
        axis=-1,
    )


def token_layout(req_lens, live_counts, page_len, tok_total):
    end_pos = jnp.cumsum(req_lens, dtype=jnp.int32)
    starts = end_pos - req_lens
    tok_index = jnp.arange(tok_total, dtype=jnp.int32)
    request = jnp.sum(
        (tok_index[:, None] >= end_pos[None, :]).astype(jnp.int32), axis=1, dtype=jnp.int32
    )
    onehot = request[:, None] == jnp.arange(req_lens.shape[0], dtype=jnp.int32)[None, :]
    first_pos = jnp.sum(jnp.where(onehot, starts[None, :], 0), axis=1, dtype=jnp.int32)
    cached = jnp.sum(jnp.where(onehot, live_counts[None, :], 0), axis=1, dtype=jnp.int32)
    return (onehot, cached * page_len + tok_index - first_pos)


def want_kernel(n_dp, cap, pool_dev, me_ref, table_ref, want_ref, pos_ref, count):
    me = me_ref[0]
    slots = table_ref.shape[1]

    def clear(g, carry):
        count[g] = 0
        for j in range(n_dp * cap):
            want_ref[g, j] = 0
        return carry

    lax.fori_loop(0, n_dp, clear, 0)

    def place(p, carry):
        page = table_ref[0, p]
        home = page // pool_dev
        rank = count[home]
        count[home] = rank + 1
        want_ref[me, home * cap + rank] = page - home * pool_dev
        pos_ref[p] = jnp.bitwise_xor(home, me) * cap + rank
        return carry

    lax.fori_loop(0, slots, place, 0)


def want(me, page_table, n_dp, cap, pool_dev):
    smem = pl.BlockSpec(memory_space=pltpu.SMEM)
    return pl.pallas_call(
        functools.partial(want_kernel, n_dp, cap, pool_dev),
        out_shape=(
            jax.ShapeDtypeStruct((n_dp, n_dp * cap), jnp.int32),
            jax.ShapeDtypeStruct((page_table.shape[1],), jnp.int32),
        ),
        in_specs=[smem, smem],
        out_specs=(smem, smem),
        scratch_shapes=[pltpu.SMEM((n_dp,), jnp.int32)],
        name="want_pages",
    )(me, page_table)


def pick_kernel(n_dp, cap, me_ref, asked_ref, pool_ref, *rest):
    outs, (buf, sem_in, sem_out) = rest[:n_dp], rest[n_dp:]
    me = me_ref[0]
    copies = []
    for d in range(n_dp - 1, -1, -1):
        partner = jnp.bitwise_xor(me, d)
        for k in range(cap):
            page = asked_ref[partner, me * cap + k]
            copy = pltpu.make_async_copy(pool_ref.at[page], buf.at[d, k], sem_in.at[d, k])
            copy.start()
            copies.append(copy)
    done = []
    for i, d in enumerate(range(n_dp - 1, -1, -1)):
        for k in range(cap):
            copies[i * cap + k].wait()
        copy = pltpu.make_async_copy(buf.at[d], outs[d], sem_out.at[d])
        copy.start()
        done.append(copy)
    for copy in done:
        copy.wait()


def pick(me, asked, pool, n_dp, cap):
    smem = pl.BlockSpec(memory_space=pltpu.SMEM)
    hbm = pl.BlockSpec(memory_space=pl.ANY)
    shape = (cap,) + pool.shape[1:]
    return pl.pallas_call(
        functools.partial(pick_kernel, n_dp, cap),
        out_shape=[jax.ShapeDtypeStruct(shape, pool.dtype)] * n_dp,
        in_specs=[smem, smem, hbm],
        out_specs=[hbm] * n_dp,
        scratch_shapes=[
            pltpu.VMEM((n_dp,) + shape, pool.dtype),
            pltpu.SemaphoreType.DMA((n_dp, cap)),
            pltpu.SemaphoreType.DMA((n_dp,)),
        ],
        name="pick_pages",
    )(me, asked, pool)


def split_kernel(n_in, cap, *refs):
    ins, (k_ref, v_ref), (buf, sem) = refs[:n_in], refs[n_in : n_in + 2], refs[n_in + 2 :]
    page_len = k_ref.shape[1]
    copies = []
    for d in range(n_in):
        copy = pltpu.make_async_copy(ins[d], buf.at[d], sem.at[d])
        copy.start()
        copies.append(copy)
    row = lax.broadcasted_iota(jnp.int32, (2 * page_len, 2 * page_len), 0)
    col = lax.broadcasted_iota(jnp.int32, (2 * page_len, 2 * page_len), 1)
    src = jnp.where(row < page_len, 2 * row, 2 * row - (2 * page_len - 1))
    choose = (col == src).astype(F32).astype(BF)
    for d in range(n_in):
        copies[d].wait()
        for k in range(cap):
            page = buf[d, k].reshape(2 * page_len, buf.shape[-1])
            both = jnp.dot(choose, page, preferred_element_type=F32).astype(BF)
            k_ref[d * cap + k] = both[:page_len]
            v_ref[d * cap + k] = both[page_len:]


def split(pages):
    n_in = len(pages)
    cap, page_len, _, width = pages[0].shape
    out = jax.ShapeDtypeStruct((n_in * cap, page_len, width), BF)
    return pl.pallas_call(
        functools.partial(split_kernel, n_in, cap),
        out_shape=(out, out),
        in_specs=[pl.BlockSpec(memory_space=pl.ANY)] * n_in,
        out_specs=(pl.BlockSpec(memory_space=pltpu.VMEM),) * 2,
        scratch_shapes=[
            pltpu.VMEM((n_in,) + pages[0].shape, BF),
            pltpu.SemaphoreType.DMA((n_in,)),
        ],
        compiler_params=pltpu.CompilerParams(vmem_limit_bytes=40 << 20),
        name="split_pages",
    )(*pages)


def attend_kernel(
    first, stride, n_tiles, heads,
    lens_ref, counts_ref, pos_ref, bias_ref,
    q_ref, kn_ref, vn_ref, kc_ref, vc_ref, out_ref,
    qbd, sbuf, same, diff,
):
    page_len = kc_ref.shape[1]
    width = q_ref.shape[1]
    rows = heads * TILE
    n_req = lens_ref.shape[1]
    pair = 2 * HD if heads > 1 else HD
    n_pair = width // pair
    per = pair // HD
    prow = per * TILE
    lane = lax.broadcasted_iota(jnp.int32, (1, width), 1)
    tile_row = lax.broadcasted_iota(jnp.int32, (TILE, 1), 0)
    for h in range(heads):
        delta = bias_ref[0, h] - bias_ref[1, h]
        diff[h * TILE : (h + 1) * TILE, :] = jnp.full((TILE, KCH), 1.0, F32) * delta

    def variate(position):
        return jnp.floor((position.astype(F32) + 0.5) * (1.0 / VARLEN))

    def tile_body(t, carry):
        row0 = pl.multiple_of(first + t * stride, TILE)
        qt = q_ref[pl.ds(row0, TILE), :]
        for h in range(heads):
            mine = (lane >= h * HD) & (lane < (h + 1) * HD)
            qbd[h * TILE : (h + 1) * TILE, :] = jnp.where(mine, qt.astype(F32), 0.0).astype(BF)

        def req_body(r, start):
            length = lens_ref[0, r]
            end = start + length
            live = counts_ref[0, r]

            @pl.when((start < row0 + TILE) & (end > row0))
            def _():
                row = row0 + tile_row
                qvar = variate(live * page_len + row - start)
                for h in range(heads):
                    same[h * TILE : (h + 1) * TILE, :] = jnp.broadcast_to(qvar, (TILE, KCH))
                first_var = (live * page_len) // VARLEN

                def scores(keys):
                    return lax.dot_general(
                        qbd[...], keys, (((1,), (1,)), ((), ())), preferred_element_type=F32
                    )

                key_lane = lax.broadcasted_iota(jnp.int32, (1, KCH), 1)

                def biased(s, key_pos):
                    return s + jnp.where(same[...] == variate(key_pos), diff[...], 0.0)

                def page_scores(j, top):
                    s = scores(kc_ref[pos_ref[r * PAGES_REQ + j]])
                    sbuf[j] = s
                    return jnp.maximum(top, s)

                def page_scores_biased(j, top):
                    s = biased(
                        scores(kc_ref[pos_ref[r * PAGES_REQ + j]]), j * page_len + key_lane
                    )
                    sbuf[j] = s
                    return jnp.maximum(top, s)

                plain = jnp.minimum((first_var * VARLEN) // page_len, live)
                top = jnp.full((rows, KCH), NEG, F32)
                top = lax.fori_loop(0, plain, page_scores, top)
                top = lax.fori_loop(plain, live, page_scores_biased, top)

                c0 = jnp.maximum(start, 0) // KCH
                c1 = (row0 + TILE - 1) // KCH + 1

                def new_scores(c, top):
                    base = pl.multiple_of(c * KCH, KCH)
                    key_row = base + key_lane
                    s = biased(
                        scores(kn_ref[pl.ds(base, KCH), :]), live * page_len + key_row - start
                    )
                    query_row = row0 + jnp.bitwise_and(
                        lax.broadcasted_iota(jnp.int32, (rows, KCH), 0), TILE - 1
                    )
                    s = jnp.where((key_row <= query_row) & (key_row >= start), s, NEG)
                    sbuf[live + c - c0] = s
                    return jnp.maximum(top, s)

                top = lax.fori_loop(c0, c1, new_scores, top)
                peak = jnp.max(top, axis=1, keepdims=True)
                total_chunks = live + c1 - c0

                def weigh(j, total):
                    p = jnp.exp(sbuf[j] - peak)
                    sbuf[j] = p
                    return total + p

                total = lax.fori_loop(0, total_chunks, weigh, jnp.zeros((rows, KCH), F32))
                inverse = 1.0 / jnp.sum(total, axis=1, keepdims=True)

                def mix(w, values, acc):
                    return tuple(
                        acc[a]
                        + jnp.dot(
                            w[a * prow : (a + 1) * prow],
                            values[:, a * pair : (a + 1) * pair],
                            preferred_element_type=F32,
                        )
                        for a in range(n_pair)
                    )

                def page_mix(j, acc):
                    w = (sbuf[j] * inverse).astype(BF)
                    return mix(w, vc_ref[pos_ref[r * PAGES_REQ + j]], acc)

                def new_mix(c, acc):
                    base = pl.multiple_of(c * KCH, KCH)
                    w = (sbuf[live + c - c0] * inverse).astype(BF)
                    return mix(w, vn_ref[pl.ds(base, KCH), :], acc)

                acc = tuple(jnp.zeros((prow, pair), F32) for _ in range(n_pair))
                acc = lax.fori_loop(0, live, page_mix, acc)
                acc = lax.fori_loop(c0, c1, new_mix, acc)
                inside = (row >= start) & (row < end)
                pair_lane = lax.broadcasted_iota(jnp.int32, (1, pair), 1)
                for a in range(n_pair):
                    o = acc[a][:TILE]
                    for b in range(1, per):
                        o = jnp.where(pair_lane >= b * HD, acc[a][b * TILE : (b + 1) * TILE], o)
                    dst = (pl.ds(pl.multiple_of(t * TILE, TILE), TILE), slice(a * pair, (a + 1) * pair))
                    before = out_ref[dst]
                    out_ref[dst] = jnp.where(inside, o, before.astype(F32)).astype(BF)

            return end

        lax.fori_loop(0, n_req, req_body, 0)
        return carry

    out_ref[...] = jnp.zeros_like(out_ref)
    lax.fori_loop(0, n_tiles, tile_body, 0)


def attend(chunk, n_chunk, lens, counts, pos, bias, q, kn, vn, kc, vc, owners):
    heads = bias.shape[1]
    rows = q.shape[0]
    span = rows // owners // n_chunk
    per_owner = span // TILE
    stride = rows // owners if per_owner == 1 else TILE
    smem = pl.BlockSpec(memory_space=pltpu.SMEM)
    vmem = pl.BlockSpec(memory_space=pltpu.VMEM)
    n_tiles = rows // n_chunk // TILE
    n_new = 2 + 2 * PAGES_REQ * kc.shape[1] // (PAGES_REQ * KCH)
    return pl.pallas_call(
        functools.partial(attend_kernel, chunk * TILE, stride, n_tiles, heads),
        out_shape=jax.ShapeDtypeStruct((rows // n_chunk, q.shape[1]), BF),
        in_specs=[smem] * 4 + [vmem] * 5,
        out_specs=vmem,
        scratch_shapes=[
            pltpu.VMEM((heads * TILE, q.shape[1]), BF),
            pltpu.VMEM((PAGES_REQ + rows // KCH, heads * TILE, KCH), F32),
            pltpu.VMEM((heads * TILE, KCH), F32),
            pltpu.VMEM((heads * TILE, KCH), F32),
        ],
        compiler_params=pltpu.CompilerParams(vmem_limit_bytes=40 << 20),
        name="attend",
    )(lens, counts, pos, bias, q, kn, vn, kc, vc)


def shift(value, axis, n, k):
    return lax.ppermute(value, axis, [(i, (i + k) % n) for i in range(n)])


def per_device(
    tokens,
    attn_gain,
    ffn_gain,
    w_qkv,
    w_out,
    w_gateup,
    w_down,
    variate_bias,
    adapter_down,
    adapter_up,
    owner_table,
    lengths,
    adapter_ids,
    page_counts,
    page_table,
    cache_pool,
):
    n_tp = lax.axis_size("tensor")
    n_dp = lax.axis_size("dp")
    tp = lax.axis_index("tensor")
    dp = lax.axis_index("dp")
    me = dp.astype(jnp.int32).reshape(1)
    row_count, d_model = tokens.shape
    tok_total = row_count * n_tp
    width = w_out.shape[0]
    heads = width // HD
    page_len = cache_pool.shape[1]
    cap = max(1, page_table.shape[1] // n_dp)
    far_first = [k for k in range(1, n_tp)]

    wanted, buffer_pos = want(me, page_table, n_dp, cap, cache_pool.shape[0])
    asked = lax.psum(wanted, "dp")
    picked = pick(me, asked, cache_pool, n_dp, cap)
    order = sorted(range(1, n_dp), key=lambda d: (-bin(d >> 1).count("1"), d))
    fetched = {0: picked[0]}
    for d in order:
        fetched[d] = lax.ppermute(picked[d], "dp", [(i, i ^ d) for i in range(n_dp)])

    token_blocks = [tokens] + [shift(tokens, "tensor", n_tp, k) for k in far_first]
    all_tokens = jnp.zeros((n_tp, row_count, d_model), BF)
    for k, block in enumerate(token_blocks):
        all_tokens = lax.dynamic_update_index_in_dim(all_tokens, block, (tp - k) % n_tp, 0)
    normed = normalize(all_tokens.reshape(tok_total, d_model), attn_gain).astype(BF)

    half = width // 2
    core = dp % 2
    own_half = lax.dynamic_slice_in_dim(w_out, core * half, half, 0)
    halves = jnp.stack([shift(own_half, "tensor", n_tp, k) for k in far_first])
    twins = lax.ppermute(halves, "dp", [(i, i ^ 1) for i in range(n_dp)])
    w_rest = jnp.where(
        core == 0,
        jnp.concatenate([halves, twins], axis=1),
        jnp.concatenate([twins, halves], axis=1),
    )
    w_whole = jnp.concatenate([w_out[None], w_rest], axis=0).reshape(n_tp * width, d_model)

    dd = d_model // n_tp
    down_part = lax.dynamic_slice_in_dim(adapter_down, tp * dd, dd, 3)
    slot_ids = jnp.take(owner_table, adapter_ids[0])
    down_all = lax.all_gather(down_part, "dp", axis=0, tiled=True)
    up_all = lax.all_gather(adapter_up, "dp", axis=0, tiled=True)
    select = (
        slot_ids[:, None] == jnp.arange(down_all.shape[0], dtype=jnp.int32)[None, :]
    ).astype(BF)
    down_named = jnp.einsum("rn,nkcd->rkcd", select, down_all, preferred_element_type=F32).astype(BF)
    up_sel = jnp.einsum("rn,nkce->rkce", select, up_all, preferred_element_type=F32).astype(BF)
    down_sel = lax.all_gather(down_named, "tensor", axis=3, tiled=True)

    live_counts = page_counts[0]
    onehot, position = token_layout(lengths[0], live_counts, page_len, tok_total)
    member = onehot.astype(F32)
    projected = jnp.einsum("td,kde->kte", normed, w_qkv, preferred_element_type=F32)
    lowall = jnp.einsum("td,rkcd->rtkc", normed, down_sel, preferred_element_type=F32)
    low_rank = jnp.einsum(
        "rtkc,tr->tkc", lowall, member, precision=lax.Precision.HIGHEST
    ).astype(BF)
    spread = (jnp.transpose(member)[:, :, None, None] * low_rank.astype(F32)).astype(BF)
    delta_proj = jnp.einsum("rtkc,rkce->kte", spread, up_sel, preferred_element_type=F32)
    time_pos = position % VARLEN
    query = rotary((projected[0] + delta_proj[0]).reshape(tok_total, heads, HD), time_pos)
    query = (query.astype(BF) * BF(HD ** -0.5)).reshape(tok_total, width)
    new_keys = rotary(projected[1].reshape(tok_total, heads, HD), time_pos)
    new_keys = new_keys.astype(BF).reshape(tok_total, width)
    new_values = (projected[2] + delta_proj[1]).astype(BF)

    keys, values = split([fetched[d] for d in range(n_dp)])

    n_chunk = max(1, row_count // TILE) if row_count % TILE == 0 else 1
    sub = row_count // n_chunk
    outs = []
    for c in range(n_chunk):
        mix = attend(
            c, n_chunk, lengths, page_counts, buffer_pos, variate_bias,
            query, new_keys, new_values, keys, values, n_tp,
        )
        mixes = jnp.concatenate([mix] + [shift(mix, "tensor", n_tp, k) for k in far_first], axis=1)
        base = all_tokens[:, c * sub : (c + 1) * sub].reshape(n_tp * sub, d_model)
        residual = base.astype(F32) + jnp.dot(mixes, w_whole, preferred_element_type=F32)
        ffn_in = normalize(residual, ffn_gain).astype(BF)
        gate_up = jnp.einsum("td,kdf->ktf", ffn_in, w_gateup, preferred_element_type=F32)
        hidden = (jax.nn.silu(gate_up[0]) * gate_up[1]).astype(BF)
        down = jnp.dot(hidden, w_down, preferred_element_type=F32).reshape(n_tp, sub, d_model)
        total = lax.dynamic_index_in_dim(down, tp, 0, False)
        total = total + lax.dynamic_index_in_dim(
            residual.reshape(n_tp, sub, d_model), tp, 0, False
        )
        down = down.astype(BF)
        for k in far_first:
            piece = lax.dynamic_index_in_dim(down, (tp + k) % n_tp, 0, False)
            total = total + shift(piece, "tensor", n_tp, k).astype(F32)
        outs.append(total.astype(BF))
    return jnp.concatenate(outs, axis=0)


def solution(mesh):
    return jax.shard_map(
        per_device,
        mesh=mesh,
        in_specs=(
            P(("dp", "tensor"), None),
            P(),
            P(),
            P(None, None, "tensor"),
            P("tensor", None),
            P(None, None, "tensor"),
            P("tensor", None),
            P(None, "tensor"),
            P("dp", None, None, None),
            P("dp", None, None, "tensor"),
            P(),
            P("dp", None),
            P("dp", None),
            P("dp", None),
            P("dp", None),
            P("dp", None, None, "tensor"),
        ),
        out_specs=P(("dp", "tensor"), None),
        check_vma=False,
    )
```

```python
import functools

import jax
import jax.numpy as jnp
from jax import lax
from jax.experimental import pallas as pl
from jax.experimental.pallas import tpu as pltpu
from jax.sharding import PartitionSpec as P

HD = 64
PAGES_REQ = 8
VARLEN = 160
TILE = 128
KCH = 128
BLK = 4
CHUNK = 64
BF = jnp.bfloat16
F32 = jnp.float32
NEG = -1e30


def normalize(values, gain):
    values = values.astype(F32)
    inv_scale = lax.rsqrt(jnp.mean(values * values, axis=-1, keepdims=True) + 1e-05)
    return values * inv_scale * gain.astype(F32)


def rotary(values, time_pos):
    half_dim = values.shape[-1] // 2
    frequency = 10000.0 ** (-2.0 * jnp.arange(half_dim, dtype=F32) / values.shape[-1])
    angles = time_pos.astype(F32)[:, None] * frequency[None, :]
    cosine = jnp.cos(angles)[:, None, :]
    sine_part = jnp.sin(angles)[:, None, :]
    first_half = values[..., :half_dim]
    second_half = values[..., half_dim:]
    return jnp.concatenate(
        [
            first_half * cosine - second_half * sine_part,
            first_half * sine_part + second_half * cosine,
        ],
        axis=-1,
    )


def token_layout(req_lens, live_counts, page_len, tok_total):
    end_pos = jnp.cumsum(req_lens, dtype=jnp.int32)
    starts = end_pos - req_lens
    tok_index = jnp.arange(tok_total, dtype=jnp.int32)
    request = jnp.sum(
        (tok_index[:, None] >= end_pos[None, :]).astype(jnp.int32), axis=1, dtype=jnp.int32
    )
    onehot = request[:, None] == jnp.arange(req_lens.shape[0], dtype=jnp.int32)[None, :]
    first_pos = jnp.sum(jnp.where(onehot, starts[None, :], 0), axis=1, dtype=jnp.int32)
    cached = jnp.sum(jnp.where(onehot, live_counts[None, :], 0), axis=1, dtype=jnp.int32)
    return (onehot, cached * page_len + tok_index - first_pos)


def want_kernel(n_dp, cap, pool_dev, me_ref, table_ref, want_ref, pos_ref, count):
    me = me_ref[0]
    slots = table_ref.shape[1]

    def clear(g, carry):
        count[g] = 0
        for j in range(n_dp * cap):
            want_ref[g, j] = 0
        return carry

    lax.fori_loop(0, n_dp, clear, 0)

    def place(p, carry):
        page = table_ref[0, p]
        home = page // pool_dev
        rank = count[home]
        count[home] = rank + 1
        want_ref[me, home * cap + rank] = page - home * pool_dev
        pos_ref[p] = home * cap + rank
        return carry

    lax.fori_loop(0, slots, place, 0)


def want(me, page_table, n_dp, cap, pool_dev):
    smem = pl.BlockSpec(memory_space=pltpu.SMEM)
    return pl.pallas_call(
        functools.partial(want_kernel, n_dp, cap, pool_dev),
        out_shape=(
            jax.ShapeDtypeStruct((n_dp, n_dp * cap), jnp.int32),
            jax.ShapeDtypeStruct((page_table.shape[1],), jnp.int32),
        ),
        in_specs=[smem, smem],
        out_specs=(smem, smem),
        scratch_shapes=[pltpu.SMEM((n_dp,), jnp.int32)],
        name="want_pages",
    )(me, page_table)


def pick_kernel(n_dp, cap, me_ref, asked_ref, pool_ref, *rest):
    n_out = len(rest) - 3
    outs, (buf, sem_in, sem_out) = rest[:n_out], rest[n_out:]
    lanes = outs[0].shape[-1]
    me = me_ref[0]
    copies = []
    for g in range(n_dp):
        for k in range(cap):
            page = asked_ref[g, me * cap + k]
            copy = pltpu.make_async_copy(pool_ref.at[page], buf.at[g, k], sem_in.at[g, k])
            copy.start()
            copies.append(copy)
    done = []
    for g in range(n_dp):
        for k in range(cap):
            copies[g * cap + k].wait()
        for a in range(n_out):
            copy = pltpu.make_async_copy(
                buf.at[g, :, :, :, pl.ds(a * lanes, lanes)], outs[a].at[g], sem_out.at[a, g]
            )
            copy.start()
            done.append(copy)
    for copy in done:
        copy.wait()


def pick(me, asked, pool, n_dp, cap, lanes):
    smem = pl.BlockSpec(memory_space=pltpu.SMEM)
    hbm = pl.BlockSpec(memory_space=pl.ANY)
    n_out = pool.shape[-1] // lanes
    shape = (n_dp, cap) + pool.shape[1:-1]
    return pl.pallas_call(
        functools.partial(pick_kernel, n_dp, cap),
        out_shape=[jax.ShapeDtypeStruct(shape + (lanes,), pool.dtype)] * n_out,
        in_specs=[smem, smem, hbm],
        out_specs=[hbm] * n_out,
        scratch_shapes=[
            pltpu.VMEM(shape + pool.shape[-1:], pool.dtype),
            pltpu.SemaphoreType.DMA((n_dp, cap)),
            pltpu.SemaphoreType.DMA((n_out, n_dp)),
        ],
        name="pick_pages",
    )(me, asked, pool)


def attend_kernel(
    group, per, lens_ref, counts_ref, pos_ref, bias_ref,
    q_ref, kn_ref, vn_ref, raw_ref, out_ref,
    kc, vc, knp, vnp, qbd, info, sbuf, wbuf, obuf,
):
    page_len = kc.shape[1]
    width = q_ref.shape[1]
    rows = q_ref.shape[0]
    n_req = lens_ref.shape[1]
    back = knp.shape[0] - rows
    n_page = PAGES_REQ
    n_new = (back + TILE) // KCH

    row = lax.broadcasted_iota(jnp.int32, (2 * page_len, 2 * page_len), 0)
    col = lax.broadcasted_iota(jnp.int32, (2 * page_len, 2 * page_len), 1)
    src = jnp.where(row < page_len, 2 * row, 2 * row - (2 * page_len - 1))
    choose = (col == src).astype(F32).astype(BF)

    def unpack(slot):
        pages = [raw_ref[pos_ref[slot + i]] for i in range(BLK)]
        both = jnp.dot(
            choose, jnp.concatenate(pages, axis=1), preferred_element_type=F32
        ).astype(BF)
        for i in range(BLK):
            kc[slot + i] = both[:page_len, i * width : (i + 1) * width]
            vc[slot + i] = both[page_len:, i * width : (i + 1) * width]

    for r in range(n_req):
        unpack(r * n_page)
    for r in range(n_req):
        for b in range(1, n_page // BLK):
            @pl.when(counts_ref[0, r] > b * BLK)
            def _():
                unpack(r * n_page + b * BLK)

    knp[:back, :] = jnp.zeros((back, width), BF)
    vnp[:back, :] = jnp.zeros((back, width), BF)
    knp[back:, :] = kn_ref[...]
    vnp[back:, :] = vn_ref[...]

    lane = lax.broadcasted_iota(jnp.int32, (1, width), 1)
    lane_f = lax.broadcasted_iota(jnp.int32, (1, KCH), 1).astype(F32)
    delta = [bias_ref[0, group * per + a] - bias_ref[1, group * per + a] for a in range(per)]
    starts = [jnp.int32(0)]
    for r in range(n_req):
        starts.append(starts[-1] + lens_ref[0, r])

    def tile_body(t, carry):
        row0 = pl.multiple_of(t * TILE, TILE)
        qt = q_ref[pl.ds(row0, TILE), :].astype(F32)
        for a in range(per):
            mine = (lane >= a * HD) & (lane < (a + 1) * HD)
            qbd[a * TILE : (a + 1) * TILE, :] = jnp.where(mine, qt, 0.0).astype(BF)

        row = (row0 + lax.broadcasted_iota(jnp.int32, (TILE, KCH), 0)).astype(F32)
        start_row = jnp.zeros((TILE, KCH), F32)
        offset = jnp.zeros((TILE, KCH), F32)
        blocks = jnp.int32(1)
        for r in range(n_req):
            start, end, live = starts[r], starts[r + 1], counts_ref[0, r]
            inside = (row >= start.astype(F32)) & (row < end.astype(F32))
            start_row = jnp.where(inside, start.astype(F32), start_row)
            offset = jnp.where(inside, (live * page_len - start).astype(F32), offset)
            here = (start < row0 + TILE) & (end > row0)
            blocks = jnp.maximum(blocks, jnp.where(here, (live + BLK - 1) // BLK, 0))
        var_first = jnp.floor((row + offset + 0.5) * (1.0 / VARLEN)) * VARLEN
        info[0] = row
        info[1] = start_row
        info[2] = var_first
        info[3] = var_first - offset

        for b in range(n_page // BLK):
            @pl.when(b < blocks)
            def _():
                for i in range(BLK):
                    sbuf[b * BLK + i] = jnp.full((per * TILE, KCH), NEG, F32)

        def scores(keys):
            return lax.dot_general(
                qbd[...], keys, (((1,), (1,)), ((), ())), preferred_element_type=F32
            )

        for r in range(n_req):
            start, end, live = starts[r], starts[r + 1], counts_ref[0, r]
            here = (start < row0 + TILE) & (end > row0)
            for b in range(n_page // BLK):
                @pl.when(here & (live > b * BLK))
                def _():
                    s_all = scores(
                        kc[r * n_page + b * BLK : r * n_page + (b + 1) * BLK].reshape(
                            BLK * page_len, width
                        )
                    )
                    row = info[0]
                    inside = (row >= start.astype(F32)) & (row < end.astype(F32))
                    for i in range(BLK):
                        page = b * BLK + i
                        dead = jnp.where(page < live, 0.0, NEG)
                        same = info[2] <= lane_f + page * page_len
                        for a in range(per):
                            part = slice(a * TILE, (a + 1) * TILE)
                            s = s_all[part, i * KCH : (i + 1) * KCH]
                            s = s + jnp.where(same, delta[a] + dead, dead)
                            sbuf[page, part, :] = jnp.where(inside, s, sbuf[page, part, :])

        s_all = scores(knp[pl.ds(row0, back + TILE), :])
        for i in range(n_new):
            key_row = lane_f + (row0 - back + i * KCH).astype(F32)
            allowed = (key_row >= info[1]) & (key_row <= info[0])
            same = info[3] <= key_row
            for a in range(per):
                part = slice(a * TILE, (a + 1) * TILE)
                s = s_all[part, i * KCH : (i + 1) * KCH]
                s = jnp.where(allowed, s + jnp.where(same, delta[a], 0.0), NEG)
                sbuf[n_page + i, part, :] = s

        for a in range(per):
            part = slice(a * TILE, (a + 1) * TILE)

            def top_block(b, top):
                for i in range(BLK):
                    top = jnp.maximum(top, sbuf[b * BLK + i, part, :])
                return top

            top = sbuf[n_page, part, :]
            for i in range(1, n_new):
                top = jnp.maximum(top, sbuf[n_page + i, part, :])
            top = lax.fori_loop(0, blocks, top_block, top)
            peak = jnp.broadcast_to(jnp.max(top, axis=1, keepdims=True), (TILE, KCH))

            def weigh(c, total):
                p = jnp.exp(sbuf[c, part, :] - peak)
                sbuf[c, part, :] = p
                return total + p

            def weigh_block(b, total):
                for i in range(BLK):
                    total = weigh(b * BLK + i, total)
                return total

            total = jnp.zeros((TILE, KCH), F32)
            for i in range(n_new):
                total = weigh(n_page + i, total)
            total = lax.fori_loop(0, blocks, weigh_block, total)
            inverse = jnp.broadcast_to(
                1.0 / jnp.sum(total, axis=1, keepdims=True), (TILE, KCH)
            )
            for i in range(n_new):
                c = n_page + i
                wbuf[part, c * KCH : (c + 1) * KCH] = (sbuf[c, part, :] * inverse).astype(BF)
            for b in range(n_page // BLK):
                @pl.when(b < blocks)
                def _():
                    for i in range(BLK):
                        c = b * BLK + i
                        wbuf[part, c * KCH : (c + 1) * KCH] = (
                            sbuf[c, part, :] * inverse
                        ).astype(BF)

        obuf[...] = jnp.dot(
            wbuf[:, n_page * KCH :], vnp[pl.ds(row0, back + TILE), :],
            preferred_element_type=F32,
        )
        for r in range(n_req):
            start, end, live = starts[r], starts[r + 1], counts_ref[0, r]
            here = (start < row0 + TILE) & (end > row0)
            for b in range(n_page // BLK):
                @pl.when(here & (live > b * BLK))
                def _():
                    o = jnp.dot(
                        wbuf[:, b * BLK * KCH : (b + 1) * BLK * KCH],
                        vc[r * n_page + b * BLK : r * n_page + (b + 1) * BLK].reshape(
                            BLK * page_len, width
                        ),
                        preferred_element_type=F32,
                    )
                    row = info[0]
                    inside = (row >= start.astype(F32)) & (row < end.astype(F32))
                    for a in range(per):
                        part = slice(a * TILE, (a + 1) * TILE)
                        before = obuf[part, :]
                        obuf[part, :] = jnp.where(inside[:, :width], before + o[part], before)
        o = obuf[:TILE, :]
        for a in range(1, per):
            o = jnp.where(lane >= a * HD, obuf[a * TILE : (a + 1) * TILE, :], o)
        out_ref[pl.ds(row0, TILE), :] = o.astype(BF)
        return carry

    lax.fori_loop(0, rows // TILE, tile_body, 0)


def attend(group, lanes, most, lens, counts, pos, bias, q, kn, vn, raw):
    rows = q.shape[0]
    per = lanes // HD
    page_len = raw.shape[1] // 2
    slots = raw.shape[0]
    back = -(-most // KCH) * KCH
    n_all = PAGES_REQ + (back + TILE) // KCH
    smem = pl.BlockSpec(memory_space=pltpu.SMEM)
    part = pl.BlockSpec((rows, lanes), lambda i: (0, group))
    return pl.pallas_call(
        functools.partial(attend_kernel, group, per),
        grid=(1,),
        out_shape=jax.ShapeDtypeStruct((rows, lanes), BF),
        in_specs=[smem] * 4
        + [part] * 3
        + [pl.BlockSpec(raw.shape, lambda i: (0, 0, 0), pipeline_mode=pl.Buffered(1))],
        out_specs=pl.BlockSpec((rows, lanes), lambda i: (0, 0)),
        scratch_shapes=[
            pltpu.VMEM((slots, page_len, lanes), BF),
            pltpu.VMEM((slots, page_len, lanes), BF),
            pltpu.VMEM((back + rows, lanes), BF),
            pltpu.VMEM((back + rows, lanes), BF),
            pltpu.VMEM((per * TILE, lanes), BF),
            pltpu.VMEM((4, TILE, KCH), F32),
            pltpu.VMEM((n_all, per * TILE, KCH), F32),
            pltpu.VMEM((per * TILE, n_all * KCH), BF),
            pltpu.VMEM((per * TILE, lanes), F32),
        ],
        compiler_params=pltpu.CompilerParams(vmem_limit_bytes=32 << 20),
        cost_estimate=pl.CostEstimate(
            flops=4 * rows * per * 1408 * lanes, bytes_accessed=raw.size * 2, transcendentals=0
        ),
        name="attend",
    )(lens, counts, pos, bias, q, kn, vn, raw)


def shift(value, axis, n, k):
    return lax.ppermute(value, axis, [(i, (i + k) % n) for i in range(n)])


def per_device(
    tokens,
    attn_gain,
    ffn_gain,
    w_qkv,
    w_out,
    w_gateup,
    w_down,
    variate_bias,
    adapter_down,
    adapter_up,
    owner_table,
    lengths,
    adapter_ids,
    page_counts,
    page_table,
    cache_pool,
):
    n_tp = lax.axis_size("tensor")
    n_dp = lax.axis_size("dp")
    tp = lax.axis_index("tensor")
    dp = lax.axis_index("dp")
    me = dp.astype(jnp.int32).reshape(1)
    row_count, d_model = tokens.shape
    tok_total = row_count * n_tp
    width = w_out.shape[0]
    heads = width // HD
    page_len = cache_pool.shape[1]
    cap = max(1, page_table.shape[1] // n_dp)
    far_first = [k for k in range(1, n_tp)]

    lanes = min(width, 2 * HD)
    n_group = width // lanes
    slots = n_dp * cap
    wanted, buffer_pos = want(me, page_table, n_dp, cap, cache_pool.shape[0])
    asked = lax.psum(wanted, "dp")
    picked = pick(me, asked, cache_pool, n_dp, cap, lanes)
    own_half = lax.dynamic_slice_in_dim(w_out, (dp % 2) * (width // 2), width // 2, 0)
    picked, own_half, lengths, adapter_ids, page_counts = lax.optimization_barrier(
        (picked, own_half, lengths, adapter_ids, page_counts)
    )
    fetched = []
    for a in range(n_group):
        send = picked[a]
        if fetched:
            send, _ = lax.optimization_barrier((send, fetched[-1]))
        got = lax.all_to_all(send, "dp", split_axis=0, concat_axis=0, tiled=True)
        fetched.append(got.reshape(slots, 2 * page_len, lanes))

    all_tokens = lax.all_gather(tokens, "tensor", axis=0, tiled=True)
    normed = normalize(all_tokens, attn_gain).astype(BF)

    dd = d_model // n_tp
    down_part = lax.dynamic_slice_in_dim(adapter_down, tp * dd, dd, 3)
    both_parts = jnp.concatenate([down_part, adapter_up], axis=3)
    both_all = lax.all_gather(both_parts, "dp", axis=0, tiled=True)
    slot_ids = jnp.take(owner_table, adapter_ids[0])
    select = (
        slot_ids[:, None] == jnp.arange(both_all.shape[0], dtype=jnp.int32)[None, :]
    ).astype(BF)
    both_sel = jnp.einsum("rn,nkce->rkce", select, both_all, preferred_element_type=F32).astype(BF)
    down_named, up_sel = both_sel[..., :dd], both_sel[..., dd:]
    down_blocks = [down_named] + [shift(down_named, "tensor", n_tp, k) for k in far_first]

    halves = jnp.stack([shift(own_half, "tensor", n_tp, k) for k in far_first])
    twins = lax.ppermute(halves, "dp", [(i, i ^ 1) for i in range(n_dp)])
    w_rest = jnp.where(
        dp % 2 == 0,
        jnp.concatenate([halves, twins], axis=1),
        jnp.concatenate([twins, halves], axis=1),
    )
    w_whole = jnp.concatenate([w_out[None], w_rest], axis=0)

    live_counts = page_counts[0]
    onehot, position = token_layout(lengths[0], live_counts, page_len, tok_total)
    member = onehot.astype(F32)
    projected = jnp.einsum("td,kde->kte", normed, w_qkv, preferred_element_type=F32)
    n_req = member.shape[1]
    rank = down_named.shape[2]
    down_sel = jnp.zeros((n_req, 2, rank, n_tp, dd), BF)
    for k, block in enumerate(down_blocks):
        down_sel = lax.dynamic_update_index_in_dim(down_sel, block, (tp - k) % n_tp, 3)
    down_sel = down_sel.reshape(n_req, 2, rank, d_model)
    lowall = jnp.einsum("td,rkcd->rtkc", normed, down_sel, preferred_element_type=F32)
    low_rank = jnp.sum(
        lowall * jnp.transpose(member)[:, :, None, None], axis=0
    ).astype(BF)
    spread = (jnp.transpose(member)[:, :, None, None] * low_rank.astype(F32)).astype(BF)
    delta_proj = jnp.einsum("rtkc,rkce->kte", spread, up_sel, preferred_element_type=F32)
    time_pos = position % VARLEN
    query = rotary((projected[0] + delta_proj[0]).reshape(tok_total, heads, HD), time_pos)
    query = (query.astype(BF) * BF(HD ** -0.5)).reshape(tok_total, width)
    new_keys = rotary(projected[1].reshape(tok_total, heads, HD), time_pos)
    new_keys = new_keys.astype(BF).reshape(tok_total, width)
    new_values = (projected[2] + delta_proj[1]).astype(BF)

    n_chunk = max(1, row_count // CHUNK)
    sub = row_count // n_chunk
    mixes = [[] for _ in range(n_chunk)]
    for a in range(n_group):
        mix = attend(
            a, lanes, 2 * TILE, lengths, page_counts, buffer_pos, variate_bias,
            query, new_keys, new_values, fetched[a],
        ).reshape(n_tp, n_chunk, sub, lanes)
        for c in range(n_chunk):
            own = mix[:, c].reshape(n_tp * sub, lanes)
            mixes[c].append([own] + [shift(own, "tensor", n_tp, k) for k in far_first])

    base = all_tokens.reshape(n_tp, n_chunk, sub, d_model)
    w_parts = w_whole.reshape(n_tp, n_group, lanes, d_model)
    outs = []
    for c in range(n_chunk):
        residual = base[:, c].reshape(n_tp * sub, d_model).astype(F32)
        for a in range(n_group):
            residual = residual + jnp.dot(
                jnp.concatenate(mixes[c][a], axis=1),
                w_parts[:, a].reshape(n_tp * lanes, d_model),
                preferred_element_type=F32,
            )
        ffn_in = normalize(residual, ffn_gain).astype(BF)
        gate_up = jnp.einsum("td,kdf->ktf", ffn_in, w_gateup, preferred_element_type=F32)
        hidden = (jax.nn.silu(gate_up[0]) * gate_up[1]).astype(BF)
        down = jnp.dot(hidden, w_down, preferred_element_type=F32).reshape(n_tp, sub, d_model)
        total = lax.dynamic_index_in_dim(down, tp, 0, False)
        total = total + lax.dynamic_index_in_dim(
            residual.reshape(n_tp, sub, d_model), tp, 0, False
        )
        down = down.astype(BF)
        for k in far_first:
            piece = lax.dynamic_index_in_dim(down, (tp + k) % n_tp, 0, False)
            total = total + shift(piece, "tensor", n_tp, k).astype(F32)
        outs.append(total.astype(BF))
    return jnp.concatenate(outs, axis=0)


def solution(mesh):
    return jax.shard_map(
        per_device,
        mesh=mesh,
        in_specs=(
            P(("dp", "tensor"), None),
            P(),
            P(),
            P(None, None, "tensor"),
            P("tensor", None),
            P(None, None, "tensor"),
            P("tensor", None),
            P(None, "tensor"),
            P("dp", None, None, None),
            P("dp", None, None, "tensor"),
            P(),
            P("dp", None),
            P("dp", None),
            P("dp", None),
            P("dp", None),
            P("dp", None, None, "tensor"),
        ),
        out_specs=P(("dp", "tensor"), None),
        check_vma=False,
    )
```

```python
import functools

import jax
import jax.numpy as jnp
from jax import lax
from jax.experimental import pallas as pl
from jax.experimental.pallas import tpu as pltpu
from jax.sharding import PartitionSpec as P

HD = 64
PAGES_REQ = 8
VARLEN = 160
TILE = 128
KCH = 128
BLK = 4
CHUNK = 64
BF = jnp.bfloat16
F32 = jnp.float32
NEG = -1e30


def normalize(values, gain):
    values = values.astype(F32)
    inv_scale = lax.rsqrt(jnp.mean(values * values, axis=-1, keepdims=True) + 1e-05)
    return values * inv_scale * gain.astype(F32)


def token_layout(req_lens, live_counts, page_len, tok_total):
    end_pos = jnp.cumsum(req_lens, dtype=jnp.int32)
    starts = end_pos - req_lens
    tok_index = jnp.arange(tok_total, dtype=jnp.int32)
    request = jnp.sum(
        (tok_index[:, None] >= end_pos[None, :]).astype(jnp.int32), axis=1, dtype=jnp.int32
    )
    onehot = request[:, None] == jnp.arange(req_lens.shape[0], dtype=jnp.int32)[None, :]
    first_pos = jnp.sum(jnp.where(onehot, starts[None, :], 0), axis=1, dtype=jnp.int32)
    cached = jnp.sum(jnp.where(onehot, live_counts[None, :], 0), axis=1, dtype=jnp.int32)
    return (onehot, cached * page_len + tok_index - first_pos)


def pick_kernel(n_dp, cap, me_ref, asked_ref, pool_ref, *rest):
    n_out = len(rest) - 3
    outs, (buf, sem_in, sem_out) = rest[:n_out], rest[n_out:]
    lanes = outs[0].shape[-1]
    me = me_ref[0]
    slots = asked_ref.shape[2]

    def find(g, carry):
        count = jnp.int32(0)
        for p in range(slots):
            hit = asked_ref[g, 0, p] == me

            @pl.when(hit)
            def _():
                pltpu.make_async_copy(
                    pool_ref.at[asked_ref[g, 1, p]], buf.at[g, count], sem_in.at[g]
                ).start()

            count = count + hit.astype(jnp.int32)
        return carry

    lax.fori_loop(0, n_dp, find, 0)
    done = []
    for g in range(n_dp):
        pltpu.make_async_copy(pool_ref.at[pl.ds(0, cap)], buf.at[g], sem_in.at[g]).wait()
        for a in range(n_out):
            copy = pltpu.make_async_copy(
                buf.at[g, :, :, :, pl.ds(a * lanes, lanes)], outs[a].at[g], sem_out.at[a, g]
            )
            copy.start()
            done.append(copy)
    for copy in done:
        copy.wait()


def pick(me, asked, pool, n_dp, cap, lanes):
    smem = pl.BlockSpec(memory_space=pltpu.SMEM)
    hbm = pl.BlockSpec(memory_space=pl.ANY)
    n_out = pool.shape[-1] // lanes
    shape = (n_dp, cap) + pool.shape[1:-1]
    return pl.pallas_call(
        functools.partial(pick_kernel, n_dp, cap),
        out_shape=[jax.ShapeDtypeStruct(shape + (lanes,), pool.dtype)] * n_out,
        in_specs=[smem, smem, hbm],
        out_specs=[hbm] * n_out,
        scratch_shapes=[
            pltpu.VMEM(shape + pool.shape[-1:], pool.dtype),
            pltpu.SemaphoreType.DMA((n_dp,)),
            pltpu.SemaphoreType.DMA((n_out, n_dp)),
        ],
        cost_estimate=pl.CostEstimate(flops=0, bytes_accessed=4 * pool.size, transcendentals=0),
        name="pick_pages",
    )(me, asked, pool)


def named_kernel(n_loc, span, table_ref, ids_ref, all_ref, down_ref, up_ref, sem):
    copies = []
    for r in range(ids_ref.shape[1]):
        slot = table_ref[ids_ref[0, r]]
        home, inner = slot // n_loc, slot % n_loc
        for half, out in ((0, down_ref), (1, up_ref)):
            base = pl.multiple_of((half * n_loc + inner) * span, span)
            copy = pltpu.make_async_copy(
                all_ref.at[home, pl.ds(base, span)], out.at[pl.ds(r * span, span)], sem.at[r, half]
            )
            copy.start()
            copies.append(copy)
    for copy in copies:
        copy.wait()


def named(owner_table, adapter_ids, gathered, n_loc, span):
    n_req = adapter_ids.shape[1]
    smem = pl.BlockSpec(memory_space=pltpu.SMEM)
    vmem = pl.BlockSpec(memory_space=pltpu.VMEM)
    out = jax.ShapeDtypeStruct((n_req * span, gathered.shape[-1]), BF)
    return pl.pallas_call(
        functools.partial(named_kernel, n_loc, span),
        out_shape=(out, out),
        in_specs=[smem, smem, pl.BlockSpec(memory_space=pl.ANY)],
        out_specs=(vmem, vmem),
        scratch_shapes=[pltpu.SemaphoreType.DMA((n_req, 2))],
        name="named_adapters",
    )(owner_table, adapter_ids, gathered)


def project_kernel(
    n_tp, cap, pool_dev, tp_ref, lens_ref, table_ref, gain_ref, w_ref, up_ref, cos_ref, sin_ref, *rest
):
    tok_refs, down_refs = rest[:n_tp], rest[n_tp : 2 * n_tp]
    q_ref, k_ref, v_ref, pos_ref, down, count = rest[2 * n_tp :]
    tp = tp_ref[0]
    rows, _ = tok_refs[0].shape
    width = q_ref.shape[1]
    dd = down_refs[0].shape[1]
    n_low = down_refs[0].shape[0]
    n_req = lens_ref.shape[1]
    rank = n_low // n_req // 2

    for g in range(count.shape[0]):
        count[g] = 0

    def place(p, carry):
        home = table_ref[0, p] // pool_dev
        seen = count[home]
        count[home] = seen + 1
        pos_ref[p] = home * cap + seen
        return carry

    lax.fori_loop(0, table_ref.shape[1], place, 0)

    for k in range(n_tp):
        at = lax.rem(tp - k + n_tp, n_tp)
        down[at] = down_refs[k][...]
    lane = lax.broadcasted_iota(jnp.int32, (1, 128), 1)
    first = jnp.bitwise_and(lane, HD - 1) < HD // 2

    def rope(u, cos, sin):
        parts = []
        for a in range(width // 128):
            part = u[:, a * 128 : (a + 1) * 128]
            other = jnp.where(
                first, pltpu.roll(part, 128 - HD // 2, 1), pltpu.roll(part, HD // 2, 1)
            )
            parts.append(part * cos + other * sin)
        return parts

    for k in range(n_tp):
        row0 = pl.multiple_of(lax.rem(tp - k + n_tp, n_tp) * rows, rows)
        x = tok_refs[k][...].astype(F32)
        inv = lax.rsqrt(jnp.mean(x * x, axis=1, keepdims=True) + 1e-05)
        normed = (x * inv * gain_ref[...].astype(F32)).astype(BF)
        low = jnp.zeros((rows, n_low), F32)
        for j in range(n_tp):
            low = low + lax.dot_general(
                normed[:, j * dd : (j + 1) * dd], down[j], (((1,), (1,)), ((), ())),
                preferred_element_type=F32,
            )
        row = row0 + lax.broadcasted_iota(jnp.int32, (rows, n_low), 0)
        col = lax.broadcasted_iota(jnp.int32, (rows, n_low), 1)
        request = jnp.zeros((rows, n_low), jnp.int32)
        end = jnp.int32(0)
        for r in range(n_req - 1):
            end = end + lens_ref[0, r]
            request = request + (row >= end).astype(jnp.int32)
        own = col // (2 * rank) == request
        kind = (col // rank) % 2
        deltas = []
        for kk in range(2):
            part = jnp.where(own & (kind == kk), low, 0.0).astype(BF)
            deltas.append(jnp.dot(part, up_ref[...], preferred_element_type=F32))
        cos = cos_ref[pl.ds(row0, rows), :]
        sin = sin_ref[pl.ds(row0, rows), :]
        q = jnp.dot(normed, w_ref[0], preferred_element_type=F32) + deltas[0]
        for a, part in enumerate(rope(q, cos, sin)):
            part = part.astype(BF).astype(F32) * (HD ** -0.5)
            q_ref[pl.ds(row0, rows), a * 128 : (a + 1) * 128] = part.astype(BF)
        kk = jnp.dot(normed, w_ref[1], preferred_element_type=F32)
        for a, part in enumerate(rope(kk, cos, sin)):
            k_ref[pl.ds(row0, rows), a * 128 : (a + 1) * 128] = part.astype(BF)
        v = jnp.dot(normed, w_ref[2], preferred_element_type=F32) + deltas[1]
        v_ref[pl.ds(row0, rows), :] = v.astype(BF)


def project(tp, lens, table, gain, w_qkv, up, cos, sin, toks, downs, n_dp, cap, pool_dev):
    n_tp = len(toks)
    rows = toks[0].shape[0] * n_tp
    width = w_qkv.shape[2]
    smem = pl.BlockSpec(memory_space=pltpu.SMEM)
    vmem = pl.BlockSpec(memory_space=pltpu.VMEM)
    out = jax.ShapeDtypeStruct((rows, width), BF)
    return pl.pallas_call(
        functools.partial(project_kernel, n_tp, cap, pool_dev),
        out_shape=(out, out, out, jax.ShapeDtypeStruct((table.shape[1],), jnp.int32)),
        in_specs=[smem] * 3 + [vmem] * (5 + 2 * n_tp),
        out_specs=(vmem, vmem, vmem, smem),
        scratch_shapes=[
            pltpu.VMEM((n_tp,) + downs[0].shape, BF),
            pltpu.SMEM((n_dp,), jnp.int32),
        ],
        compiler_params=pltpu.CompilerParams(vmem_limit_bytes=32 << 20),
        cost_estimate=pl.CostEstimate(
            flops=8 * rows * w_qkv.size // 3, bytes_accessed=4 * w_qkv.size, transcendentals=0
        ),
        name="project",
    )(tp, lens, table, gain, w_qkv, up, cos, sin, *toks, *downs)


def attend_kernel(
    group, per, lens_ref, counts_ref, pos_ref, bias_ref,
    q_ref, kn_ref, vn_ref, raw_ref, out_ref,
    kc, vc, knp, vnp, qbd, info, sbuf, wbuf, obuf,
):
    page_len = kc.shape[1]
    width = q_ref.shape[1]
    rows = q_ref.shape[0]
    n_req = lens_ref.shape[1]
    back = knp.shape[0] - rows
    n_page = PAGES_REQ
    n_new = (back + TILE) // KCH

    row = lax.broadcasted_iota(jnp.int32, (2 * page_len, 2 * page_len), 0)
    col = lax.broadcasted_iota(jnp.int32, (2 * page_len, 2 * page_len), 1)
    src = jnp.where(row < page_len, 2 * row, 2 * row - (2 * page_len - 1))
    choose = (col == src).astype(F32).astype(BF)

    def unpack(slot):
        pages = [raw_ref[pos_ref[slot + i]] for i in range(BLK)]
        both = jnp.dot(
            choose, jnp.concatenate(pages, axis=1), preferred_element_type=F32
        ).astype(BF)
        for i in range(BLK):
            kc[slot + i] = both[:page_len, i * width : (i + 1) * width]
            vc[slot + i] = both[page_len:, i * width : (i + 1) * width]

    for r in range(n_req):
        unpack(r * n_page)
    for r in range(n_req):
        for b in range(1, n_page // BLK):
            @pl.when(counts_ref[0, r] > b * BLK)
            def _():
                unpack(r * n_page + b * BLK)

    knp[:back, :] = jnp.zeros((back, width), BF)
    vnp[:back, :] = jnp.zeros((back, width), BF)
    knp[back:, :] = kn_ref[...]
    vnp[back:, :] = vn_ref[...]

    lane = lax.broadcasted_iota(jnp.int32, (1, width), 1)
    lane_f = lax.broadcasted_iota(jnp.int32, (1, KCH), 1).astype(F32)
    delta = [bias_ref[0, group * per + a] - bias_ref[1, group * per + a] for a in range(per)]
    starts = [jnp.int32(0)]
    for r in range(n_req):
        starts.append(starts[-1] + lens_ref[0, r])

    def tile_body(t, carry):
        row0 = pl.multiple_of(t * TILE, TILE)
        qt = q_ref[pl.ds(row0, TILE), :].astype(F32)
        for a in range(per):
            mine = (lane >= a * HD) & (lane < (a + 1) * HD)
            qbd[a * TILE : (a + 1) * TILE, :] = jnp.where(mine, qt, 0.0).astype(BF)

        row = (row0 + lax.broadcasted_iota(jnp.int32, (TILE, KCH), 0)).astype(F32)
        start_row = jnp.zeros((TILE, KCH), F32)
        offset = jnp.zeros((TILE, KCH), F32)
        blocks = jnp.int32(1)
        for r in range(n_req):
            start, end, live = starts[r], starts[r + 1], counts_ref[0, r]
            inside = (row >= start.astype(F32)) & (row < end.astype(F32))
            start_row = jnp.where(inside, start.astype(F32), start_row)
            offset = jnp.where(inside, (live * page_len - start).astype(F32), offset)
            here = (start < row0 + TILE) & (end > row0)
            blocks = jnp.maximum(blocks, jnp.where(here, (live + BLK - 1) // BLK, 0))
        var_first = jnp.floor((row + offset + 0.5) * (1.0 / VARLEN)) * VARLEN
        info[0] = row
        info[1] = start_row
        info[2] = var_first
        info[3] = var_first - offset

        for b in range(n_page // BLK):
            @pl.when(b < blocks)
            def _():
                for i in range(BLK):
                    sbuf[b * BLK + i] = jnp.full((per * TILE, KCH), NEG, F32)

        def scores(keys):
            return lax.dot_general(
                qbd[...], keys, (((1,), (1,)), ((), ())), preferred_element_type=F32
            )

        for r in range(n_req):
            start, end, live = starts[r], starts[r + 1], counts_ref[0, r]
            here = (start < row0 + TILE) & (end > row0)
            for b in range(n_page // BLK):
                @pl.when(here & (live > b * BLK))
                def _():
                    s_all = scores(
                        kc[r * n_page + b * BLK : r * n_page + (b + 1) * BLK].reshape(
                            BLK * page_len, width
                        )
                    )
                    row = info[0]
                    inside = (row >= start.astype(F32)) & (row < end.astype(F32))
                    for i in range(BLK):
                        page = b * BLK + i
                        dead = jnp.where(page < live, 0.0, NEG)
                        same = info[2] <= lane_f + page * page_len
                        for a in range(per):
                            part = slice(a * TILE, (a + 1) * TILE)
                            s = s_all[part, i * KCH : (i + 1) * KCH]
                            s = s + jnp.where(same, delta[a] + dead, dead)
                            sbuf[page, part, :] = jnp.where(inside, s, sbuf[page, part, :])

        s_all = scores(knp[pl.ds(row0, back + TILE), :])
        for i in range(n_new):
            key_row = lane_f + (row0 - back + i * KCH).astype(F32)
            allowed = (key_row >= info[1]) & (key_row <= info[0])
            same = info[3] <= key_row
            for a in range(per):
                part = slice(a * TILE, (a + 1) * TILE)
                s = s_all[part, i * KCH : (i + 1) * KCH]
                s = jnp.where(allowed, s + jnp.where(same, delta[a], 0.0), NEG)
                sbuf[n_page + i, part, :] = s

        for a in range(per):
            part = slice(a * TILE, (a + 1) * TILE)

            def top_block(b, top):
                for i in range(BLK):
                    top = jnp.maximum(top, sbuf[b * BLK + i, part, :])
                return top

            top = sbuf[n_page, part, :]
            for i in range(1, n_new):
                top = jnp.maximum(top, sbuf[n_page + i, part, :])
            top = lax.fori_loop(0, blocks, top_block, top)
            peak = jnp.broadcast_to(jnp.max(top, axis=1, keepdims=True), (TILE, KCH))

            def weigh(c, total):
                p = jnp.exp(sbuf[c, part, :] - peak)
                sbuf[c, part, :] = p
                return total + p

            def weigh_block(b, total):
                for i in range(BLK):
                    total = weigh(b * BLK + i, total)
                return total

            total = jnp.zeros((TILE, KCH), F32)
            for i in range(n_new):
                total = weigh(n_page + i, total)
            total = lax.fori_loop(0, blocks, weigh_block, total)
            inverse = jnp.broadcast_to(
                1.0 / jnp.sum(total, axis=1, keepdims=True), (TILE, KCH)
            )
            for i in range(n_new):
                c = n_page + i
                wbuf[part, c * KCH : (c + 1) * KCH] = (sbuf[c, part, :] * inverse).astype(BF)
            for b in range(n_page // BLK):
                @pl.when(b < blocks)
                def _():
                    for i in range(BLK):
                        c = b * BLK + i
                        wbuf[part, c * KCH : (c + 1) * KCH] = (
                            sbuf[c, part, :] * inverse
                        ).astype(BF)

        obuf[...] = jnp.dot(
            wbuf[:, n_page * KCH :], vnp[pl.ds(row0, back + TILE), :],
            preferred_element_type=F32,
        )
        for r in range(n_req):
            start, end, live = starts[r], starts[r + 1], counts_ref[0, r]
            here = (start < row0 + TILE) & (end > row0)
            for b in range(n_page // BLK):
                @pl.when(here & (live > b * BLK))
                def _():
                    o = jnp.dot(
                        wbuf[:, b * BLK * KCH : (b + 1) * BLK * KCH],
                        vc[r * n_page + b * BLK : r * n_page + (b + 1) * BLK].reshape(
                            BLK * page_len, width
                        ),
                        preferred_element_type=F32,
                    )
                    row = info[0]
                    inside = (row >= start.astype(F32)) & (row < end.astype(F32))
                    for a in range(per):
                        part = slice(a * TILE, (a + 1) * TILE)
                        before = obuf[part, :]
                        obuf[part, :] = jnp.where(inside[:, :width], before + o[part], before)
        o = obuf[:TILE, :]
        for a in range(1, per):
            o = jnp.where(lane >= a * HD, obuf[a * TILE : (a + 1) * TILE, :], o)
        out_ref[pl.ds(row0, TILE), :] = o.astype(BF)
        return carry

    lax.fori_loop(0, rows // TILE, tile_body, 0)


def attend(group, lanes, most, lens, counts, pos, bias, q, kn, vn, raw):
    rows = q.shape[0]
    per = lanes // HD
    page_len = raw.shape[1] // 2
    slots = raw.shape[0]
    back = -(-most // KCH) * KCH
    n_all = PAGES_REQ + (back + TILE) // KCH
    smem = pl.BlockSpec(memory_space=pltpu.SMEM)
    part = pl.BlockSpec((rows, lanes), lambda i: (0, group))
    return pl.pallas_call(
        functools.partial(attend_kernel, group, per),
        grid=(1,),
        out_shape=jax.ShapeDtypeStruct((rows, lanes), BF),
        in_specs=[smem] * 4
        + [part] * 3
        + [pl.BlockSpec(raw.shape, lambda i: (0, 0, 0), pipeline_mode=pl.Buffered(1))],
        out_specs=pl.BlockSpec((rows, lanes), lambda i: (0, 0)),
        scratch_shapes=[
            pltpu.VMEM((slots, page_len, lanes), BF),
            pltpu.VMEM((slots, page_len, lanes), BF),
            pltpu.VMEM((back + rows, lanes), BF),
            pltpu.VMEM((back + rows, lanes), BF),
            pltpu.VMEM((per * TILE, lanes), BF),
            pltpu.VMEM((4, TILE, KCH), F32),
            pltpu.VMEM((n_all, per * TILE, KCH), F32),
            pltpu.VMEM((per * TILE, n_all * KCH), BF),
            pltpu.VMEM((per * TILE, lanes), F32),
        ],
        compiler_params=pltpu.CompilerParams(vmem_limit_bytes=32 << 20),
        cost_estimate=pl.CostEstimate(
            flops=4 * rows * per * 1408 * lanes, bytes_accessed=raw.size * 2, transcendentals=0
        ),
        name="attend",
    )(lens, counts, pos, bias, q, kn, vn, raw)


def shift(value, axis, n, k):
    return lax.ppermute(value, axis, [(i, (i + k) % n) for i in range(n)])


def per_device(
    tokens,
    attn_gain,
    ffn_gain,
    w_qkv,
    w_out,
    w_gateup,
    w_down,
    variate_bias,
    adapter_down,
    adapter_up,
    owner_table,
    lengths,
    adapter_ids,
    page_counts,
    page_table,
    cache_pool,
):
    n_tp = lax.axis_size("tensor")
    n_dp = lax.axis_size("dp")
    tp = lax.axis_index("tensor")
    dp = lax.axis_index("dp")
    me = dp.astype(jnp.int32).reshape(1)
    tp_id = tp.astype(jnp.int32).reshape(1)
    row_count, d_model = tokens.shape
    tok_total = row_count * n_tp
    width = w_out.shape[0]
    page_len = cache_pool.shape[1]
    pool_dev = cache_pool.shape[0]
    cap = max(1, page_table.shape[1] // n_dp)
    far_first = [k for k in range(1, n_tp)]
    lanes = min(width, 2 * HD)
    n_group = width // lanes
    slots = n_dp * cap
    dd = d_model // n_tp
    n_loc, _, rank, _ = adapter_down.shape
    span = 2 * rank

    toks = [tokens] + [shift(tokens, "tensor", n_tp, k) for k in far_first]

    down_part = lax.dynamic_slice_in_dim(adapter_down, tp * dd, dd, 3).reshape(n_loc * span, dd)
    names = jnp.concatenate([page_table // pool_dev, page_table % pool_dev], axis=0).astype(BF)
    names = jnp.pad(names, ((0, 14), (0, dd - names.shape[1])))
    payload = jnp.concatenate([down_part, adapter_up.reshape(n_loc * span, width), names], axis=0)
    gathered = lax.all_gather(payload, "dp", axis=0)
    asked = gathered[:, 2 * n_loc * span : 2 * n_loc * span + 2, : page_table.shape[1]]
    picked = pick(me, asked.astype(jnp.int32), cache_pool, n_dp, cap, lanes)
    fetched = [
        lax.all_to_all(picked[0], "dp", split_axis=0, concat_axis=0, tiled=True)
    ]

    own_half = lax.dynamic_slice_in_dim(w_out, (dp % 2) * (width // 2), width // 2, 0)
    gathered, lengths_b = lax.optimization_barrier((gathered, lengths, picked))[:2]
    down_named, up_named = named(owner_table, adapter_ids, gathered, n_loc, span)
    downs = [down_named] + [shift(down_named, "tensor", n_tp, k) for k in far_first]

    own_half = lax.optimization_barrier((own_half, toks[1:], downs[1:]))[0]
    halves = jnp.stack([shift(own_half, "tensor", n_tp, k) for k in far_first])
    twins = lax.ppermute(halves, "dp", [(i, i ^ 1) for i in range(n_dp)])
    w_rest = jnp.where(
        dp % 2 == 0,
        jnp.concatenate([halves, twins], axis=1),
        jnp.concatenate([twins, halves], axis=1),
    )
    w_whole = jnp.concatenate([w_out[None], w_rest], axis=0)

    _, position = token_layout(lengths_b[0], page_counts[0], page_len, tok_total)
    index = jnp.arange(2 * HD, dtype=jnp.int32)
    frequency = 10000.0 ** (-2.0 * (index % (HD // 2)).astype(F32) / HD)
    angles = (position % VARLEN).astype(F32)[:, None] * frequency[None, :]
    sign = jnp.where(index % HD < HD // 2, -1.0, 1.0).astype(F32)
    query, new_keys, new_values, buffer_pos = project(
        tp_id, lengths, page_table, attn_gain.reshape(1, d_model), w_qkv, up_named,
        jnp.cos(angles), jnp.sin(angles) * sign[None, :], toks, downs, n_dp, cap, pool_dev,
    )
    for a in range(1, n_group):
        send, _ = lax.optimization_barrier((picked[a], fetched[-1]))
        fetched.append(lax.all_to_all(send, "dp", split_axis=0, concat_axis=0, tiled=True))
    fetched = [f.reshape(slots, 2 * page_len, lanes) for f in fetched]

    all_tokens = jnp.zeros((n_tp, row_count, d_model), BF)
    for k, block in enumerate(toks):
        all_tokens = lax.dynamic_update_index_in_dim(all_tokens, block, (tp - k) % n_tp, 0)

    n_chunk = max(1, row_count // CHUNK)
    sub = row_count // n_chunk
    w_parts = w_whole.reshape(n_tp, n_group, lanes, d_model)
    base = all_tokens.astype(F32).reshape(tok_total, d_model)

    def mixed(blocks, a):
        return jnp.dot(
            jnp.concatenate(blocks, axis=1),
            w_parts[:, a].reshape(n_tp * lanes, d_model),
            preferred_element_type=F32,
        )

    def attended(a, q):
        return attend(
            a, lanes, 2 * TILE, lengths, page_counts, buffer_pos, variate_bias,
            q, new_keys, new_values, fetched[a],
        )

    for a in range(n_group - 1):
        mix = attended(a, query)
        blocks = [mix] + [shift(mix, "tensor", n_tp, k) for k in far_first]
        base = base + mixed(blocks, a)
        query, base = lax.optimization_barrier((query, base))
    mix = attended(n_group - 1, query).reshape(n_tp, n_chunk, sub, lanes)
    base = base.reshape(n_tp, n_chunk, sub, d_model)
    gathered_mix = []
    for c in range(n_chunk):
        own = mix[:, c].reshape(n_tp * sub, lanes)
        gathered_mix.append([own] + [shift(own, "tensor", n_tp, k) for k in far_first])
    outs = []
    for c in range(n_chunk):
        residual = base[:, c].reshape(n_tp * sub, d_model) + mixed(gathered_mix[c], n_group - 1)
        ffn_in = normalize(residual, ffn_gain).astype(BF)
        gate_up = jnp.einsum("td,kdf->ktf", ffn_in, w_gateup, preferred_element_type=F32)
        hidden = (jax.nn.silu(gate_up[0]) * gate_up[1]).astype(BF)
        down = jnp.dot(hidden, w_down, preferred_element_type=F32).reshape(n_tp, sub, d_model)
        total = lax.dynamic_index_in_dim(down, tp, 0, False)
        total = total + lax.dynamic_index_in_dim(
            residual.reshape(n_tp, sub, d_model), tp, 0, False
        )
        down = down.astype(BF)
        for k in far_first:
            piece = lax.dynamic_index_in_dim(down, (tp + k) % n_tp, 0, False)
            total = total + shift(piece, "tensor", n_tp, k).astype(F32)
        outs.append(total.astype(BF))
    return jnp.concatenate(outs, axis=0)


def solution(mesh):
    return jax.shard_map(
        per_device,
        mesh=mesh,
        in_specs=(
            P(("dp", "tensor"), None),
            P(),
            P(),
            P(None, None, "tensor"),
            P("tensor", None),
            P(None, None, "tensor"),
            P("tensor", None),
            P(None, "tensor"),
            P("dp", None, None, None),
            P("dp", None, None, "tensor"),
            P(),
            P("dp", None),
            P("dp", None),
            P("dp", None),
            P("dp", None),
            P("dp", None, None, "tensor"),
        ),
        out_specs=P(("dp", "tensor"), None),
        check_vma=False,
    )
```

```python
import functools

import jax
import jax.numpy as jnp
from jax import lax
from jax.experimental import pallas as pl
from jax.experimental.pallas import tpu as pltpu
from jax.sharding import PartitionSpec as P

HD = 64
PAGES_REQ = 8
VARLEN = 160
TILE = 128
KCH = 128
BLK = 4
CHUNK = 64
BF = jnp.bfloat16
F32 = jnp.float32
NEG = -1e30


def normalize(values, gain):
    values = values.astype(F32)
    inv_scale = lax.rsqrt(jnp.mean(values * values, axis=-1, keepdims=True) + 1e-05)
    return values * inv_scale * gain.astype(F32)


def token_layout(req_lens, live_counts, page_len, tok_total):
    end_pos = jnp.cumsum(req_lens, dtype=jnp.int32)
    starts = end_pos - req_lens
    tok_index = jnp.arange(tok_total, dtype=jnp.int32)
    request = jnp.sum(
        (tok_index[:, None] >= end_pos[None, :]).astype(jnp.int32), axis=1, dtype=jnp.int32
    )
    onehot = request[:, None] == jnp.arange(req_lens.shape[0], dtype=jnp.int32)[None, :]
    first_pos = jnp.sum(jnp.where(onehot, starts[None, :], 0), axis=1, dtype=jnp.int32)
    cached = jnp.sum(jnp.where(onehot, live_counts[None, :], 0), axis=1, dtype=jnp.int32)
    return (onehot, cached * page_len + tok_index - first_pos)


def pick_kernel(n_dp, cap, me_ref, asked_ref, pool_ref, *rest):
    n_out = len(rest) - 3
    outs, (buf, sem_in, sem_out) = rest[:n_out], rest[n_out:]
    lanes = outs[0].shape[-1]
    me = me_ref[0]
    slots = asked_ref.shape[2]

    def find(g, carry):
        count = jnp.int32(0)
        for p in range(slots):
            hit = asked_ref[g, 0, p] == me

            @pl.when(hit)
            def _():
                pltpu.make_async_copy(
                    pool_ref.at[asked_ref[g, 1, p]], buf.at[g, count], sem_in.at[g]
                ).start()

            count = count + hit.astype(jnp.int32)
        return carry

    lax.fori_loop(0, n_dp, find, 0)
    done = []
    for g in range(n_dp):
        pltpu.make_async_copy(pool_ref.at[pl.ds(0, cap)], buf.at[g], sem_in.at[g]).wait()
        for a in range(n_out):
            copy = pltpu.make_async_copy(
                buf.at[g, :, :, :, pl.ds(a * lanes, lanes)], outs[a].at[g], sem_out.at[a, g]
            )
            copy.start()
            done.append(copy)
    for copy in done:
        copy.wait()


def pick(me, asked, pool, n_dp, cap, lanes):
    smem = pl.BlockSpec(memory_space=pltpu.SMEM)
    hbm = pl.BlockSpec(memory_space=pl.ANY)
    n_out = pool.shape[-1] // lanes
    shape = (n_dp, cap) + pool.shape[1:-1]
    return pl.pallas_call(
        functools.partial(pick_kernel, n_dp, cap),
        out_shape=[jax.ShapeDtypeStruct(shape + (lanes,), pool.dtype)] * n_out,
        in_specs=[smem, smem, hbm],
        out_specs=[hbm] * n_out,
        scratch_shapes=[
            pltpu.VMEM(shape + pool.shape[-1:], pool.dtype),
            pltpu.SemaphoreType.DMA((n_dp,)),
            pltpu.SemaphoreType.DMA((n_out, n_dp)),
        ],
        cost_estimate=pl.CostEstimate(flops=0, bytes_accessed=4 * pool.size, transcendentals=0),
        name="pick_pages",
    )(me, asked, pool)


def named_kernel(n_loc, span, table_ref, ids_ref, all_ref, down_out, up_out, down_ref, up_ref, sem):
    copies = []
    for r in range(ids_ref.shape[1]):
        slot = table_ref[ids_ref[0, r]]
        home, inner = slot // n_loc, slot % n_loc
        for half, out in ((0, down_ref), (1, up_ref)):
            base = pl.multiple_of((half * n_loc + inner) * span, span)
            copy = pltpu.make_async_copy(
                all_ref.at[home, pl.ds(base, span)], out.at[pl.ds(r * span, span)], sem.at[r, half]
            )
            copy.start()
            copies.append(copy)
    for copy in copies:
        copy.wait()
    last = [
        pltpu.make_async_copy(down_ref, down_out, sem.at[0, 0]),
        pltpu.make_async_copy(up_ref, up_out, sem.at[0, 1]),
    ]
    for copy in last:
        copy.start()
    for copy in last:
        copy.wait()


def named(owner_table, adapter_ids, gathered, n_loc, span):
    n_req = adapter_ids.shape[1]
    smem = pl.BlockSpec(memory_space=pltpu.SMEM)
    hbm = pl.BlockSpec(memory_space=pltpu.HBM)
    out = jax.ShapeDtypeStruct((n_req * span, gathered.shape[-1]), BF)
    return pl.pallas_call(
        functools.partial(named_kernel, n_loc, span),
        out_shape=(out, out),
        in_specs=[smem, smem, hbm],
        out_specs=(hbm, hbm),
        scratch_shapes=[
            pltpu.VMEM(out.shape, BF),
            pltpu.VMEM(out.shape, BF),
            pltpu.SemaphoreType.DMA((n_req, 2)),
        ],
        name="named_adapters",
    )(owner_table, adapter_ids, gathered)


def project_kernel(n_tp, cap, pool_dev, tp_ref, lens_ref, table_ref, *rest):
    hbm_refs, rest = rest[: 5 + 2 * n_tp], rest[5 + 2 * n_tp :]
    q_ref, k_ref, v_ref, pos_ref, down, count, *held = rest
    held, sem = held[:-1], held[-1]
    gain_ref, w_ref, up_ref, cos_ref, sin_ref, tok_ref = held
    tp = tp_ref[0]
    copies = []
    targets = list(held[:5]) + [tok_ref.at[k] for k in range(n_tp)]
    for k in range(n_tp):
        targets.append(down.at[lax.rem(tp - k + n_tp, n_tp)])
    for i in list(range(5, 5 + 2 * n_tp)) + list(range(5)):
        copy = pltpu.make_async_copy(hbm_refs[i], targets[i], sem.at[i])
        copy.start()
        copies.append(copy)
    _, rows, _ = tok_ref.shape
    width = q_ref.shape[1]
    n_low, dd = down.shape[1:]
    n_req = lens_ref.shape[1]
    rank = n_low // n_req // 2

    for g in range(count.shape[0]):
        count[g] = 0

    def place(p, carry):
        home = table_ref[0, p] // pool_dev
        seen = count[home]
        count[home] = seen + 1
        pos_ref[p] = home * cap + seen
        return carry

    lax.fori_loop(0, table_ref.shape[1], place, 0)

    for copy in copies:
        copy.wait()
    lane = lax.broadcasted_iota(jnp.int32, (1, 128), 1)
    first = jnp.bitwise_and(lane, HD - 1) < HD // 2

    def rope(u, cos, sin):
        parts = []
        for a in range(width // 128):
            part = u[:, a * 128 : (a + 1) * 128]
            other = jnp.where(
                first, pltpu.roll(part, 128 - HD // 2, 1), pltpu.roll(part, HD // 2, 1)
            )
            parts.append(part * cos + other * sin)
        return parts

    for k in range(n_tp):
        row0 = pl.multiple_of(lax.rem(tp - k + n_tp, n_tp) * rows, rows)
        x = tok_ref[k].astype(F32)
        inv = lax.rsqrt(jnp.mean(x * x, axis=1, keepdims=True) + 1e-05)
        normed = (x * inv * gain_ref[...].astype(F32)).astype(BF)
        low = jnp.zeros((rows, n_low), F32)
        for j in range(n_tp):
            low = low + lax.dot_general(
                normed[:, j * dd : (j + 1) * dd], down[j], (((1,), (1,)), ((), ())),
                preferred_element_type=F32,
            )
        row = row0 + lax.broadcasted_iota(jnp.int32, (rows, n_low), 0)
        col = lax.broadcasted_iota(jnp.int32, (rows, n_low), 1)
        request = jnp.zeros((rows, n_low), jnp.int32)
        end = jnp.int32(0)
        for r in range(n_req - 1):
            end = end + lens_ref[0, r]
            request = request + (row >= end).astype(jnp.int32)
        own = col // (2 * rank) == request
        kind = (col // rank) % 2
        deltas = []
        for kk in range(2):
            part = jnp.where(own & (kind == kk), low, 0.0).astype(BF)
            deltas.append(jnp.dot(part, up_ref[...], preferred_element_type=F32))
        cos = cos_ref[pl.ds(row0, rows), :]
        sin = sin_ref[pl.ds(row0, rows), :]
        q = jnp.dot(normed, w_ref[0], preferred_element_type=F32) + deltas[0]
        for a, part in enumerate(rope(q, cos, sin)):
            part = part.astype(BF).astype(F32) * (HD ** -0.5)
            q_ref[pl.ds(row0, rows), a * 128 : (a + 1) * 128] = part.astype(BF)
        kk = jnp.dot(normed, w_ref[1], preferred_element_type=F32)
        for a, part in enumerate(rope(kk, cos, sin)):
            k_ref[pl.ds(row0, rows), a * 128 : (a + 1) * 128] = part.astype(BF)
        v = jnp.dot(normed, w_ref[2], preferred_element_type=F32) + deltas[1]
        v_ref[pl.ds(row0, rows), :] = v.astype(BF)


def project(tp, lens, table, gain, w_qkv, up, cos, sin, toks, downs, n_dp, cap, pool_dev):
    n_tp = len(toks)
    rows = toks[0].shape[0] * n_tp
    width = w_qkv.shape[2]
    smem = pl.BlockSpec(memory_space=pltpu.SMEM)
    vmem = pl.BlockSpec(memory_space=pltpu.VMEM)
    out = jax.ShapeDtypeStruct((rows, width), BF)
    return pl.pallas_call(
        functools.partial(project_kernel, n_tp, cap, pool_dev),
        out_shape=(out, out, out, jax.ShapeDtypeStruct((table.shape[1],), jnp.int32)),
        in_specs=[smem] * 3 + [pl.BlockSpec(memory_space=pltpu.HBM)] * (5 + 2 * n_tp),
        out_specs=(vmem, vmem, vmem, smem),
        scratch_shapes=[
            pltpu.VMEM((n_tp,) + downs[0].shape, BF),
            pltpu.SMEM((n_dp,), jnp.int32),
        ]
        + [pltpu.VMEM(x.shape, x.dtype) for x in (gain, w_qkv, up, cos, sin)]
        + [
            pltpu.VMEM((n_tp,) + toks[0].shape, BF),
            pltpu.SemaphoreType.DMA((5 + 2 * n_tp,)),
        ],
        compiler_params=pltpu.CompilerParams(vmem_limit_bytes=32 << 20),
        cost_estimate=pl.CostEstimate(
            flops=8 * rows * w_qkv.size // 3, bytes_accessed=4 * w_qkv.size, transcendentals=0
        ),
        name="project",
    )(tp, lens, table, gain, w_qkv, up, cos, sin, *toks, *downs)


def attend_kernel(
    group, per, lens_ref, counts_ref, pos_ref, bias_ref,
    q_ref, kn_ref, vn_ref, raw_ref, out_ref,
    kc, vc, knp, vnp, qbd, info, sbuf, wbuf, obuf,
):
    page_len = kc.shape[1]
    width = q_ref.shape[1]
    rows = q_ref.shape[0]
    n_req = lens_ref.shape[1]
    back = knp.shape[0] - rows
    n_page = PAGES_REQ
    n_new = (back + TILE) // KCH

    row = lax.broadcasted_iota(jnp.int32, (2 * page_len, 2 * page_len), 0)
    col = lax.broadcasted_iota(jnp.int32, (2 * page_len, 2 * page_len), 1)
    src = jnp.where(row < page_len, 2 * row, 2 * row - (2 * page_len - 1))
    choose = (col == src).astype(F32).astype(BF)

    def unpack(slot):
        pages = [raw_ref[pos_ref[slot + i]] for i in range(BLK)]
        both = jnp.dot(
            choose, jnp.concatenate(pages, axis=1), preferred_element_type=F32
        ).astype(BF)
        for i in range(BLK):
            kc[slot + i] = both[:page_len, i * width : (i + 1) * width]
            vc[slot + i] = both[page_len:, i * width : (i + 1) * width]

    for r in range(n_req):
        unpack(r * n_page)
    for r in range(n_req):
        for b in range(1, n_page // BLK):
            @pl.when(counts_ref[0, r] > b * BLK)
            def _():
                unpack(r * n_page + b * BLK)

    knp[:back, :] = jnp.zeros((back, width), BF)
    vnp[:back, :] = jnp.zeros((back, width), BF)
    knp[back:, :] = kn_ref[...]
    vnp[back:, :] = vn_ref[...]

    lane = lax.broadcasted_iota(jnp.int32, (1, width), 1)
    lane_f = lax.broadcasted_iota(jnp.int32, (1, KCH), 1).astype(F32)
    delta = [bias_ref[0, group * per + a] - bias_ref[1, group * per + a] for a in range(per)]
    starts = [jnp.int32(0)]
    for r in range(n_req):
        starts.append(starts[-1] + lens_ref[0, r])

    def tile_body(t, carry):
        row0 = pl.multiple_of(t * TILE, TILE)
        qt = q_ref[pl.ds(row0, TILE), :].astype(F32)
        for a in range(per):
            mine = (lane >= a * HD) & (lane < (a + 1) * HD)
            qbd[a * TILE : (a + 1) * TILE, :] = jnp.where(mine, qt, 0.0).astype(BF)

        row = (row0 + lax.broadcasted_iota(jnp.int32, (TILE, KCH), 0)).astype(F32)
        start_row = jnp.zeros((TILE, KCH), F32)
        offset = jnp.zeros((TILE, KCH), F32)
        blocks = jnp.int32(1)
        for r in range(n_req):
            start, end, live = starts[r], starts[r + 1], counts_ref[0, r]
            inside = (row >= start.astype(F32)) & (row < end.astype(F32))
            start_row = jnp.where(inside, start.astype(F32), start_row)
            offset = jnp.where(inside, (live * page_len - start).astype(F32), offset)
            here = (start < row0 + TILE) & (end > row0)
            blocks = jnp.maximum(blocks, jnp.where(here, (live + BLK - 1) // BLK, 0))
        var_first = jnp.floor((row + offset + 0.5) * (1.0 / VARLEN)) * VARLEN
        info[0] = row
        info[1] = start_row
        info[2] = var_first
        info[3] = var_first - offset

        for b in range(n_page // BLK):
            @pl.when(b < blocks)
            def _():
                for i in range(BLK):
                    sbuf[b * BLK + i] = jnp.full((per * TILE, KCH), NEG, F32)

        def scores(keys):
            return lax.dot_general(
                qbd[...], keys, (((1,), (1,)), ((), ())), preferred_element_type=F32
            )

        for r in range(n_req):
            start, end, live = starts[r], starts[r + 1], counts_ref[0, r]
            here = (start < row0 + TILE) & (end > row0)
            for b in range(n_page // BLK):
                @pl.when(here & (live > b * BLK))
                def _():
                    s_all = scores(
                        kc[r * n_page + b * BLK : r * n_page + (b + 1) * BLK].reshape(
                            BLK * page_len, width
                        )
                    )
                    row = info[0]
                    inside = (row >= start.astype(F32)) & (row < end.astype(F32))
                    for i in range(BLK):
                        page = b * BLK + i
                        dead = jnp.where(page < live, 0.0, NEG)
                        same = info[2] <= lane_f + page * page_len
                        for a in range(per):
                            part = slice(a * TILE, (a + 1) * TILE)
                            s = s_all[part, i * KCH : (i + 1) * KCH]
                            s = s + jnp.where(same, delta[a] + dead, dead)
                            sbuf[page, part, :] = jnp.where(inside, s, sbuf[page, part, :])

        s_all = scores(knp[pl.ds(row0, back + TILE), :])
        for i in range(n_new):
            key_row = lane_f + (row0 - back + i * KCH).astype(F32)
            allowed = (key_row >= info[1]) & (key_row <= info[0])
            same = info[3] <= key_row
            for a in range(per):
                part = slice(a * TILE, (a + 1) * TILE)
                s = s_all[part, i * KCH : (i + 1) * KCH]
                s = jnp.where(allowed, s + jnp.where(same, delta[a], 0.0), NEG)
                sbuf[n_page + i, part, :] = s

        for a in range(per):
            part = slice(a * TILE, (a + 1) * TILE)

            def top_block(b, top):
                for i in range(BLK):
                    top = jnp.maximum(top, sbuf[b * BLK + i, part, :])
                return top

            top = sbuf[n_page, part, :]
            for i in range(1, n_new):
                top = jnp.maximum(top, sbuf[n_page + i, part, :])
            top = lax.fori_loop(0, blocks, top_block, top)
            peak = jnp.broadcast_to(jnp.max(top, axis=1, keepdims=True), (TILE, KCH))

            def weigh(c, total):
                p = jnp.exp(sbuf[c, part, :] - peak)
                sbuf[c, part, :] = p
                return total + p

            def weigh_block(b, total):
                for i in range(BLK):
                    total = weigh(b * BLK + i, total)
                return total

            total = jnp.zeros((TILE, KCH), F32)
            for i in range(n_new):
                total = weigh(n_page + i, total)
            total = lax.fori_loop(0, blocks, weigh_block, total)
            inverse = jnp.broadcast_to(
                1.0 / jnp.sum(total, axis=1, keepdims=True), (TILE, KCH)
            )
            for i in range(n_new):
                c = n_page + i
                wbuf[part, c * KCH : (c + 1) * KCH] = (sbuf[c, part, :] * inverse).astype(BF)
            for b in range(n_page // BLK):
                @pl.when(b < blocks)
                def _():
                    for i in range(BLK):
                        c = b * BLK + i
                        wbuf[part, c * KCH : (c + 1) * KCH] = (
                            sbuf[c, part, :] * inverse
                        ).astype(BF)

        obuf[...] = jnp.dot(
            wbuf[:, n_page * KCH :], vnp[pl.ds(row0, back + TILE), :],
            preferred_element_type=F32,
        )
        for r in range(n_req):
            start, end, live = starts[r], starts[r + 1], counts_ref[0, r]
            here = (start < row0 + TILE) & (end > row0)
            for b in range(n_page // BLK):
                @pl.when(here & (live > b * BLK))
                def _():
                    o = jnp.dot(
                        wbuf[:, b * BLK * KCH : (b + 1) * BLK * KCH],
                        vc[r * n_page + b * BLK : r * n_page + (b + 1) * BLK].reshape(
                            BLK * page_len, width
                        ),
                        preferred_element_type=F32,
                    )
                    row = info[0]
                    inside = (row >= start.astype(F32)) & (row < end.astype(F32))
                    for a in range(per):
                        part = slice(a * TILE, (a + 1) * TILE)
                        before = obuf[part, :]
                        obuf[part, :] = jnp.where(inside[:, :width], before + o[part], before)
        o = obuf[:TILE, :]
        for a in range(1, per):
            o = jnp.where(lane >= a * HD, obuf[a * TILE : (a + 1) * TILE, :], o)
        out_ref[pl.ds(row0, TILE), :] = o.astype(BF)
        return carry

    lax.fori_loop(0, rows // TILE, tile_body, 0)


def attend(group, lanes, most, lens, counts, pos, bias, q, kn, vn, raw):
    rows = q.shape[0]
    per = lanes // HD
    page_len = raw.shape[1] // 2
    slots = raw.shape[0]
    back = -(-most // KCH) * KCH
    n_all = PAGES_REQ + (back + TILE) // KCH
    smem = pl.BlockSpec(memory_space=pltpu.SMEM)
    part = pl.BlockSpec((rows, lanes), lambda i: (0, group))
    return pl.pallas_call(
        functools.partial(attend_kernel, group, per),
        grid=(1,),
        out_shape=jax.ShapeDtypeStruct((rows, lanes), BF),
        in_specs=[smem] * 4
        + [part] * 3
        + [pl.BlockSpec(raw.shape, lambda i: (0, 0, 0), pipeline_mode=pl.Buffered(1))],
        out_specs=pl.BlockSpec((rows, lanes), lambda i: (0, 0)),
        scratch_shapes=[
            pltpu.VMEM((slots, page_len, lanes), BF),
            pltpu.VMEM((slots, page_len, lanes), BF),
            pltpu.VMEM((back + rows, lanes), BF),
            pltpu.VMEM((back + rows, lanes), BF),
            pltpu.VMEM((per * TILE, lanes), BF),
            pltpu.VMEM((4, TILE, KCH), F32),
            pltpu.VMEM((n_all, per * TILE, KCH), F32),
            pltpu.VMEM((per * TILE, n_all * KCH), BF),
            pltpu.VMEM((per * TILE, lanes), F32),
        ],
        compiler_params=pltpu.CompilerParams(vmem_limit_bytes=32 << 20),
        cost_estimate=pl.CostEstimate(
            flops=4 * rows * per * 1408 * lanes, bytes_accessed=raw.size * 2, transcendentals=0
        ),
        name="attend",
    )(lens, counts, pos, bias, q, kn, vn, raw)


def shift(value, axis, n, k):
    return lax.ppermute(value, axis, [(i, (i + k) % n) for i in range(n)])


def whole_weight(own, halves, dp, n_dp):
    halves = jnp.stack(halves)
    twins = lax.ppermute(halves, "dp", [(i, i ^ 1) for i in range(n_dp)])
    rest = jnp.where(
        dp % 2 == 0,
        jnp.concatenate([halves, twins], axis=1),
        jnp.concatenate([twins, halves], axis=1),
    )
    return jnp.concatenate([own[None], rest], axis=0)


def per_device(
    tokens,
    attn_gain,
    ffn_gain,
    w_qkv,
    w_out,
    w_gateup,
    w_down,
    variate_bias,
    adapter_down,
    adapter_up,
    owner_table,
    lengths,
    adapter_ids,
    page_counts,
    page_table,
    cache_pool,
):
    n_tp = lax.axis_size("tensor")
    n_dp = lax.axis_size("dp")
    tp = lax.axis_index("tensor")
    dp = lax.axis_index("dp")
    me = dp.astype(jnp.int32).reshape(1)
    tp_id = tp.astype(jnp.int32).reshape(1)
    row_count, d_model = tokens.shape
    tok_total = row_count * n_tp
    width = w_out.shape[0]
    page_len = cache_pool.shape[1]
    pool_dev = cache_pool.shape[0]
    cap = max(1, page_table.shape[1] // n_dp)
    far_first = [k for k in range(1, n_tp)]
    lanes = min(width, 2 * HD)
    n_group = width // lanes
    slots = n_dp * cap
    dd = d_model // n_tp
    n_loc, _, rank, _ = adapter_down.shape
    span = 2 * rank

    toks = [tokens] + [shift(tokens, "tensor", n_tp, k) for k in far_first]

    down_part = lax.dynamic_slice_in_dim(adapter_down, tp * dd, dd, 3).reshape(n_loc * span, dd)
    names = jnp.concatenate([page_table // pool_dev, page_table % pool_dev], axis=0).astype(BF)
    names = jnp.pad(names, ((0, 14), (0, dd - names.shape[1])))
    payload = jnp.concatenate([down_part, adapter_up.reshape(n_loc * span, width), names], axis=0)
    gathered = lax.all_gather(payload, "dp", axis=0)
    asked = gathered[:, 2 * n_loc * span : 2 * n_loc * span + 2, : page_table.shape[1]]
    picked = pick(me, asked.astype(jnp.int32), cache_pool, n_dp, cap, lanes)
    send = lax.optimization_barrier((picked[0], toks[1:]))[0]
    fetched = [lax.all_to_all(send, "dp", split_axis=0, concat_axis=0, tiled=True)]

    own_half = lax.dynamic_slice_in_dim(w_out, (dp % 2) * (width // 2), width // 2, 0)
    gathered, lengths_b = lax.optimization_barrier((gathered, lengths, picked))[:2]
    down_named, up_named = named(owner_table, adapter_ids, gathered, n_loc, span)
    downs = [down_named] + [shift(down_named, "tensor", n_tp, k) for k in far_first]

    _, position = token_layout(lengths_b[0], page_counts[0], page_len, tok_total)
    index = jnp.arange(2 * HD, dtype=jnp.int32)
    frequency = 10000.0 ** (-2.0 * (index % (HD // 2)).astype(F32) / HD)
    angles = (position % VARLEN).astype(F32)[:, None] * frequency[None, :]
    sign = jnp.where(index % HD < HD // 2, -1.0, 1.0).astype(F32)
    query, new_keys, new_values, buffer_pos = project(
        tp_id, lengths, page_table, attn_gain.reshape(1, d_model), w_qkv, up_named,
        jnp.cos(angles), jnp.sin(angles) * sign[None, :], toks, downs, n_dp, cap, pool_dev,
    )
    own_half = lax.optimization_barrier((own_half, query))[0]
    halves = [shift(own_half, "tensor", n_tp, k) for k in far_first]
    for a in range(1, n_group):
        send, _ = lax.optimization_barrier((picked[a], fetched[-1]))
        fetched.append(lax.all_to_all(send, "dp", split_axis=0, concat_axis=0, tiled=True))
    fetched = [f.reshape(slots, 2 * page_len, lanes) for f in fetched]

    all_tokens = jnp.zeros((n_tp, row_count, d_model), BF)
    for k, block in enumerate(toks):
        all_tokens = lax.dynamic_update_index_in_dim(all_tokens, block, (tp - k) % n_tp, 0)

    n_chunk = max(1, row_count // CHUNK)
    sub = row_count // n_chunk
    base = all_tokens.astype(F32).reshape(tok_total, d_model)

    def mixed(blocks, a):
        w_parts = w_whole.reshape(n_tp, n_group, lanes, d_model)
        return jnp.dot(
            jnp.concatenate(blocks, axis=1),
            w_parts[:, a].reshape(n_tp * lanes, d_model),
            preferred_element_type=F32,
        )

    def attended(a, q):
        return attend(
            a, lanes, 2 * TILE, lengths, page_counts, buffer_pos, variate_bias,
            q, new_keys, new_values, fetched[a],
        )

    w_whole = None
    for a in range(n_group - 1):
        mix = attended(a, query)
        if w_whole is None:
            mix, halves = lax.optimization_barrier((mix, halves))
            w_whole = whole_weight(w_out, halves, dp, n_dp)
        blocks = [mix] + [shift(mix, "tensor", n_tp, k) for k in far_first]
        base = base + mixed(blocks, a)
        query, base = lax.optimization_barrier((query, base))
    if w_whole is None:
        w_whole = whole_weight(w_out, halves, dp, n_dp)
    mix = attended(n_group - 1, query).reshape(n_tp, n_chunk, sub, lanes)
    base = base.reshape(n_tp, n_chunk, sub, d_model)
    gathered_mix = []
    for c in range(n_chunk):
        own = mix[:, c].reshape(n_tp * sub, lanes)
        gathered_mix.append([own] + [shift(own, "tensor", n_tp, k) for k in far_first])
    outs = []
    pieces = None
    for c in range(n_chunk):
        blocks = gathered_mix[c]
        if pieces is not None:
            blocks = lax.optimization_barrier((blocks, pieces))[0]
        residual = base[:, c].reshape(n_tp * sub, d_model) + mixed(blocks, n_group - 1)
        ffn_in = normalize(residual, ffn_gain).astype(BF)
        gate_up = jnp.einsum("td,kdf->ktf", ffn_in, w_gateup, preferred_element_type=F32)
        hidden = (jax.nn.silu(gate_up[0]) * gate_up[1]).astype(BF)
        down = jnp.dot(hidden, w_down, preferred_element_type=F32).reshape(n_tp, sub, d_model)
        total = lax.dynamic_index_in_dim(down, tp, 0, False)
        total = total + lax.dynamic_index_in_dim(
            residual.reshape(n_tp, sub, d_model), tp, 0, False
        )
        down = down.astype(BF)
        pieces = [lax.dynamic_index_in_dim(down, (tp + k) % n_tp, 0, False) for k in far_first]
        for k, piece in zip(far_first, pieces):
            total = total + shift(piece, "tensor", n_tp, k).astype(F32)
        outs.append(total.astype(BF))
    return jnp.concatenate(outs, axis=0)


def solution(mesh):
    return jax.shard_map(
        per_device,
        mesh=mesh,
        in_specs=(
            P(("dp", "tensor"), None),
            P(),
            P(),
            P(None, None, "tensor"),
            P("tensor", None),
            P(None, None, "tensor"),
            P("tensor", None),
            P(None, "tensor"),
            P("dp", None, None, None),
            P("dp", None, None, "tensor"),
            P(),
            P("dp", None),
            P("dp", None),
            P("dp", None),
            P("dp", None),
            P("dp", None, None, "tensor"),
        ),
        out_specs=P(("dp", "tensor"), None),
        check_vma=False,
    )
```

```python
import functools

import jax
import jax.numpy as jnp
from jax import lax
from jax.experimental import pallas as pl
from jax.experimental.pallas import tpu as pltpu
from jax.sharding import PartitionSpec as P

HD = 64
PAGES_REQ = 8
VARLEN = 160
TILE = 128
KCH = 128
BLK = 4
CHUNK = 64
BF = jnp.bfloat16
F32 = jnp.float32
NEG = -1e30
LIGHT = pl.CostEstimate(flops=1000, bytes_accessed=1000, transcendentals=0)


def normalize(values, gain):
    values = values.astype(F32)
    inv_scale = lax.rsqrt(jnp.mean(values * values, axis=-1, keepdims=True) + 1e-05)
    return values * inv_scale * gain.astype(F32)


def token_layout(req_lens, live_counts, page_len, tok_total):
    end_pos = jnp.cumsum(req_lens, dtype=jnp.int32)
    starts = end_pos - req_lens
    tok_index = jnp.arange(tok_total, dtype=jnp.int32)
    request = jnp.sum(
        (tok_index[:, None] >= end_pos[None, :]).astype(jnp.int32), axis=1, dtype=jnp.int32
    )
    onehot = request[:, None] == jnp.arange(req_lens.shape[0], dtype=jnp.int32)[None, :]
    first_pos = jnp.sum(jnp.where(onehot, starts[None, :], 0), axis=1, dtype=jnp.int32)
    cached = jnp.sum(jnp.where(onehot, live_counts[None, :], 0), axis=1, dtype=jnp.int32)
    return (onehot, cached * page_len + tok_index - first_pos)


def pick_kernel(n_dp, cap, me_ref, asked_ref, pool_ref, *rest):
    n_out = len(rest) - 3
    outs, (buf, sem_in, sem_out) = rest[:n_out], rest[n_out:]
    lanes = outs[0].shape[-1]
    me = me_ref[0]
    slots = asked_ref.shape[2]

    def find(g, carry):
        count = jnp.int32(0)
        for p in range(slots):
            hit = asked_ref[g, 0, p] == me

            @pl.when(hit)
            def _():
                pltpu.make_async_copy(
                    pool_ref.at[asked_ref[g, 1, p]], buf.at[g, count], sem_in.at[g]
                ).start()

            count = count + hit.astype(jnp.int32)
        return carry

    lax.fori_loop(0, n_dp, find, 0)
    done = []
    for g in range(n_dp):
        pltpu.make_async_copy(pool_ref.at[pl.ds(0, cap)], buf.at[g], sem_in.at[g]).wait()
        for a in range(n_out):
            copy = pltpu.make_async_copy(
                buf.at[g, :, :, :, pl.ds(a * lanes, lanes)], outs[a].at[g], sem_out.at[a, g]
            )
            copy.start()
            done.append(copy)
    for copy in done:
        copy.wait()


def pick(me, asked, pool, n_dp, cap, lanes):
    smem = pl.BlockSpec(memory_space=pltpu.SMEM)
    hbm = pl.BlockSpec(memory_space=pl.ANY)
    n_out = pool.shape[-1] // lanes
    shape = (n_dp, cap) + pool.shape[1:-1]
    return pl.pallas_call(
        functools.partial(pick_kernel, n_dp, cap),
        out_shape=[jax.ShapeDtypeStruct(shape + (lanes,), pool.dtype)] * n_out,
        in_specs=[smem, smem, hbm],
        out_specs=[hbm] * n_out,
        scratch_shapes=[
            pltpu.VMEM(shape + pool.shape[-1:], pool.dtype),
            pltpu.SemaphoreType.DMA((n_dp,)),
            pltpu.SemaphoreType.DMA((n_out, n_dp)),
        ],
        cost_estimate=LIGHT,
        name="pick_pages",
    )(me, asked, pool)


def named_kernel(n_loc, span, table_ref, ids_ref, all_ref, down_out, up_out, down_ref, up_ref, sem):
    copies = []
    for r in range(ids_ref.shape[1]):
        slot = table_ref[ids_ref[0, r]]
        home, inner = slot // n_loc, slot % n_loc
        for half, out in ((0, down_ref), (1, up_ref)):
            base = pl.multiple_of((half * n_loc + inner) * span, span)
            copy = pltpu.make_async_copy(
                all_ref.at[home, pl.ds(base, span)], out.at[pl.ds(r * span, span)], sem.at[r, half]
            )
            copy.start()
            copies.append(copy)
    for copy in copies:
        copy.wait()
    last = [
        pltpu.make_async_copy(down_ref, down_out, sem.at[0, 0]),
        pltpu.make_async_copy(up_ref, up_out, sem.at[0, 1]),
    ]
    for copy in last:
        copy.start()
    for copy in last:
        copy.wait()


def named(owner_table, adapter_ids, gathered, n_loc, span):
    n_req = adapter_ids.shape[1]
    smem = pl.BlockSpec(memory_space=pltpu.SMEM)
    hbm = pl.BlockSpec(memory_space=pltpu.HBM)
    out = jax.ShapeDtypeStruct((n_req * span, gathered.shape[-1]), BF)
    return pl.pallas_call(
        functools.partial(named_kernel, n_loc, span),
        out_shape=(out, out),
        in_specs=[smem, smem, hbm],
        out_specs=(hbm, hbm),
        scratch_shapes=[
            pltpu.VMEM(out.shape, BF),
            pltpu.VMEM(out.shape, BF),
            pltpu.SemaphoreType.DMA((n_req, 2)),
        ],
        cost_estimate=LIGHT,
        name="named_adapters",
    )(owner_table, adapter_ids, gathered)


def project_kernel(n_tp, cap, pool_dev, tp_ref, lens_ref, table_ref, *rest):
    hbm_refs, rest = rest[: 5 + 2 * n_tp], rest[5 + 2 * n_tp :]
    q_ref, k_ref, v_ref, pos_ref, all_ref, down, count, *held = rest
    held, sem, sem_out = held[:-2], held[-2], held[-1]
    gain_ref, w_ref, up_ref, cos_ref, sin_ref, tok_ref = held
    tp = tp_ref[0]
    copies = []
    targets = list(held[:5]) + [tok_ref.at[k] for k in range(n_tp)]
    for k in range(n_tp):
        targets.append(down.at[lax.rem(tp - k + n_tp, n_tp)])
    for i in list(range(5, 5 + 2 * n_tp)) + list(range(5)):
        copy = pltpu.make_async_copy(hbm_refs[i], targets[i], sem.at[i])
        copy.start()
        copies.append(copy)
    _, rows, _ = tok_ref.shape
    width = q_ref.shape[1]
    n_low, dd = down.shape[1:]
    n_req = lens_ref.shape[1]
    rank = n_low // n_req // 2

    for g in range(count.shape[0]):
        count[g] = 0

    def place(p, carry):
        home = table_ref[0, p] // pool_dev
        seen = count[home]
        count[home] = seen + 1
        pos_ref[p] = home * cap + seen
        return carry

    lax.fori_loop(0, table_ref.shape[1], place, 0)

    for copy in copies:
        copy.wait()
    n_chunk, _, sub, _ = all_ref.shape
    stores = []
    for k in range(n_tp):
        for c in range(n_chunk):
            copy = pltpu.make_async_copy(
                tok_ref.at[k, pl.ds(c * sub, sub)],
                all_ref.at[c, lax.rem(tp - k + n_tp, n_tp)],
                sem_out.at[k, c],
            )
            copy.start()
            stores.append(copy)
    lane = lax.broadcasted_iota(jnp.int32, (1, 128), 1)
    first = jnp.bitwise_and(lane, HD - 1) < HD // 2

    def rope(u, cos, sin):
        parts = []
        for a in range(width // 128):
            part = u[:, a * 128 : (a + 1) * 128]
            other = jnp.where(
                first, pltpu.roll(part, 128 - HD // 2, 1), pltpu.roll(part, HD // 2, 1)
            )
            parts.append(part * cos + other * sin)
        return parts

    for k in range(n_tp):
        row0 = pl.multiple_of(lax.rem(tp - k + n_tp, n_tp) * rows, rows)
        x = tok_ref[k].astype(F32)
        inv = lax.rsqrt(jnp.mean(x * x, axis=1, keepdims=True) + 1e-05)
        normed = (x * inv * gain_ref[...].astype(F32)).astype(BF)
        low = jnp.zeros((rows, n_low), F32)
        for j in range(n_tp):
            low = low + lax.dot_general(
                normed[:, j * dd : (j + 1) * dd], down[j], (((1,), (1,)), ((), ())),
                preferred_element_type=F32,
            )
        row = row0 + lax.broadcasted_iota(jnp.int32, (rows, n_low), 0)
        col = lax.broadcasted_iota(jnp.int32, (rows, n_low), 1)
        request = jnp.zeros((rows, n_low), jnp.int32)
        end = jnp.int32(0)
        for r in range(n_req - 1):
            end = end + lens_ref[0, r]
            request = request + (row >= end).astype(jnp.int32)
        own = col // (2 * rank) == request
        kind = (col // rank) % 2
        deltas = []
        for kk in range(2):
            part = jnp.where(own & (kind == kk), low, 0.0).astype(BF)
            deltas.append(jnp.dot(part, up_ref[...], preferred_element_type=F32))
        cos = cos_ref[pl.ds(row0, rows), :]
        sin = sin_ref[pl.ds(row0, rows), :]
        q = jnp.dot(normed, w_ref[0], preferred_element_type=F32) + deltas[0]
        for a, part in enumerate(rope(q, cos, sin)):
            part = part.astype(BF).astype(F32) * (HD ** -0.5)
            q_ref[pl.ds(row0, rows), a * 128 : (a + 1) * 128] = part.astype(BF)
        kk = jnp.dot(normed, w_ref[1], preferred_element_type=F32)
        for a, part in enumerate(rope(kk, cos, sin)):
            k_ref[pl.ds(row0, rows), a * 128 : (a + 1) * 128] = part.astype(BF)
        v = jnp.dot(normed, w_ref[2], preferred_element_type=F32) + deltas[1]
        v_ref[pl.ds(row0, rows), :] = v.astype(BF)
    for copy in stores:
        copy.wait()


def project(
    tp, lens, table, gain, w_qkv, up, cos, sin, toks, downs, n_dp, cap, pool_dev, n_chunk
):
    n_tp = len(toks)
    sub = toks[0].shape[0] // n_chunk
    rows = toks[0].shape[0] * n_tp
    width = w_qkv.shape[2]
    smem = pl.BlockSpec(memory_space=pltpu.SMEM)
    vmem = pl.BlockSpec(memory_space=pltpu.VMEM)
    out = jax.ShapeDtypeStruct((rows, width), BF)
    return pl.pallas_call(
        functools.partial(project_kernel, n_tp, cap, pool_dev),
        out_shape=(
            out, out, out, jax.ShapeDtypeStruct((table.shape[1],), jnp.int32),
            jax.ShapeDtypeStruct((n_chunk, n_tp, sub, toks[0].shape[1]), BF),
        ),
        in_specs=[smem] * 3 + [pl.BlockSpec(memory_space=pltpu.HBM)] * (5 + 2 * n_tp),
        out_specs=(vmem, vmem, vmem, smem, pl.BlockSpec(memory_space=pltpu.HBM)),
        scratch_shapes=[
            pltpu.VMEM((n_tp,) + downs[0].shape, BF),
            pltpu.SMEM((n_dp,), jnp.int32),
        ]
        + [pltpu.VMEM(x.shape, x.dtype) for x in (gain, w_qkv, up, cos, sin)]
        + [
            pltpu.VMEM((n_tp,) + toks[0].shape, BF),
            pltpu.SemaphoreType.DMA((5 + 2 * n_tp,)),
            pltpu.SemaphoreType.DMA((n_tp, n_chunk)),
        ],
        compiler_params=pltpu.CompilerParams(vmem_limit_bytes=60 << 20),
        cost_estimate=LIGHT,
        name="project",
    )(tp, lens, table, gain, w_qkv, up, cos, sin, *toks, *downs)


def attend_kernel(
    group, per, lens_ref, counts_ref, pos_ref, bias_ref,
    q_ref, kn_ref, vn_ref, raw_ref, out_ref,
    kc, vc, knp, vnp, qbd, info, sbuf, wbuf, obuf,
):
    page_len = kc.shape[1]
    width = q_ref.shape[1]
    rows = q_ref.shape[0]
    n_req = lens_ref.shape[1]
    back = knp.shape[0] - rows
    n_page = PAGES_REQ
    n_new = (back + TILE) // KCH

    row = lax.broadcasted_iota(jnp.int32, (2 * page_len, 2 * page_len), 0)
    col = lax.broadcasted_iota(jnp.int32, (2 * page_len, 2 * page_len), 1)
    src = jnp.where(row < page_len, 2 * row, 2 * row - (2 * page_len - 1))
    choose = (col == src).astype(F32).astype(BF)

    def unpack(slot):
        pages = [raw_ref[pos_ref[slot + i]] for i in range(BLK)]
        both = jnp.dot(
            choose, jnp.concatenate(pages, axis=1), preferred_element_type=F32
        ).astype(BF)
        for i in range(BLK):
            kc[slot + i] = both[:page_len, i * width : (i + 1) * width]
            vc[slot + i] = both[page_len:, i * width : (i + 1) * width]

    for r in range(n_req):
        unpack(r * n_page)
    for r in range(n_req):
        for b in range(1, n_page // BLK):
            @pl.when(counts_ref[0, r] > b * BLK)
            def _():
                unpack(r * n_page + b * BLK)

    knp[:back, :] = jnp.zeros((back, width), BF)
    vnp[:back, :] = jnp.zeros((back, width), BF)
    knp[back:, :] = kn_ref[...]
    vnp[back:, :] = vn_ref[...]

    lane = lax.broadcasted_iota(jnp.int32, (1, width), 1)
    lane_f = lax.broadcasted_iota(jnp.int32, (1, KCH), 1).astype(F32)
    delta = [bias_ref[0, group * per + a] - bias_ref[1, group * per + a] for a in range(per)]
    starts = [jnp.int32(0)]
    for r in range(n_req):
        starts.append(starts[-1] + lens_ref[0, r])

    def tile_body(t, carry):
        row0 = pl.multiple_of(t * TILE, TILE)
        qt = q_ref[pl.ds(row0, TILE), :].astype(F32)
        for a in range(per):
            mine = (lane >= a * HD) & (lane < (a + 1) * HD)
            qbd[a * TILE : (a + 1) * TILE, :] = jnp.where(mine, qt, 0.0).astype(BF)

        row = (row0 + lax.broadcasted_iota(jnp.int32, (TILE, KCH), 0)).astype(F32)
        start_row = jnp.zeros((TILE, KCH), F32)
        offset = jnp.zeros((TILE, KCH), F32)
        blocks = jnp.int32(1)
        for r in range(n_req):
            start, end, live = starts[r], starts[r + 1], counts_ref[0, r]
            inside = (row >= start.astype(F32)) & (row < end.astype(F32))
            start_row = jnp.where(inside, start.astype(F32), start_row)
            offset = jnp.where(inside, (live * page_len - start).astype(F32), offset)
            here = (start < row0 + TILE) & (end > row0)
            blocks = jnp.maximum(blocks, jnp.where(here, (live + BLK - 1) // BLK, 0))
        var_first = jnp.floor((row + offset + 0.5) * (1.0 / VARLEN)) * VARLEN
        info[0] = row
        info[1] = start_row
        info[2] = var_first
        info[3] = var_first - offset

        for b in range(n_page // BLK):
            @pl.when(b < blocks)
            def _():
                for i in range(BLK):
                    sbuf[b * BLK + i] = jnp.full((per * TILE, KCH), NEG, F32)

        def scores(keys):
            return lax.dot_general(
                qbd[...], keys, (((1,), (1,)), ((), ())), preferred_element_type=F32
            )

        for r in range(n_req):
            start, end, live = starts[r], starts[r + 1], counts_ref[0, r]
            here = (start < row0 + TILE) & (end > row0)
            for b in range(n_page // BLK):
                @pl.when(here & (live > b * BLK))
                def _():
                    s_all = scores(
                        kc[r * n_page + b * BLK : r * n_page + (b + 1) * BLK].reshape(
                            BLK * page_len, width
                        )
                    )
                    row = info[0]
                    inside = (row >= start.astype(F32)) & (row < end.astype(F32))
                    for i in range(BLK):
                        page = b * BLK + i
                        dead = jnp.where(page < live, 0.0, NEG)
                        same = info[2] <= lane_f + page * page_len
                        for a in range(per):
                            part = slice(a * TILE, (a + 1) * TILE)
                            s = s_all[part, i * KCH : (i + 1) * KCH]
                            s = s + jnp.where(same, delta[a] + dead, dead)
                            sbuf[page, part, :] = jnp.where(inside, s, sbuf[page, part, :])

        s_all = scores(knp[pl.ds(row0, back + TILE), :])
        for i in range(n_new):
            key_row = lane_f + (row0 - back + i * KCH).astype(F32)
            allowed = (key_row >= info[1]) & (key_row <= info[0])
            same = info[3] <= key_row
            for a in range(per):
                part = slice(a * TILE, (a + 1) * TILE)
                s = s_all[part, i * KCH : (i + 1) * KCH]
                s = jnp.where(allowed, s + jnp.where(same, delta[a], 0.0), NEG)
                sbuf[n_page + i, part, :] = s

        for a in range(per):
            part = slice(a * TILE, (a + 1) * TILE)

            def top_block(b, top):
                for i in range(BLK):
                    top = jnp.maximum(top, sbuf[b * BLK + i, part, :])
                return top

            top = sbuf[n_page, part, :]
            for i in range(1, n_new):
                top = jnp.maximum(top, sbuf[n_page + i, part, :])
            top = lax.fori_loop(0, blocks, top_block, top)
            peak = jnp.broadcast_to(jnp.max(top, axis=1, keepdims=True), (TILE, KCH))

            def weigh(c, total):
                p = jnp.exp(sbuf[c, part, :] - peak)
                sbuf[c, part, :] = p
                return total + p

            def weigh_block(b, total):
                for i in range(BLK):
                    total = weigh(b * BLK + i, total)
                return total

            total = jnp.zeros((TILE, KCH), F32)
            for i in range(n_new):
                total = weigh(n_page + i, total)
            total = lax.fori_loop(0, blocks, weigh_block, total)
            inverse = jnp.broadcast_to(
                1.0 / jnp.sum(total, axis=1, keepdims=True), (TILE, KCH)
            )
            for i in range(n_new):
                c = n_page + i
                wbuf[part, c * KCH : (c + 1) * KCH] = (sbuf[c, part, :] * inverse).astype(BF)
            for b in range(n_page // BLK):
                @pl.when(b < blocks)
                def _():
                    for i in range(BLK):
                        c = b * BLK + i
                        wbuf[part, c * KCH : (c + 1) * KCH] = (
                            sbuf[c, part, :] * inverse
                        ).astype(BF)

        obuf[...] = jnp.dot(
            wbuf[:, n_page * KCH :], vnp[pl.ds(row0, back + TILE), :],
            preferred_element_type=F32,
        )
        for r in range(n_req):
            start, end, live = starts[r], starts[r + 1], counts_ref[0, r]
            here = (start < row0 + TILE) & (end > row0)
            for b in range(n_page // BLK):
                @pl.when(here & (live > b * BLK))
                def _():
                    o = jnp.dot(
                        wbuf[:, b * BLK * KCH : (b + 1) * BLK * KCH],
                        vc[r * n_page + b * BLK : r * n_page + (b + 1) * BLK].reshape(
                            BLK * page_len, width
                        ),
                        preferred_element_type=F32,
                    )
                    row = info[0]
                    inside = (row >= start.astype(F32)) & (row < end.astype(F32))
                    for a in range(per):
                        part = slice(a * TILE, (a + 1) * TILE)
                        before = obuf[part, :]
                        obuf[part, :] = jnp.where(inside[:, :width], before + o[part], before)
        o = obuf[:TILE, :]
        for a in range(1, per):
            o = jnp.where(lane >= a * HD, obuf[a * TILE : (a + 1) * TILE, :], o)
        out_ref[pl.ds(row0, TILE), :] = o.astype(BF)
        return carry

    lax.fori_loop(0, rows // TILE, tile_body, 0)


def attend(group, lanes, most, lens, counts, pos, bias, q, kn, vn, raw):
    rows = q.shape[0]
    per = lanes // HD
    page_len = raw.shape[1] // 2
    slots = raw.shape[0]
    back = -(-most // KCH) * KCH
    n_all = PAGES_REQ + (back + TILE) // KCH
    smem = pl.BlockSpec(memory_space=pltpu.SMEM)
    part = pl.BlockSpec((rows, lanes), lambda i: (0, group))
    return pl.pallas_call(
        functools.partial(attend_kernel, group, per),
        grid=(1,),
        out_shape=jax.ShapeDtypeStruct((rows, lanes), BF),
        in_specs=[smem] * 4
        + [part] * 3
        + [pl.BlockSpec(raw.shape, lambda i: (0, 0, 0), pipeline_mode=pl.Buffered(1))],
        out_specs=pl.BlockSpec((rows, lanes), lambda i: (0, 0)),
        scratch_shapes=[
            pltpu.VMEM((slots, page_len, lanes), BF),
            pltpu.VMEM((slots, page_len, lanes), BF),
            pltpu.VMEM((back + rows, lanes), BF),
            pltpu.VMEM((back + rows, lanes), BF),
            pltpu.VMEM((per * TILE, lanes), BF),
            pltpu.VMEM((4, TILE, KCH), F32),
            pltpu.VMEM((n_all, per * TILE, KCH), F32),
            pltpu.VMEM((per * TILE, n_all * KCH), BF),
            pltpu.VMEM((per * TILE, lanes), F32),
        ],
        compiler_params=pltpu.CompilerParams(vmem_limit_bytes=60 << 20),
        cost_estimate=LIGHT,
        name="attend",
    )(lens, counts, pos, bias, q, kn, vn, raw)


def shift(value, axis, n, k):
    return lax.ppermute(value, axis, [(i, (i + k) % n) for i in range(n)])


def whole_weight(own, halves, dp, n_dp):
    halves = jnp.stack(halves)
    twins = lax.ppermute(halves, "dp", [(i, i ^ 1) for i in range(n_dp)])
    rest = jnp.where(
        dp % 2 == 0,
        jnp.concatenate([halves, twins], axis=1),
        jnp.concatenate([twins, halves], axis=1),
    )
    return jnp.concatenate([own[None], rest], axis=0)


def per_device(
    tokens,
    attn_gain,
    ffn_gain,
    w_qkv,
    w_out,
    w_gateup,
    w_down,
    variate_bias,
    adapter_down,
    adapter_up,
    owner_table,
    lengths,
    adapter_ids,
    page_counts,
    page_table,
    cache_pool,
):
    n_tp = lax.axis_size("tensor")
    n_dp = lax.axis_size("dp")
    tp = lax.axis_index("tensor")
    dp = lax.axis_index("dp")
    me = dp.astype(jnp.int32).reshape(1)
    tp_id = tp.astype(jnp.int32).reshape(1)
    row_count, d_model = tokens.shape
    tok_total = row_count * n_tp
    width = w_out.shape[0]
    page_len = cache_pool.shape[1]
    pool_dev = cache_pool.shape[0]
    cap = max(1, page_table.shape[1] // n_dp)
    far_first = [k for k in range(1, n_tp)]
    lanes = min(width, 2 * HD)
    n_group = width // lanes
    slots = n_dp * cap
    dd = d_model // n_tp
    n_loc, _, rank, _ = adapter_down.shape
    n_chunk = max(1, row_count // CHUNK)
    sub = row_count // n_chunk
    span = 2 * rank

    toks = [tokens] + [shift(tokens, "tensor", n_tp, k) for k in far_first]

    down_part = lax.dynamic_slice_in_dim(adapter_down, tp * dd, dd, 3).reshape(n_loc * span, dd)
    names = jnp.concatenate([page_table // pool_dev, page_table % pool_dev], axis=0).astype(BF)
    names = jnp.pad(names, ((0, 14), (0, dd - names.shape[1])))
    payload = jnp.concatenate([down_part, adapter_up.reshape(n_loc * span, width), names], axis=0)
    gathered = lax.all_gather(payload, "dp", axis=0)
    asked = gathered[:, 2 * n_loc * span : 2 * n_loc * span + 2, : page_table.shape[1]]
    picked = pick(me, asked.astype(jnp.int32), cache_pool, n_dp, cap, lanes)
    send = lax.optimization_barrier((picked[0], toks[1:-1]))[0]
    fetched = [lax.all_to_all(send, "dp", split_axis=0, concat_axis=0, tiled=True)]

    own_half = lax.dynamic_slice_in_dim(w_out, (dp % 2) * (width // 2), width // 2, 0)
    gathered, lengths_b = lax.optimization_barrier((gathered, lengths, send))[:2]
    down_named, up_named = named(owner_table, adapter_ids, gathered, n_loc, span)
    downs = [down_named] + [shift(down_named, "tensor", n_tp, k) for k in far_first]

    _, position = token_layout(lengths_b[0], page_counts[0], page_len, tok_total)
    index = jnp.arange(2 * HD, dtype=jnp.int32)
    frequency = 10000.0 ** (-2.0 * (index % (HD // 2)).astype(F32) / HD)
    angles = (position % VARLEN).astype(F32)[:, None] * frequency[None, :]
    sign = jnp.where(index % HD < HD // 2, -1.0, 1.0).astype(F32)
    query, new_keys, new_values, buffer_pos, all_tokens = project(
        tp_id, lengths, page_table, attn_gain.reshape(1, d_model), w_qkv, up_named,
        jnp.cos(angles), jnp.sin(angles) * sign[None, :], toks, downs, n_dp, cap, pool_dev, n_chunk,
    )
    own_half = lax.optimization_barrier((own_half, down_named))[0]
    halves = [shift(own_half, "tensor", n_tp, k) for k in far_first]
    halves = lax.optimization_barrier((halves, query))[0]
    for a in range(1, n_group):
        send, _ = lax.optimization_barrier((picked[a], fetched[-1]))
        fetched.append(lax.all_to_all(send, "dp", split_axis=0, concat_axis=0, tiled=True))
    fetched = [f.reshape(slots, 2 * page_len, lanes) for f in fetched]


    def mixed(blocks, a):
        w_parts = w_whole.reshape(n_tp, n_group, lanes, d_model)
        return jnp.dot(
            jnp.concatenate(blocks, axis=1),
            w_parts[:, a].reshape(n_tp * lanes, d_model),
            preferred_element_type=F32,
        )

    def attended(a, q):
        return attend(
            a, lanes, 2 * TILE, lengths, page_counts, buffer_pos, variate_bias,
            q, new_keys, new_values, fetched[a],
        )

    def by_chunk(mix):
        mix = mix.reshape(n_tp, n_chunk, sub, lanes)
        return [mix[:, c].reshape(n_tp * sub, lanes) for c in range(n_chunk)]

    early = []
    w_whole = None
    for a in range(n_group - 1):
        mix = attended(a, query)
        if w_whole is None:
            mix, halves = lax.optimization_barrier((mix, halves))
            w_whole = whole_weight(w_out, halves, dp, n_dp)
        blocks = [mix] + [shift(mix, "tensor", n_tp, k) for k in far_first]
        query, w_whole, blocks = lax.optimization_barrier((query, w_whole, blocks))
        early.append(blocks)
    if w_whole is None:
        w_whole = whole_weight(w_out, halves, dp, n_dp)
    last = attended(n_group - 1, query)
    early, last, w_whole = lax.optimization_barrier((early, last, w_whole))
    early = [[by_chunk(block) for block in blocks] for blocks in early]
    last = by_chunk(last)
    late = [[own] + [shift(own, "tensor", n_tp, k) for k in far_first] for own in last]
    outs = []
    pieces = None
    for c in range(n_chunk):
        residual = all_tokens[c].reshape(n_tp * sub, d_model).astype(F32)
        for a in range(n_group - 1):
            residual = residual + mixed([block[c] for block in early[a]], a)
        blocks = late[c]
        if pieces is not None:
            blocks = lax.optimization_barrier((blocks, pieces))[0]
        residual = residual + mixed(blocks, n_group - 1)
        ffn_in = normalize(residual, ffn_gain).astype(BF)
        gate_up = jnp.einsum("td,kdf->ktf", ffn_in, w_gateup, preferred_element_type=F32)
        hidden = (jax.nn.silu(gate_up[0]) * gate_up[1]).astype(BF)
        down = jnp.dot(hidden, w_down, preferred_element_type=F32).reshape(n_tp, sub, d_model)
        total = lax.dynamic_index_in_dim(down, tp, 0, False)
        total = total + lax.dynamic_index_in_dim(
            residual.reshape(n_tp, sub, d_model), tp, 0, False
        )
        down = down.astype(BF)
        pieces = [lax.dynamic_index_in_dim(down, (tp + k) % n_tp, 0, False) for k in far_first]
        for k, piece in zip(far_first, pieces):
            total = total + shift(piece, "tensor", n_tp, k).astype(F32)
        outs.append(total.astype(BF))
    return jnp.concatenate(outs, axis=0)


def solution(mesh):
    return jax.shard_map(
        per_device,
        mesh=mesh,
        in_specs=(
            P(("dp", "tensor"), None),
            P(),
            P(),
            P(None, None, "tensor"),
            P("tensor", None),
            P(None, None, "tensor"),
            P("tensor", None),
            P(None, "tensor"),
            P("dp", None, None, None),
            P("dp", None, None, "tensor"),
            P(),
            P("dp", None),
            P("dp", None),
            P("dp", None),
            P("dp", None),
            P("dp", None, None, "tensor"),
        ),
        out_specs=P(("dp", "tensor"), None),
        check_vma=False,
    )
```

```python
import functools

import jax
import jax.numpy as jnp
from jax import lax
from jax.experimental import pallas as pl
from jax.experimental.pallas import tpu as pltpu
from jax.sharding import PartitionSpec as P

HD = 64
PAGES_REQ = 8
VARLEN = 160
TILE = 128
KCH = 128
BLK = 4
CHUNK = 64
BF = jnp.bfloat16
F32 = jnp.float32
NEG = -1e30
LIGHT = pl.CostEstimate(flops=1000, bytes_accessed=1000, transcendentals=0)


def normalize(values, gain):
    values = values.astype(F32)
    inv_scale = lax.rsqrt(jnp.mean(values * values, axis=-1, keepdims=True) + 1e-05)
    return values * inv_scale * gain.astype(F32)


def token_layout(req_lens, live_counts, page_len, tok_total):
    end_pos = jnp.cumsum(req_lens, dtype=jnp.int32)
    starts = end_pos - req_lens
    tok_index = jnp.arange(tok_total, dtype=jnp.int32)
    request = jnp.sum(
        (tok_index[:, None] >= end_pos[None, :]).astype(jnp.int32), axis=1, dtype=jnp.int32
    )
    onehot = request[:, None] == jnp.arange(req_lens.shape[0], dtype=jnp.int32)[None, :]
    first_pos = jnp.sum(jnp.where(onehot, starts[None, :], 0), axis=1, dtype=jnp.int32)
    cached = jnp.sum(jnp.where(onehot, live_counts[None, :], 0), axis=1, dtype=jnp.int32)
    return (onehot, cached * page_len + tok_index - first_pos)


def pick_kernel(n_dp, cap, me_ref, asked_ref, pool_ref, *rest):
    n_out = len(rest) - 3
    outs, (buf, sem_in, sem_out) = rest[:n_out], rest[n_out:]
    lanes = outs[0].shape[-1]
    me = me_ref[0]
    slots = asked_ref.shape[2]

    def find(g, carry):
        count = jnp.int32(0)
        for p in range(slots):
            hit = asked_ref[g, 0, p] == me

            @pl.when(hit)
            def _():
                pltpu.make_async_copy(
                    pool_ref.at[asked_ref[g, 1, p]], buf.at[g, count], sem_in.at[g]
                ).start()

            count = count + hit.astype(jnp.int32)
        return carry

    lax.fori_loop(0, n_dp, find, 0)
    done = []
    for g in range(n_dp):
        pltpu.make_async_copy(pool_ref.at[pl.ds(0, cap)], buf.at[g], sem_in.at[g]).wait()
        for a in range(n_out):
            copy = pltpu.make_async_copy(
                buf.at[g, :, :, :, pl.ds(a * lanes, lanes)], outs[a].at[g], sem_out.at[a, g]
            )
            copy.start()
            done.append(copy)
    for copy in done:
        copy.wait()


def pick(me, asked, pool, n_dp, cap, lanes):
    smem = pl.BlockSpec(memory_space=pltpu.SMEM)
    hbm = pl.BlockSpec(memory_space=pl.ANY)
    n_out = pool.shape[-1] // lanes
    shape = (n_dp, cap) + pool.shape[1:-1]
    return pl.pallas_call(
        functools.partial(pick_kernel, n_dp, cap),
        out_shape=[jax.ShapeDtypeStruct(shape + (lanes,), pool.dtype)] * n_out,
        in_specs=[smem, smem, hbm],
        out_specs=[hbm] * n_out,
        scratch_shapes=[
            pltpu.VMEM(shape + pool.shape[-1:], pool.dtype),
            pltpu.SemaphoreType.DMA((n_dp,)),
            pltpu.SemaphoreType.DMA((n_out, n_dp)),
        ],
        cost_estimate=LIGHT,
        name="pick_pages",
    )(me, asked, pool)


def named_kernel(n_loc, span, table_ref, ids_ref, all_ref, down_out, up_out, down_ref, up_ref, sem):
    copies = []
    for r in range(ids_ref.shape[1]):
        slot = table_ref[ids_ref[0, r]]
        home, inner = slot // n_loc, slot % n_loc
        for half, out in ((0, down_ref), (1, up_ref)):
            base = pl.multiple_of((half * n_loc + inner) * span, span)
            copy = pltpu.make_async_copy(
                all_ref.at[home, pl.ds(base, span)], out.at[pl.ds(r * span, span)], sem.at[r, half]
            )
            copy.start()
            copies.append(copy)
    for copy in copies:
        copy.wait()
    last = [
        pltpu.make_async_copy(down_ref, down_out, sem.at[0, 0]),
        pltpu.make_async_copy(up_ref, up_out, sem.at[0, 1]),
    ]
    for copy in last:
        copy.start()
    for copy in last:
        copy.wait()


def named(owner_table, adapter_ids, gathered, n_loc, span):
    n_req = adapter_ids.shape[1]
    smem = pl.BlockSpec(memory_space=pltpu.SMEM)
    hbm = pl.BlockSpec(memory_space=pltpu.HBM)
    out = jax.ShapeDtypeStruct((n_req * span, gathered.shape[-1]), BF)
    return pl.pallas_call(
        functools.partial(named_kernel, n_loc, span),
        out_shape=(out, out),
        in_specs=[smem, smem, hbm],
        out_specs=(hbm, hbm),
        scratch_shapes=[
            pltpu.VMEM(out.shape, BF),
            pltpu.VMEM(out.shape, BF),
            pltpu.SemaphoreType.DMA((n_req, 2)),
        ],
        cost_estimate=LIGHT,
        name="named_adapters",
    )(owner_table, adapter_ids, gathered)


def project_kernel(n_tp, cap, pool_dev, tp_ref, lens_ref, table_ref, *rest):
    hbm_refs, rest = rest[: 5 + 2 * n_tp], rest[5 + 2 * n_tp :]
    q_ref, k_ref, v_ref, pos_ref, all_ref, down, count, *held = rest
    held, sem, sem_out = held[:-2], held[-2], held[-1]
    gain_ref, w_ref, up_ref, cos_ref, sin_ref, tok_ref = held
    tp = tp_ref[0]
    copies = []
    targets = list(held[:5]) + [tok_ref.at[k] for k in range(n_tp)]
    for k in range(n_tp):
        targets.append(down.at[lax.rem(tp - k + n_tp, n_tp)])
    for i in list(range(5, 5 + 2 * n_tp)) + list(range(5)):
        copy = pltpu.make_async_copy(hbm_refs[i], targets[i], sem.at[i])
        copy.start()
        copies.append(copy)
    _, rows, _ = tok_ref.shape
    width = q_ref.shape[1]
    n_low, dd = down.shape[1:]
    n_req = lens_ref.shape[1]
    rank = n_low // n_req // 2

    for g in range(count.shape[0]):
        count[g] = 0

    def place(p, carry):
        home = table_ref[0, p] // pool_dev
        seen = count[home]
        count[home] = seen + 1
        pos_ref[p] = home * cap + seen
        return carry

    lax.fori_loop(0, table_ref.shape[1], place, 0)

    for copy in copies:
        copy.wait()
    n_chunk, _, sub, _ = all_ref.shape
    stores = []
    for k in range(n_tp):
        for c in range(n_chunk):
            copy = pltpu.make_async_copy(
                tok_ref.at[k, pl.ds(c * sub, sub)],
                all_ref.at[c, lax.rem(tp - k + n_tp, n_tp)],
                sem_out.at[k, c],
            )
            copy.start()
            stores.append(copy)
    lane = lax.broadcasted_iota(jnp.int32, (1, 128), 1)
    first = jnp.bitwise_and(lane, HD - 1) < HD // 2

    def rope(u, cos, sin):
        parts = []
        for a in range(width // 128):
            part = u[:, a * 128 : (a + 1) * 128]
            other = jnp.where(
                first, pltpu.roll(part, 128 - HD // 2, 1), pltpu.roll(part, HD // 2, 1)
            )
            parts.append(part * cos + other * sin)
        return parts

    for k in range(n_tp):
        row0 = pl.multiple_of(lax.rem(tp - k + n_tp, n_tp) * rows, rows)
        x = tok_ref[k].astype(F32)
        inv = lax.rsqrt(jnp.mean(x * x, axis=1, keepdims=True) + 1e-05)
        normed = (x * inv * gain_ref[...].astype(F32)).astype(BF)
        low = jnp.zeros((rows, n_low), F32)
        for j in range(n_tp):
            low = low + lax.dot_general(
                normed[:, j * dd : (j + 1) * dd], down[j], (((1,), (1,)), ((), ())),
                preferred_element_type=F32,
            )
        row = row0 + lax.broadcasted_iota(jnp.int32, (rows, n_low), 0)
        col = lax.broadcasted_iota(jnp.int32, (rows, n_low), 1)
        request = jnp.zeros((rows, n_low), jnp.int32)
        end = jnp.int32(0)
        for r in range(n_req - 1):
            end = end + lens_ref[0, r]
            request = request + (row >= end).astype(jnp.int32)
        own = col // (2 * rank) == request
        kind = (col // rank) % 2
        deltas = []
        for kk in range(2):
            part = jnp.where(own & (kind == kk), low, 0.0).astype(BF)
            deltas.append(jnp.dot(part, up_ref[...], preferred_element_type=F32))
        cos = cos_ref[pl.ds(row0, rows), :]
        sin = sin_ref[pl.ds(row0, rows), :]
        q = jnp.dot(normed, w_ref[0], preferred_element_type=F32) + deltas[0]
        for a, part in enumerate(rope(q, cos, sin)):
            part = part.astype(BF).astype(F32) * (HD ** -0.5)
            q_ref[pl.ds(row0, rows), a * 128 : (a + 1) * 128] = part.astype(BF)
        kk = jnp.dot(normed, w_ref[1], preferred_element_type=F32)
        for a, part in enumerate(rope(kk, cos, sin)):
            k_ref[pl.ds(row0, rows), a * 128 : (a + 1) * 128] = part.astype(BF)
        v = jnp.dot(normed, w_ref[2], preferred_element_type=F32) + deltas[1]
        v_ref[pl.ds(row0, rows), :] = v.astype(BF)
    for copy in stores:
        copy.wait()


def project(
    tp, lens, table, gain, w_qkv, up, cos, sin, toks, downs, n_dp, cap, pool_dev, n_chunk
):
    n_tp = len(toks)
    sub = toks[0].shape[0] // n_chunk
    rows = toks[0].shape[0] * n_tp
    width = w_qkv.shape[2]
    smem = pl.BlockSpec(memory_space=pltpu.SMEM)
    vmem = pl.BlockSpec(memory_space=pltpu.VMEM)
    out = jax.ShapeDtypeStruct((rows, width), BF)
    return pl.pallas_call(
        functools.partial(project_kernel, n_tp, cap, pool_dev),
        out_shape=(
            out, out, out, jax.ShapeDtypeStruct((table.shape[1],), jnp.int32),
            jax.ShapeDtypeStruct((n_chunk, n_tp, sub, toks[0].shape[1]), BF),
        ),
        in_specs=[smem] * 3 + [pl.BlockSpec(memory_space=pltpu.HBM)] * (5 + 2 * n_tp),
        out_specs=(vmem, vmem, vmem, smem, pl.BlockSpec(memory_space=pltpu.HBM)),
        scratch_shapes=[
            pltpu.VMEM((n_tp,) + downs[0].shape, BF),
            pltpu.SMEM((n_dp,), jnp.int32),
        ]
        + [pltpu.VMEM(x.shape, x.dtype) for x in (gain, w_qkv, up, cos, sin)]
        + [
            pltpu.VMEM((n_tp,) + toks[0].shape, BF),
            pltpu.SemaphoreType.DMA((5 + 2 * n_tp,)),
            pltpu.SemaphoreType.DMA((n_tp, n_chunk)),
        ],
        compiler_params=pltpu.CompilerParams(vmem_limit_bytes=60 << 20),
        cost_estimate=LIGHT,
        name="project",
    )(tp, lens, table, gain, w_qkv, up, cos, sin, *toks, *downs)


def attend_kernel(
    group, per, lens_ref, counts_ref, pos_ref, bias_ref,
    q_ref, kn_ref, vn_ref, raw_ref, out_ref,
    kc, vc, knp, vnp, qbd, info, sbuf, wbuf, obuf,
):
    page_len = kc.shape[1]
    width = q_ref.shape[1]
    rows = q_ref.shape[0]
    n_req = lens_ref.shape[1]
    back = knp.shape[0] - rows
    n_page = PAGES_REQ
    n_new = (back + TILE) // KCH

    row = lax.broadcasted_iota(jnp.int32, (2 * page_len, 2 * page_len), 0)
    col = lax.broadcasted_iota(jnp.int32, (2 * page_len, 2 * page_len), 1)
    src = jnp.where(row < page_len, 2 * row, 2 * row - (2 * page_len - 1))
    choose = (col == src).astype(F32).astype(BF)

    def unpack(slot):
        pages = [raw_ref[pos_ref[slot + i]] for i in range(BLK)]
        both = jnp.dot(
            choose, jnp.concatenate(pages, axis=1), preferred_element_type=F32
        ).astype(BF)
        for i in range(BLK):
            kc[slot + i] = both[:page_len, i * width : (i + 1) * width]
            vc[slot + i] = both[page_len:, i * width : (i + 1) * width]

    for r in range(n_req):
        unpack(r * n_page)
    for r in range(n_req):
        for b in range(1, n_page // BLK):
            @pl.when(counts_ref[0, r] > b * BLK)
            def _():
                unpack(r * n_page + b * BLK)

    knp[:back, :] = jnp.zeros((back, width), BF)
    vnp[:back, :] = jnp.zeros((back, width), BF)
    knp[back:, :] = kn_ref[...]
    vnp[back:, :] = vn_ref[...]

    lane = lax.broadcasted_iota(jnp.int32, (1, width), 1)
    lane_f = lax.broadcasted_iota(jnp.int32, (1, KCH), 1).astype(F32)
    delta = [bias_ref[0, group * per + a] - bias_ref[1, group * per + a] for a in range(per)]
    starts = [jnp.int32(0)]
    for r in range(n_req):
        starts.append(starts[-1] + lens_ref[0, r])

    def tile_body(t, carry):
        row0 = pl.multiple_of(t * TILE, TILE)
        qt = q_ref[pl.ds(row0, TILE), :].astype(F32)
        for a in range(per):
            mine = (lane >= a * HD) & (lane < (a + 1) * HD)
            qbd[a * TILE : (a + 1) * TILE, :] = jnp.where(mine, qt, 0.0).astype(BF)

        row = (row0 + lax.broadcasted_iota(jnp.int32, (TILE, KCH), 0)).astype(F32)
        start_row = jnp.zeros((TILE, KCH), F32)
        offset = jnp.zeros((TILE, KCH), F32)
        blocks = jnp.int32(1)
        for r in range(n_req):
            start, end, live = starts[r], starts[r + 1], counts_ref[0, r]
            inside = (row >= start.astype(F32)) & (row < end.astype(F32))
            start_row = jnp.where(inside, start.astype(F32), start_row)
            offset = jnp.where(inside, (live * page_len - start).astype(F32), offset)
            here = (start < row0 + TILE) & (end > row0)
            blocks = jnp.maximum(blocks, jnp.where(here, (live + BLK - 1) // BLK, 0))
        var_first = jnp.floor((row + offset + 0.5) * (1.0 / VARLEN)) * VARLEN
        info[0] = row
        info[1] = start_row
        info[2] = var_first
        info[3] = var_first - offset

        for b in range(n_page // BLK):
            @pl.when(b < blocks)
            def _():
                for i in range(BLK):
                    sbuf[b * BLK + i] = jnp.full((per * TILE, KCH), NEG, F32)

        def scores(keys):
            return lax.dot_general(
                qbd[...], keys, (((1,), (1,)), ((), ())), preferred_element_type=F32
            )

        for r in range(n_req):
            start, end, live = starts[r], starts[r + 1], counts_ref[0, r]
            here = (start < row0 + TILE) & (end > row0)
            for b in range(n_page // BLK):
                @pl.when(here & (live > b * BLK))
                def _():
                    s_all = scores(
                        kc[r * n_page + b * BLK : r * n_page + (b + 1) * BLK].reshape(
                            BLK * page_len, width
                        )
                    )
                    row = info[0]
                    inside = (row >= start.astype(F32)) & (row < end.astype(F32))
                    for i in range(BLK):
                        page = b * BLK + i
                        dead = jnp.where(page < live, 0.0, NEG)
                        same = info[2] <= lane_f + page * page_len
                        for a in range(per):
                            part = slice(a * TILE, (a + 1) * TILE)
                            s = s_all[part, i * KCH : (i + 1) * KCH]
                            s = s + jnp.where(same, delta[a] + dead, dead)
                            sbuf[page, part, :] = jnp.where(inside, s, sbuf[page, part, :])

        s_all = scores(knp[pl.ds(row0, back + TILE), :])
        for i in range(n_new):
            key_row = lane_f + (row0 - back + i * KCH).astype(F32)
            allowed = (key_row >= info[1]) & (key_row <= info[0])
            same = info[3] <= key_row
            for a in range(per):
                part = slice(a * TILE, (a + 1) * TILE)
                s = s_all[part, i * KCH : (i + 1) * KCH]
                s = jnp.where(allowed, s + jnp.where(same, delta[a], 0.0), NEG)
                sbuf[n_page + i, part, :] = s

        for a in range(per):
            part = slice(a * TILE, (a + 1) * TILE)

            def top_block(b, top):
                for i in range(BLK):
                    top = jnp.maximum(top, sbuf[b * BLK + i, part, :])
                return top

            top = sbuf[n_page, part, :]
            for i in range(1, n_new):
                top = jnp.maximum(top, sbuf[n_page + i, part, :])
            top = lax.fori_loop(0, blocks, top_block, top)
            peak = jnp.broadcast_to(jnp.max(top, axis=1, keepdims=True), (TILE, KCH))

            def weigh(c, total):
                p = jnp.exp(sbuf[c, part, :] - peak)
                sbuf[c, part, :] = p
                return total + p

            def weigh_block(b, total):
                for i in range(BLK):
                    total = weigh(b * BLK + i, total)
                return total

            total = jnp.zeros((TILE, KCH), F32)
            for i in range(n_new):
                total = weigh(n_page + i, total)
            total = lax.fori_loop(0, blocks, weigh_block, total)
            inverse = jnp.broadcast_to(
                1.0 / jnp.sum(total, axis=1, keepdims=True), (TILE, KCH)
            )
            for i in range(n_new):
                c = n_page + i
                wbuf[part, c * KCH : (c + 1) * KCH] = (sbuf[c, part, :] * inverse).astype(BF)
            for b in range(n_page // BLK):
                @pl.when(b < blocks)
                def _():
                    for i in range(BLK):
                        c = b * BLK + i
                        wbuf[part, c * KCH : (c + 1) * KCH] = (
                            sbuf[c, part, :] * inverse
                        ).astype(BF)

        obuf[...] = jnp.dot(
            wbuf[:, n_page * KCH :], vnp[pl.ds(row0, back + TILE), :],
            preferred_element_type=F32,
        )
        for r in range(n_req):
            start, end, live = starts[r], starts[r + 1], counts_ref[0, r]
            here = (start < row0 + TILE) & (end > row0)
            for b in range(n_page // BLK):
                @pl.when(here & (live > b * BLK))
                def _():
                    o = jnp.dot(
                        wbuf[:, b * BLK * KCH : (b + 1) * BLK * KCH],
                        vc[r * n_page + b * BLK : r * n_page + (b + 1) * BLK].reshape(
                            BLK * page_len, width
                        ),
                        preferred_element_type=F32,
                    )
                    row = info[0]
                    inside = (row >= start.astype(F32)) & (row < end.astype(F32))
                    for a in range(per):
                        part = slice(a * TILE, (a + 1) * TILE)
                        before = obuf[part, :]
                        obuf[part, :] = jnp.where(inside[:, :width], before + o[part], before)
        o = obuf[:TILE, :]
        for a in range(1, per):
            o = jnp.where(lane >= a * HD, obuf[a * TILE : (a + 1) * TILE, :], o)
        out_ref[pl.ds(row0, TILE), :] = o.astype(BF)
        return carry

    lax.fori_loop(0, rows // TILE, tile_body, 0)


def attend(group, lanes, most, lens, counts, pos, bias, q, kn, vn, raw):
    rows = q.shape[0]
    per = lanes // HD
    page_len = raw.shape[1] // 2
    slots = raw.shape[0]
    back = -(-most // KCH) * KCH
    n_all = PAGES_REQ + (back + TILE) // KCH
    smem = pl.BlockSpec(memory_space=pltpu.SMEM)
    part = pl.BlockSpec((rows, lanes), lambda i: (0, group))
    return pl.pallas_call(
        functools.partial(attend_kernel, group, per),
        grid=(1,),
        out_shape=jax.ShapeDtypeStruct((rows, lanes), BF),
        in_specs=[smem] * 4
        + [part] * 3
        + [pl.BlockSpec(raw.shape, lambda i: (0, 0, 0), pipeline_mode=pl.Buffered(1))],
        out_specs=pl.BlockSpec((rows, lanes), lambda i: (0, 0)),
        scratch_shapes=[
            pltpu.VMEM((slots, page_len, lanes), BF),
            pltpu.VMEM((slots, page_len, lanes), BF),
            pltpu.VMEM((back + rows, lanes), BF),
            pltpu.VMEM((back + rows, lanes), BF),
            pltpu.VMEM((per * TILE, lanes), BF),
            pltpu.VMEM((4, TILE, KCH), F32),
            pltpu.VMEM((n_all, per * TILE, KCH), F32),
            pltpu.VMEM((per * TILE, n_all * KCH), BF),
            pltpu.VMEM((per * TILE, lanes), F32),
        ],
        compiler_params=pltpu.CompilerParams(vmem_limit_bytes=60 << 20),
        cost_estimate=LIGHT,
        name="attend",
    )(lens, counts, pos, bias, q, kn, vn, raw)


def shift(value, axis, n, k):
    return lax.ppermute(value, axis, [(i, (i + k) % n) for i in range(n)])


def whole_weight(own, halves, dp, n_dp):
    halves = jnp.stack(halves)
    twins = lax.ppermute(halves, "dp", [(i, i ^ 1) for i in range(n_dp)])
    rest = jnp.where(
        dp % 2 == 0,
        jnp.concatenate([halves, twins], axis=1),
        jnp.concatenate([twins, halves], axis=1),
    )
    return jnp.concatenate([own[None], rest], axis=0)


def per_device(
    tokens,
    attn_gain,
    ffn_gain,
    w_qkv,
    w_out,
    w_gateup,
    w_down,
    variate_bias,
    adapter_down,
    adapter_up,
    owner_table,
    lengths,
    adapter_ids,
    page_counts,
    page_table,
    cache_pool,
):
    n_tp = lax.axis_size("tensor")
    n_dp = lax.axis_size("dp")
    tp = lax.axis_index("tensor")
    dp = lax.axis_index("dp")
    me = dp.astype(jnp.int32).reshape(1)
    tp_id = tp.astype(jnp.int32).reshape(1)
    row_count, d_model = tokens.shape
    tok_total = row_count * n_tp
    width = w_out.shape[0]
    page_len = cache_pool.shape[1]
    pool_dev = cache_pool.shape[0]
    cap = max(1, page_table.shape[1] // n_dp)
    far_first = [k for k in range(1, n_tp)]
    lanes = min(width, 2 * HD)
    n_group = width // lanes
    slots = n_dp * cap
    dd = d_model // n_tp
    n_loc, _, rank, _ = adapter_down.shape
    n_chunk = max(1, row_count // CHUNK)
    sub = row_count // n_chunk
    span = 2 * rank

    toks = [tokens] + [shift(tokens, "tensor", n_tp, k) for k in far_first]

    down_part = lax.dynamic_slice_in_dim(adapter_down, tp * dd, dd, 3).reshape(n_loc * span, dd)
    names = jnp.concatenate([page_table // pool_dev, page_table % pool_dev], axis=0).astype(BF)
    names = jnp.pad(names, ((0, 14), (0, dd - names.shape[1])))
    payload = jnp.concatenate([down_part, adapter_up.reshape(n_loc * span, width), names], axis=0)
    gathered = lax.all_gather(payload, "dp", axis=0)
    asked = gathered[:, 2 * n_loc * span : 2 * n_loc * span + 2, : page_table.shape[1]]
    picked = pick(me, asked.astype(jnp.int32), cache_pool, n_dp, cap, lanes)
    send = lax.optimization_barrier((picked[0], toks[1:-1]))[0]
    fetched = [lax.all_to_all(send, "dp", split_axis=0, concat_axis=0, tiled=True)]

    own_half = lax.dynamic_slice_in_dim(w_out, (dp % 2) * (width // 2), width // 2, 0)
    gathered, lengths_b = lax.optimization_barrier((gathered, lengths, send))[:2]
    down_named, up_named = named(owner_table, adapter_ids, gathered, n_loc, span)
    downs = [down_named] + [shift(down_named, "tensor", n_tp, k) for k in far_first]

    _, position = token_layout(lengths_b[0], page_counts[0], page_len, tok_total)
    index = jnp.arange(2 * HD, dtype=jnp.int32)
    frequency = 10000.0 ** (-2.0 * (index % (HD // 2)).astype(F32) / HD)
    angles = (position % VARLEN).astype(F32)[:, None] * frequency[None, :]
    sign = jnp.where(index % HD < HD // 2, -1.0, 1.0).astype(F32)
    query, new_keys, new_values, buffer_pos, all_tokens = project(
        tp_id, lengths, page_table, attn_gain.reshape(1, d_model), w_qkv, up_named,
        jnp.cos(angles), jnp.sin(angles) * sign[None, :], toks, downs, n_dp, cap, pool_dev, n_chunk,
    )
    own_half = lax.optimization_barrier((own_half, down_named))[0]
    halves = [shift(own_half, "tensor", n_tp, k) for k in far_first]
    for a in range(1, n_group):
        send = lax.optimization_barrier((picked[a], fetched[-1], query, halves[:-1]))[0]
        fetched.append(lax.all_to_all(send, "dp", split_axis=0, concat_axis=0, tiled=True))
    fetched = [f.reshape(slots, 2 * page_len, lanes) for f in fetched]


    def mixed(blocks, a):
        w_parts = w_whole.reshape(n_tp, n_group, lanes, d_model)
        return jnp.dot(
            jnp.concatenate(blocks, axis=1),
            w_parts[:, a].reshape(n_tp * lanes, d_model),
            preferred_element_type=F32,
        )

    def attended(a, q):
        return attend(
            a, lanes, 2 * TILE, lengths, page_counts, buffer_pos, variate_bias,
            q, new_keys, new_values, fetched[a],
        )

    def by_chunk(mix):
        mix = mix.reshape(n_tp, n_chunk, sub, lanes)
        return [mix[:, c].reshape(n_tp * sub, lanes) for c in range(n_chunk)]

    early = []
    w_whole = None
    for a in range(n_group - 1):
        mix = attended(a, query)
        if w_whole is None:
            mix, halves = lax.optimization_barrier((mix, halves))
            w_whole = whole_weight(w_out, halves, dp, n_dp)
        blocks = [mix] + [shift(mix, "tensor", n_tp, k) for k in far_first]
        query, w_whole, blocks = lax.optimization_barrier((query, w_whole, blocks))
        early.append(blocks)
    if w_whole is None:
        w_whole = whole_weight(w_out, halves, dp, n_dp)
    last = attended(n_group - 1, query)
    early, last, w_whole = lax.optimization_barrier((early, last, w_whole))
    early = [[by_chunk(block) for block in blocks] for blocks in early]
    last = by_chunk(last)
    outs = []
    pieces = None
    bases = []
    late = []
    for c in range(n_chunk):
        own = last[c]
        if bases:
            own = lax.optimization_barrier((own, bases[-1]))[0]
        late.append([own] + [shift(own, "tensor", n_tp, k) for k in far_first])
        base = all_tokens[c].reshape(n_tp * sub, d_model).astype(F32)
        for a in range(n_group - 1):
            base = base + mixed([block[c] for block in early[a]], a)
        bases.append(base)
    for c in range(n_chunk):
        blocks = late[c]
        if pieces is not None:
            blocks = lax.optimization_barrier((blocks, pieces))[0]
        residual = bases[c] + mixed(blocks, n_group - 1)
        ffn_in = normalize(residual, ffn_gain).astype(BF)
        gate_up = jnp.einsum("td,kdf->ktf", ffn_in, w_gateup, preferred_element_type=F32)
        hidden = (jax.nn.silu(gate_up[0]) * gate_up[1]).astype(BF)
        down = jnp.dot(hidden, w_down, preferred_element_type=F32).reshape(n_tp, sub, d_model)
        total = lax.dynamic_index_in_dim(down, tp, 0, False)
        total = total + lax.dynamic_index_in_dim(
            residual.reshape(n_tp, sub, d_model), tp, 0, False
        )
        down = down.astype(BF)
        pieces = [lax.dynamic_index_in_dim(down, (tp + k) % n_tp, 0, False) for k in far_first]
        for k, piece in zip(far_first, pieces):
            total = total + shift(piece, "tensor", n_tp, k).astype(F32)
        outs.append(total.astype(BF))
    return jnp.concatenate(outs, axis=0)


def solution(mesh):
    return jax.shard_map(
        per_device,
        mesh=mesh,
        in_specs=(
            P(("dp", "tensor"), None),
            P(),
            P(),
            P(None, None, "tensor"),
            P("tensor", None),
            P(None, None, "tensor"),
            P("tensor", None),
            P(None, "tensor"),
            P("dp", None, None, None),
            P("dp", None, None, "tensor"),
            P(),
            P("dp", None),
            P("dp", None),
            P("dp", None),
            P("dp", None),
            P("dp", None, None, "tensor"),
        ),
        out_specs=P(("dp", "tensor"), None),
        check_vma=False,
    )
```

```python
import functools

import jax
import jax.numpy as jnp
from jax import lax
from jax.experimental import pallas as pl
from jax.experimental.pallas import tpu as pltpu
from jax.sharding import PartitionSpec as P

HD = 64
PAGES_REQ = 8
VARLEN = 160
TILE = 128
KCH = 128
BLK = 4
CHUNK = 64
BF = jnp.bfloat16
F32 = jnp.float32
NEG = -1e30
LIGHT = pl.CostEstimate(flops=1000, bytes_accessed=1000, transcendentals=0)


def normalize(values, gain):
    values = values.astype(F32)
    inv_scale = lax.rsqrt(jnp.mean(values * values, axis=-1, keepdims=True) + 1e-05)
    return values * inv_scale * gain.astype(F32)


def token_layout(req_lens, live_counts, page_len, tok_total):
    end_pos = jnp.cumsum(req_lens, dtype=jnp.int32)
    starts = end_pos - req_lens
    tok_index = jnp.arange(tok_total, dtype=jnp.int32)
    request = jnp.sum(
        (tok_index[:, None] >= end_pos[None, :]).astype(jnp.int32), axis=1, dtype=jnp.int32
    )
    onehot = request[:, None] == jnp.arange(req_lens.shape[0], dtype=jnp.int32)[None, :]
    first_pos = jnp.sum(jnp.where(onehot, starts[None, :], 0), axis=1, dtype=jnp.int32)
    cached = jnp.sum(jnp.where(onehot, live_counts[None, :], 0), axis=1, dtype=jnp.int32)
    return (onehot, cached * page_len + tok_index - first_pos)


def pick_kernel(n_dp, cap, me_ref, asked_ref, pool_ref, *rest):
    n_out = len(rest) - 3
    outs, (buf, sem_in, sem_out) = rest[:n_out], rest[n_out:]
    lanes = outs[0].shape[-1]
    me = me_ref[0]
    slots = asked_ref.shape[2]

    def find(g, carry):
        count = jnp.int32(0)
        for p in range(slots):
            hit = asked_ref[g, 0, p] == me

            @pl.when(hit)
            def _():
                pltpu.make_async_copy(
                    pool_ref.at[asked_ref[g, 1, p]], buf.at[g, count], sem_in.at[g]
                ).start()

            count = count + hit.astype(jnp.int32)
        return carry

    lax.fori_loop(0, n_dp, find, 0)
    done = []
    for g in range(n_dp):
        pltpu.make_async_copy(pool_ref.at[pl.ds(0, cap)], buf.at[g], sem_in.at[g]).wait()
        for a in range(n_out):
            copy = pltpu.make_async_copy(
                buf.at[g, :, :, :, pl.ds(a * lanes, lanes)], outs[a].at[g], sem_out.at[a, g]
            )
            copy.start()
            done.append(copy)
    for copy in done:
        copy.wait()


def pick(me, asked, pool, n_dp, cap, lanes):
    smem = pl.BlockSpec(memory_space=pltpu.SMEM)
    hbm = pl.BlockSpec(memory_space=pl.ANY)
    n_out = pool.shape[-1] // lanes
    shape = (n_dp, cap) + pool.shape[1:-1]
    return pl.pallas_call(
        functools.partial(pick_kernel, n_dp, cap),
        out_shape=[jax.ShapeDtypeStruct(shape + (lanes,), pool.dtype)] * n_out,
        in_specs=[smem, smem, hbm],
        out_specs=[hbm] * n_out,
        scratch_shapes=[
            pltpu.VMEM(shape + pool.shape[-1:], pool.dtype),
            pltpu.SemaphoreType.DMA((n_dp,)),
            pltpu.SemaphoreType.DMA((n_out, n_dp)),
        ],
        cost_estimate=LIGHT,
        name="pick_pages",
    )(me, asked, pool)


def named_kernel(n_loc, span, table_ref, ids_ref, all_ref, down_out, up_out, down_ref, up_ref, sem):
    copies = []
    for r in range(ids_ref.shape[1]):
        slot = table_ref[ids_ref[0, r]]
        home, inner = slot // n_loc, slot % n_loc
        for half, out in ((0, down_ref), (1, up_ref)):
            base = pl.multiple_of((half * n_loc + inner) * span, span)
            copy = pltpu.make_async_copy(
                all_ref.at[home, pl.ds(base, span)], out.at[pl.ds(r * span, span)], sem.at[r, half]
            )
            copy.start()
            copies.append(copy)
    for copy in copies:
        copy.wait()
    last = [
        pltpu.make_async_copy(down_ref, down_out, sem.at[0, 0]),
        pltpu.make_async_copy(up_ref, up_out, sem.at[0, 1]),
    ]
    for copy in last:
        copy.start()
    for copy in last:
        copy.wait()


def named(owner_table, adapter_ids, gathered, n_loc, span):
    n_req = adapter_ids.shape[1]
    smem = pl.BlockSpec(memory_space=pltpu.SMEM)
    hbm = pl.BlockSpec(memory_space=pltpu.HBM)
    out = jax.ShapeDtypeStruct((n_req * span, gathered.shape[-1]), BF)
    return pl.pallas_call(
        functools.partial(named_kernel, n_loc, span),
        out_shape=(out, out),
        in_specs=[smem, smem, hbm],
        out_specs=(hbm, hbm),
        scratch_shapes=[
            pltpu.VMEM(out.shape, BF),
            pltpu.VMEM(out.shape, BF),
            pltpu.SemaphoreType.DMA((n_req, 2)),
        ],
        cost_estimate=LIGHT,
        name="named_adapters",
    )(owner_table, adapter_ids, gathered)


def project_kernel(n_tp, cap, pool_dev, tp_ref, lens_ref, table_ref, *rest):
    hbm_refs, rest = rest[: 5 + 2 * n_tp], rest[5 + 2 * n_tp :]
    q_ref, k_ref, v_ref, pos_ref, all_ref, down, count, *held = rest
    held, sem, sem_out = held[:-2], held[-2], held[-1]
    gain_ref, w_ref, up_ref, cos_ref, sin_ref, tok_ref = held
    tp = tp_ref[0]
    copies = []
    targets = list(held[:5]) + [tok_ref.at[k] for k in range(n_tp)]
    for k in range(n_tp):
        targets.append(down.at[lax.rem(tp - k + n_tp, n_tp)])
    for i in list(range(5, 5 + 2 * n_tp)) + list(range(5)):
        copy = pltpu.make_async_copy(hbm_refs[i], targets[i], sem.at[i])
        copy.start()
        copies.append(copy)
    _, rows, _ = tok_ref.shape
    width = q_ref.shape[1]
    n_low, dd = down.shape[1:]
    n_req = lens_ref.shape[1]
    rank = n_low // n_req // 2

    for g in range(count.shape[0]):
        count[g] = 0

    def place(p, carry):
        home = table_ref[0, p] // pool_dev
        seen = count[home]
        count[home] = seen + 1
        pos_ref[p] = home * cap + seen
        return carry

    lax.fori_loop(0, table_ref.shape[1], place, 0)

    for copy in copies:
        copy.wait()
    n_chunk, _, sub, _ = all_ref.shape
    stores = []
    for k in range(n_tp):
        for c in range(n_chunk):
            copy = pltpu.make_async_copy(
                tok_ref.at[k, pl.ds(c * sub, sub)],
                all_ref.at[c, lax.rem(tp - k + n_tp, n_tp)],
                sem_out.at[k, c],
            )
            copy.start()
            stores.append(copy)
    lane = lax.broadcasted_iota(jnp.int32, (1, 128), 1)
    first = jnp.bitwise_and(lane, HD - 1) < HD // 2

    def rope(u, cos, sin):
        parts = []
        for a in range(width // 128):
            part = u[:, a * 128 : (a + 1) * 128]
            other = jnp.where(
                first, pltpu.roll(part, 128 - HD // 2, 1), pltpu.roll(part, HD // 2, 1)
            )
            parts.append(part * cos + other * sin)
        return parts

    for k in range(n_tp):
        row0 = pl.multiple_of(lax.rem(tp - k + n_tp, n_tp) * rows, rows)
        x = tok_ref[k].astype(F32)
        inv = lax.rsqrt(jnp.mean(x * x, axis=1, keepdims=True) + 1e-05)
        normed = (x * inv * gain_ref[...].astype(F32)).astype(BF)
        low = jnp.zeros((rows, n_low), F32)
        for j in range(n_tp):
            low = low + lax.dot_general(
                normed[:, j * dd : (j + 1) * dd], down[j], (((1,), (1,)), ((), ())),
                preferred_element_type=F32,
            )
        row = row0 + lax.broadcasted_iota(jnp.int32, (rows, n_low), 0)
        col = lax.broadcasted_iota(jnp.int32, (rows, n_low), 1)
        request = jnp.zeros((rows, n_low), jnp.int32)
        end = jnp.int32(0)
        for r in range(n_req - 1):
            end = end + lens_ref[0, r]
            request = request + (row >= end).astype(jnp.int32)
        own = col // (2 * rank) == request
        kind = (col // rank) % 2
        deltas = []
        for kk in range(2):
            part = jnp.where(own & (kind == kk), low, 0.0).astype(BF)
            deltas.append(jnp.dot(part, up_ref[...], preferred_element_type=F32))
        cos = cos_ref[pl.ds(row0, rows), :]
        sin = sin_ref[pl.ds(row0, rows), :]
        q = jnp.dot(normed, w_ref[0], preferred_element_type=F32) + deltas[0]
        for a, part in enumerate(rope(q, cos, sin)):
            part = part.astype(BF).astype(F32) * (HD ** -0.5)
            q_ref[pl.ds(row0, rows), a * 128 : (a + 1) * 128] = part.astype(BF)
        kk = jnp.dot(normed, w_ref[1], preferred_element_type=F32)
        for a, part in enumerate(rope(kk, cos, sin)):
            k_ref[pl.ds(row0, rows), a * 128 : (a + 1) * 128] = part.astype(BF)
        v = jnp.dot(normed, w_ref[2], preferred_element_type=F32) + deltas[1]
        v_ref[pl.ds(row0, rows), :] = v.astype(BF)
    for copy in stores:
        copy.wait()


def project(
    tp, lens, table, gain, w_qkv, up, cos, sin, toks, downs, n_dp, cap, pool_dev, n_chunk
):
    n_tp = len(toks)
    sub = toks[0].shape[0] // n_chunk
    rows = toks[0].shape[0] * n_tp
    width = w_qkv.shape[2]
    smem = pl.BlockSpec(memory_space=pltpu.SMEM)
    vmem = pl.BlockSpec(memory_space=pltpu.VMEM)
    out = jax.ShapeDtypeStruct((rows, width), BF)
    return pl.pallas_call(
        functools.partial(project_kernel, n_tp, cap, pool_dev),
        out_shape=(
            out, out, out, jax.ShapeDtypeStruct((table.shape[1],), jnp.int32),
            jax.ShapeDtypeStruct((n_chunk, n_tp, sub, toks[0].shape[1]), BF),
        ),
        in_specs=[smem] * 3 + [pl.BlockSpec(memory_space=pltpu.HBM)] * (5 + 2 * n_tp),
        out_specs=(vmem, vmem, vmem, smem, pl.BlockSpec(memory_space=pltpu.HBM)),
        scratch_shapes=[
            pltpu.VMEM((n_tp,) + downs[0].shape, BF),
            pltpu.SMEM((n_dp,), jnp.int32),
        ]
        + [pltpu.VMEM(x.shape, x.dtype) for x in (gain, w_qkv, up, cos, sin)]
        + [
            pltpu.VMEM((n_tp,) + toks[0].shape, BF),
            pltpu.SemaphoreType.DMA((5 + 2 * n_tp,)),
            pltpu.SemaphoreType.DMA((n_tp, n_chunk)),
        ],
        compiler_params=pltpu.CompilerParams(vmem_limit_bytes=60 << 20),
        cost_estimate=LIGHT,
        name="project",
    )(tp, lens, table, gain, w_qkv, up, cos, sin, *toks, *downs)


def attend_kernel(
    group, per, lens_ref, counts_ref, pos_ref, bias_ref,
    q_ref, kn_ref, vn_ref, raw_ref, out_ref,
    kc, vc, knp, vnp, qbd, info, sbuf, wbuf, obuf,
):
    page_len = kc.shape[1]
    width = q_ref.shape[1]
    rows = q_ref.shape[0]
    n_req = lens_ref.shape[1]
    back = knp.shape[0] - rows
    n_page = PAGES_REQ
    n_new = (back + TILE) // KCH

    row = lax.broadcasted_iota(jnp.int32, (2 * page_len, 2 * page_len), 0)
    col = lax.broadcasted_iota(jnp.int32, (2 * page_len, 2 * page_len), 1)
    src = jnp.where(row < page_len, 2 * row, 2 * row - (2 * page_len - 1))
    choose = (col == src).astype(F32).astype(BF)

    def unpack(slot):
        pages = [raw_ref[pos_ref[slot + i]] for i in range(BLK)]
        both = jnp.dot(
            choose, jnp.concatenate(pages, axis=1), preferred_element_type=F32
        ).astype(BF)
        for i in range(BLK):
            kc[slot + i] = both[:page_len, i * width : (i + 1) * width]
            vc[slot + i] = both[page_len:, i * width : (i + 1) * width]

    for r in range(n_req):
        unpack(r * n_page)
    for r in range(n_req):
        for b in range(1, n_page // BLK):
            @pl.when(counts_ref[0, r] > b * BLK)
            def _():
                unpack(r * n_page + b * BLK)

    knp[:back, :] = jnp.zeros((back, width), BF)
    vnp[:back, :] = jnp.zeros((back, width), BF)
    knp[back:, :] = kn_ref[...]
    vnp[back:, :] = vn_ref[...]

    lane = lax.broadcasted_iota(jnp.int32, (1, width), 1)
    lane_f = lax.broadcasted_iota(jnp.int32, (1, KCH), 1).astype(F32)
    delta = [bias_ref[0, group * per + a] - bias_ref[1, group * per + a] for a in range(per)]
    starts = [jnp.int32(0)]
    for r in range(n_req):
        starts.append(starts[-1] + lens_ref[0, r])

    def tile_body(t, carry):
        row0 = pl.multiple_of(t * TILE, TILE)
        qt = q_ref[pl.ds(row0, TILE), :].astype(F32)
        for a in range(per):
            mine = (lane >= a * HD) & (lane < (a + 1) * HD)
            qbd[a * TILE : (a + 1) * TILE, :] = jnp.where(mine, qt, 0.0).astype(BF)

        row = (row0 + lax.broadcasted_iota(jnp.int32, (TILE, KCH), 0)).astype(F32)
        start_row = jnp.zeros((TILE, KCH), F32)
        offset = jnp.zeros((TILE, KCH), F32)
        blocks = jnp.int32(1)
        for r in range(n_req):
            start, end, live = starts[r], starts[r + 1], counts_ref[0, r]
            inside = (row >= start.astype(F32)) & (row < end.astype(F32))
            start_row = jnp.where(inside, start.astype(F32), start_row)
            offset = jnp.where(inside, (live * page_len - start).astype(F32), offset)
            here = (start < row0 + TILE) & (end > row0)
            blocks = jnp.maximum(blocks, jnp.where(here, (live + BLK - 1) // BLK, 0))
        var_first = jnp.floor((row + offset + 0.5) * (1.0 / VARLEN)) * VARLEN
        info[0] = row
        info[1] = start_row
        info[2] = var_first
        info[3] = var_first - offset

        for b in range(n_page // BLK):
            @pl.when(b < blocks)
            def _():
                for i in range(BLK):
                    sbuf[b * BLK + i] = jnp.full((per * TILE, KCH), NEG, F32)

        def scores(keys):
            return lax.dot_general(
                qbd[...], keys, (((1,), (1,)), ((), ())), preferred_element_type=F32
            )

        for r in range(n_req):
            start, end, live = starts[r], starts[r + 1], counts_ref[0, r]
            here = (start < row0 + TILE) & (end > row0)
            for b in range(n_page // BLK):
                @pl.when(here & (live > b * BLK))
                def _():
                    s_all = scores(
                        kc[r * n_page + b * BLK : r * n_page + (b + 1) * BLK].reshape(
                            BLK * page_len, width
                        )
                    )
                    row = info[0]
                    inside = (row >= start.astype(F32)) & (row < end.astype(F32))
                    for i in range(BLK):
                        page = b * BLK + i
                        dead = jnp.where(page < live, 0.0, NEG)
                        same = info[2] <= lane_f + page * page_len
                        for a in range(per):
                            part = slice(a * TILE, (a + 1) * TILE)
                            s = s_all[part, i * KCH : (i + 1) * KCH]
                            s = s + jnp.where(same, delta[a] + dead, dead)
                            sbuf[page, part, :] = jnp.where(inside, s, sbuf[page, part, :])

        s_all = scores(knp[pl.ds(row0, back + TILE), :])
        for i in range(n_new):
            key_row = lane_f + (row0 - back + i * KCH).astype(F32)
            allowed = (key_row >= info[1]) & (key_row <= info[0])
            same = info[3] <= key_row
            for a in range(per):
                part = slice(a * TILE, (a + 1) * TILE)
                s = s_all[part, i * KCH : (i + 1) * KCH]
                s = jnp.where(allowed, s + jnp.where(same, delta[a], 0.0), NEG)
                sbuf[n_page + i, part, :] = s

        for a in range(per):
            part = slice(a * TILE, (a + 1) * TILE)

            def top_block(b, top):
                for i in range(BLK):
                    top = jnp.maximum(top, sbuf[b * BLK + i, part, :])
                return top

            top = sbuf[n_page, part, :]
            for i in range(1, n_new):
                top = jnp.maximum(top, sbuf[n_page + i, part, :])
            top = lax.fori_loop(0, blocks, top_block, top)
            peak = jnp.broadcast_to(jnp.max(top, axis=1, keepdims=True), (TILE, KCH))

            def weigh(c, total):
                p = jnp.exp(sbuf[c, part, :] - peak)
                sbuf[c, part, :] = p
                return total + p

            def weigh_block(b, total):
                for i in range(BLK):
                    total = weigh(b * BLK + i, total)
                return total

            total = jnp.zeros((TILE, KCH), F32)
            for i in range(n_new):
                total = weigh(n_page + i, total)
            total = lax.fori_loop(0, blocks, weigh_block, total)
            inverse = jnp.broadcast_to(
                1.0 / jnp.sum(total, axis=1, keepdims=True), (TILE, KCH)
            )
            for i in range(n_new):
                c = n_page + i
                wbuf[part, c * KCH : (c + 1) * KCH] = (sbuf[c, part, :] * inverse).astype(BF)
            for b in range(n_page // BLK):
                @pl.when(b < blocks)
                def _():
                    for i in range(BLK):
                        c = b * BLK + i
                        wbuf[part, c * KCH : (c + 1) * KCH] = (
                            sbuf[c, part, :] * inverse
                        ).astype(BF)

        obuf[...] = jnp.dot(
            wbuf[:, n_page * KCH :], vnp[pl.ds(row0, back + TILE), :],
            preferred_element_type=F32,
        )
        for r in range(n_req):
            start, end, live = starts[r], starts[r + 1], counts_ref[0, r]
            here = (start < row0 + TILE) & (end > row0)
            for b in range(n_page // BLK):
                @pl.when(here & (live > b * BLK))
                def _():
                    o = jnp.dot(
                        wbuf[:, b * BLK * KCH : (b + 1) * BLK * KCH],
                        vc[r * n_page + b * BLK : r * n_page + (b + 1) * BLK].reshape(
                            BLK * page_len, width
                        ),
                        preferred_element_type=F32,
                    )
                    row = info[0]
                    inside = (row >= start.astype(F32)) & (row < end.astype(F32))
                    for a in range(per):
                        part = slice(a * TILE, (a + 1) * TILE)
                        before = obuf[part, :]
                        obuf[part, :] = jnp.where(inside[:, :width], before + o[part], before)
        o = obuf[:TILE, :]
        for a in range(1, per):
            o = jnp.where(lane >= a * HD, obuf[a * TILE : (a + 1) * TILE, :], o)
        out_ref[pl.ds(row0, TILE), :] = o.astype(BF)
        return carry

    lax.fori_loop(0, rows // TILE, tile_body, 0)


def attend(group, lanes, most, lens, counts, pos, bias, q, kn, vn, raw):
    rows = q.shape[0]
    per = lanes // HD
    page_len = raw.shape[1] // 2
    slots = raw.shape[0]
    back = -(-most // KCH) * KCH
    n_all = PAGES_REQ + (back + TILE) // KCH
    smem = pl.BlockSpec(memory_space=pltpu.SMEM)
    part = pl.BlockSpec((rows, lanes), lambda i: (0, group))
    return pl.pallas_call(
        functools.partial(attend_kernel, group, per),
        grid=(1,),
        out_shape=jax.ShapeDtypeStruct((rows, lanes), BF),
        in_specs=[smem] * 4
        + [part] * 3
        + [pl.BlockSpec(raw.shape, lambda i: (0, 0, 0), pipeline_mode=pl.Buffered(1))],
        out_specs=pl.BlockSpec((rows, lanes), lambda i: (0, 0)),
        scratch_shapes=[
            pltpu.VMEM((slots, page_len, lanes), BF),
            pltpu.VMEM((slots, page_len, lanes), BF),
            pltpu.VMEM((back + rows, lanes), BF),
            pltpu.VMEM((back + rows, lanes), BF),
            pltpu.VMEM((per * TILE, lanes), BF),
            pltpu.VMEM((4, TILE, KCH), F32),
            pltpu.VMEM((n_all, per * TILE, KCH), F32),
            pltpu.VMEM((per * TILE, n_all * KCH), BF),
            pltpu.VMEM((per * TILE, lanes), F32),
        ],
        compiler_params=pltpu.CompilerParams(vmem_limit_bytes=60 << 20),
        cost_estimate=LIGHT,
        name="attend",
    )(lens, counts, pos, bias, q, kn, vn, raw)


def shift(value, axis, n, k):
    return lax.ppermute(value, axis, [(i, (i + k) % n) for i in range(n)])


def whole_weight(own, halves, dp, n_dp):
    halves = jnp.stack(halves)
    twins = lax.ppermute(halves, "dp", [(i, i ^ 1) for i in range(n_dp)])
    rest = jnp.where(
        dp % 2 == 0,
        jnp.concatenate([halves, twins], axis=1),
        jnp.concatenate([twins, halves], axis=1),
    )
    return jnp.concatenate([own[None], rest], axis=0)


def per_device(
    tokens,
    attn_gain,
    ffn_gain,
    w_qkv,
    w_out,
    w_gateup,
    w_down,
    variate_bias,
    adapter_down,
    adapter_up,
    owner_table,
    lengths,
    adapter_ids,
    page_counts,
    page_table,
    cache_pool,
):
    n_tp = lax.axis_size("tensor")
    n_dp = lax.axis_size("dp")
    tp = lax.axis_index("tensor")
    dp = lax.axis_index("dp")
    me = dp.astype(jnp.int32).reshape(1)
    tp_id = tp.astype(jnp.int32).reshape(1)
    row_count, d_model = tokens.shape
    tok_total = row_count * n_tp
    width = w_out.shape[0]
    page_len = cache_pool.shape[1]
    pool_dev = cache_pool.shape[0]
    cap = max(1, page_table.shape[1] // n_dp)
    far_first = [k for k in range(1, n_tp)]
    lanes = min(width, 2 * HD)
    n_group = width // lanes
    slots = n_dp * cap
    dd = d_model // n_tp
    n_loc, _, rank, _ = adapter_down.shape
    n_chunk = max(1, row_count // CHUNK)
    sub = row_count // n_chunk
    span = 2 * rank

    toks = [tokens] + [shift(tokens, "tensor", n_tp, k) for k in far_first]

    down_part = lax.dynamic_slice_in_dim(adapter_down, tp * dd, dd, 3).reshape(n_loc * span, dd)
    names = jnp.concatenate([page_table // pool_dev, page_table % pool_dev], axis=0).astype(BF)
    names = jnp.pad(names, ((0, 14), (0, dd - names.shape[1])))
    payload = jnp.concatenate([down_part, adapter_up.reshape(n_loc * span, width), names], axis=0)
    gathered = lax.all_gather(payload, "dp", axis=0)
    asked = gathered[:, 2 * n_loc * span : 2 * n_loc * span + 2, : page_table.shape[1]]
    picked = pick(me, asked.astype(jnp.int32), cache_pool, n_dp, cap, lanes)
    send = lax.optimization_barrier((picked[0], toks[1:-1]))[0]
    fetched = [lax.all_to_all(send, "dp", split_axis=0, concat_axis=0, tiled=True)]

    own_half = lax.dynamic_slice_in_dim(w_out, (dp % 2) * (width // 2), width // 2, 0)
    gathered, lengths_b = lax.optimization_barrier((gathered, lengths, send))[:2]
    down_named, up_named = named(owner_table, adapter_ids, gathered, n_loc, span)
    downs = [down_named] + [shift(down_named, "tensor", n_tp, k) for k in far_first]

    _, position = token_layout(lengths_b[0], page_counts[0], page_len, tok_total)
    index = jnp.arange(2 * HD, dtype=jnp.int32)
    frequency = 10000.0 ** (-2.0 * (index % (HD // 2)).astype(F32) / HD)
    angles = (position % VARLEN).astype(F32)[:, None] * frequency[None, :]
    sign = jnp.where(index % HD < HD // 2, -1.0, 1.0).astype(F32)
    query, new_keys, new_values, buffer_pos, all_tokens = project(
        tp_id, lengths, page_table, attn_gain.reshape(1, d_model), w_qkv, up_named,
        jnp.cos(angles), jnp.sin(angles) * sign[None, :], toks, downs, n_dp, cap, pool_dev, n_chunk,
    )
    own_half = lax.optimization_barrier((own_half, downs[1:]))[0]
    halves = [shift(own_half, "tensor", n_tp, k) for k in far_first]
    for a in range(1, n_group):
        send = lax.optimization_barrier((picked[a], fetched[-1], query, halves[:-1]))[0]
        fetched.append(lax.all_to_all(send, "dp", split_axis=0, concat_axis=0, tiled=True))
    fetched = [f.reshape(slots, 2 * page_len, lanes) for f in fetched]


    def mixed(blocks, a):
        w_parts = w_whole.reshape(n_tp, n_group, lanes, d_model)
        return jnp.dot(
            jnp.concatenate(blocks, axis=1),
            w_parts[:, a].reshape(n_tp * lanes, d_model),
            preferred_element_type=F32,
        )

    def attended(a, q):
        return attend(
            a, lanes, 2 * TILE, lengths, page_counts, buffer_pos, variate_bias,
            q, new_keys, new_values, fetched[a],
        )

    def by_chunk(mix):
        mix = mix.reshape(n_tp, n_chunk, sub, lanes)
        return [mix[:, c].reshape(n_tp * sub, lanes) for c in range(n_chunk)]

    early = []
    w_whole = None
    for a in range(n_group - 1):
        mix = attended(a, query)
        if w_whole is None:
            mix, halves = lax.optimization_barrier((mix, halves))
            w_whole = whole_weight(w_out, halves, dp, n_dp)
        blocks = [mix] + [shift(mix, "tensor", n_tp, k) for k in far_first]
        query, w_whole, blocks = lax.optimization_barrier((query, w_whole, blocks))
        early.append(blocks)
    if w_whole is None:
        w_whole = whole_weight(w_out, halves, dp, n_dp)
    last = attended(n_group - 1, query)
    early, last, w_whole = lax.optimization_barrier((early, last, w_whole))
    early = [[by_chunk(block) for block in blocks] for blocks in early]
    last = by_chunk(last)
    outs = []
    pieces = None
    bases = []
    late = []
    for c in range(n_chunk):
        own = last[c]
        if bases:
            own = lax.optimization_barrier((own, bases[-1]))[0]
        late.append([own] + [shift(own, "tensor", n_tp, k) for k in far_first])
        base = all_tokens[c].reshape(n_tp * sub, d_model).astype(F32)
        for a in range(n_group - 1):
            base = base + mixed([block[c] for block in early[a]], a)
        bases.append(base)
    for c in range(n_chunk):
        blocks = late[c]
        if pieces is not None:
            blocks = lax.optimization_barrier((blocks, pieces))[0]
        residual = bases[c] + mixed(blocks, n_group - 1)
        ffn_in = normalize(residual, ffn_gain).astype(BF)
        gate_up = jnp.einsum("td,kdf->ktf", ffn_in, w_gateup, preferred_element_type=F32)
        hidden = (jax.nn.silu(gate_up[0]) * gate_up[1]).astype(BF)
        down = jnp.dot(hidden, w_down, preferred_element_type=F32).reshape(n_tp, sub, d_model)
        total = lax.dynamic_index_in_dim(down, tp, 0, False)
        total = total + lax.dynamic_index_in_dim(
            residual.reshape(n_tp, sub, d_model), tp, 0, False
        )
        down = down.astype(BF)
        pieces = [lax.dynamic_index_in_dim(down, (tp + k) % n_tp, 0, False) for k in far_first]
        for k, piece in zip(far_first, pieces):
            total = total + shift(piece, "tensor", n_tp, k).astype(F32)
        outs.append(total.astype(BF))
    return jnp.concatenate(outs, axis=0)


def solution(mesh):
    return jax.shard_map(
        per_device,
        mesh=mesh,
        in_specs=(
            P(("dp", "tensor"), None),
            P(),
            P(),
            P(None, None, "tensor"),
            P("tensor", None),
            P(None, None, "tensor"),
            P("tensor", None),
            P(None, "tensor"),
            P("dp", None, None, None),
            P("dp", None, None, "tensor"),
            P(),
            P("dp", None),
            P("dp", None),
            P("dp", None),
            P("dp", None),
            P("dp", None, None, "tensor"),
        ),
        out_specs=P(("dp", "tensor"), None),
        check_vma=False,
    )
```

```python
import functools

import jax
import jax.numpy as jnp
from jax import lax
from jax.experimental import pallas as pl
from jax.experimental.pallas import tpu as pltpu
from jax.sharding import PartitionSpec as P

HD = 64
PAGES_REQ = 8
VARLEN = 160
TILE = 128
KCH = 128
BLK = 4
CHUNK = 64
BF = jnp.bfloat16
F32 = jnp.float32
NEG = -1e30
LIGHT = pl.CostEstimate(flops=1000, bytes_accessed=1000, transcendentals=0)


def normalize(values, gain):
    values = values.astype(F32)
    inv_scale = lax.rsqrt(jnp.mean(values * values, axis=-1, keepdims=True) + 1e-05)
    return values * inv_scale * gain.astype(F32)


def token_layout(req_lens, live_counts, page_len, tok_total):
    end_pos = jnp.cumsum(req_lens, dtype=jnp.int32)
    starts = end_pos - req_lens
    tok_index = jnp.arange(tok_total, dtype=jnp.int32)
    request = jnp.sum(
        (tok_index[:, None] >= end_pos[None, :]).astype(jnp.int32), axis=1, dtype=jnp.int32
    )
    onehot = request[:, None] == jnp.arange(req_lens.shape[0], dtype=jnp.int32)[None, :]
    first_pos = jnp.sum(jnp.where(onehot, starts[None, :], 0), axis=1, dtype=jnp.int32)
    cached = jnp.sum(jnp.where(onehot, live_counts[None, :], 0), axis=1, dtype=jnp.int32)
    return (onehot, cached * page_len + tok_index - first_pos)


def pick_kernel(n_dp, cap, me_ref, asked_ref, pool_ref, *rest):
    n_out = len(rest) - 3
    outs, (buf, sem_in, sem_out) = rest[:n_out], rest[n_out:]
    lanes = outs[0].shape[-1]
    me = me_ref[0]
    slots = asked_ref.shape[2]

    def find(g, carry):
        count = jnp.int32(0)
        for p in range(slots):
            hit = asked_ref[g, 0, p] == me

            @pl.when(hit)
            def _():
                pltpu.make_async_copy(
                    pool_ref.at[asked_ref[g, 1, p]], buf.at[g, count], sem_in.at[g]
                ).start()

            count = count + hit.astype(jnp.int32)
        return carry

    lax.fori_loop(0, n_dp, find, 0)
    done = []
    for g in range(n_dp):
        pltpu.make_async_copy(pool_ref.at[pl.ds(0, cap)], buf.at[g], sem_in.at[g]).wait()
        for a in range(n_out):
            copy = pltpu.make_async_copy(
                buf.at[g, :, :, :, pl.ds(a * lanes, lanes)], outs[a].at[g], sem_out.at[a, g]
            )
            copy.start()
            done.append(copy)
    for copy in done:
        copy.wait()


def pick(me, asked, pool, n_dp, cap, lanes):
    smem = pl.BlockSpec(memory_space=pltpu.SMEM)
    hbm = pl.BlockSpec(memory_space=pl.ANY)
    n_out = pool.shape[-1] // lanes
    shape = (n_dp, cap) + pool.shape[1:-1]
    return pl.pallas_call(
        functools.partial(pick_kernel, n_dp, cap),
        out_shape=[jax.ShapeDtypeStruct(shape + (lanes,), pool.dtype)] * n_out,
        in_specs=[smem, smem, hbm],
        out_specs=[hbm] * n_out,
        scratch_shapes=[
            pltpu.VMEM(shape + pool.shape[-1:], pool.dtype),
            pltpu.SemaphoreType.DMA((n_dp,)),
            pltpu.SemaphoreType.DMA((n_out, n_dp)),
        ],
        cost_estimate=LIGHT,
        name="pick_pages",
    )(me, asked, pool)


def named_kernel(n_loc, span, table_ref, ids_ref, all_ref, down_out, up_out, down_ref, up_ref, sem):
    copies = []
    for r in range(ids_ref.shape[1]):
        slot = table_ref[ids_ref[0, r]]
        home, inner = slot // n_loc, slot % n_loc
        for half, out in ((0, down_ref), (1, up_ref)):
            base = pl.multiple_of((half * n_loc + inner) * span, span)
            copy = pltpu.make_async_copy(
                all_ref.at[home, pl.ds(base, span)], out.at[pl.ds(r * span, span)], sem.at[r, half]
            )
            copy.start()
            copies.append(copy)
    for copy in copies:
        copy.wait()
    last = [
        pltpu.make_async_copy(down_ref, down_out, sem.at[0, 0]),
        pltpu.make_async_copy(up_ref, up_out, sem.at[0, 1]),
    ]
    for copy in last:
        copy.start()
    for copy in last:
        copy.wait()


def named(owner_table, adapter_ids, gathered, n_loc, span):
    n_req = adapter_ids.shape[1]
    smem = pl.BlockSpec(memory_space=pltpu.SMEM)
    hbm = pl.BlockSpec(memory_space=pltpu.HBM)
    out = jax.ShapeDtypeStruct((n_req * span, gathered.shape[-1]), BF)
    return pl.pallas_call(
        functools.partial(named_kernel, n_loc, span),
        out_shape=(out, out),
        in_specs=[smem, smem, hbm],
        out_specs=(hbm, hbm),
        scratch_shapes=[
            pltpu.VMEM(out.shape, BF),
            pltpu.VMEM(out.shape, BF),
            pltpu.SemaphoreType.DMA((n_req, 2)),
        ],
        cost_estimate=LIGHT,
        name="named_adapters",
    )(owner_table, adapter_ids, gathered)


def project_kernel(n_tp, cap, pool_dev, tp_ref, lens_ref, table_ref, *rest):
    hbm_refs, rest = rest[: 5 + 2 * n_tp], rest[5 + 2 * n_tp :]
    q_ref, k_ref, v_ref, pos_ref, all_ref, down, count, *held = rest
    held, sem, sem_out = held[:-2], held[-2], held[-1]
    gain_ref, w_ref, up_ref, cos_ref, sin_ref, tok_ref = held
    tp = tp_ref[0]
    copies = []
    targets = list(held[:5]) + [tok_ref.at[k] for k in range(n_tp)]
    for k in range(n_tp):
        targets.append(down.at[lax.rem(tp - k + n_tp, n_tp)])
    for i in list(range(5, 5 + 2 * n_tp)) + list(range(5)):
        copy = pltpu.make_async_copy(hbm_refs[i], targets[i], sem.at[i])
        copy.start()
        copies.append(copy)
    _, rows, _ = tok_ref.shape
    width = q_ref.shape[1]
    n_low, dd = down.shape[1:]
    n_req = lens_ref.shape[1]
    rank = n_low // n_req // 2

    for g in range(count.shape[0]):
        count[g] = 0

    def place(p, carry):
        home = table_ref[0, p] // pool_dev
        seen = count[home]
        count[home] = seen + 1
        pos_ref[p] = home * cap + seen
        return carry

    lax.fori_loop(0, table_ref.shape[1], place, 0)

    for copy in copies:
        copy.wait()
    n_chunk, _, sub, _ = all_ref.shape
    stores = []
    for k in range(n_tp):
        for c in range(n_chunk):
            copy = pltpu.make_async_copy(
                tok_ref.at[k, pl.ds(c * sub, sub)],
                all_ref.at[c, lax.rem(tp - k + n_tp, n_tp)],
                sem_out.at[k, c],
            )
            copy.start()
            stores.append(copy)
    lane = lax.broadcasted_iota(jnp.int32, (1, 128), 1)
    first = jnp.bitwise_and(lane, HD - 1) < HD // 2

    def rope(u, cos, sin):
        parts = []
        for a in range(width // 128):
            part = u[:, a * 128 : (a + 1) * 128]
            other = jnp.where(
                first, pltpu.roll(part, 128 - HD // 2, 1), pltpu.roll(part, HD // 2, 1)
            )
            parts.append(part * cos + other * sin)
        return parts

    for k in range(n_tp):
        row0 = pl.multiple_of(lax.rem(tp - k + n_tp, n_tp) * rows, rows)
        x = tok_ref[k].astype(F32)
        inv = lax.rsqrt(jnp.mean(x * x, axis=1, keepdims=True) + 1e-05)
        normed = (x * inv * gain_ref[...].astype(F32)).astype(BF)
        low = jnp.zeros((rows, n_low), F32)
        for j in range(n_tp):
            low = low + lax.dot_general(
                normed[:, j * dd : (j + 1) * dd], down[j], (((1,), (1,)), ((), ())),
                preferred_element_type=F32,
            )
        row = row0 + lax.broadcasted_iota(jnp.int32, (rows, n_low), 0)
        col = lax.broadcasted_iota(jnp.int32, (rows, n_low), 1)
        request = jnp.zeros((rows, n_low), jnp.int32)
        end = jnp.int32(0)
        for r in range(n_req - 1):
            end = end + lens_ref[0, r]
            request = request + (row >= end).astype(jnp.int32)
        own = col // (2 * rank) == request
        kind = (col // rank) % 2
        deltas = []
        for kk in range(2):
            part = jnp.where(own & (kind == kk), low, 0.0).astype(BF)
            deltas.append(jnp.dot(part, up_ref[...], preferred_element_type=F32))
        cos = cos_ref[pl.ds(row0, rows), :]
        sin = sin_ref[pl.ds(row0, rows), :]
        q = jnp.dot(normed, w_ref[0], preferred_element_type=F32) + deltas[0]
        for a, part in enumerate(rope(q, cos, sin)):
            part = part.astype(BF).astype(F32) * (HD ** -0.5)
            q_ref[pl.ds(row0, rows), a * 128 : (a + 1) * 128] = part.astype(BF)
        kk = jnp.dot(normed, w_ref[1], preferred_element_type=F32)
        for a, part in enumerate(rope(kk, cos, sin)):
            k_ref[pl.ds(row0, rows), a * 128 : (a + 1) * 128] = part.astype(BF)
        v = jnp.dot(normed, w_ref[2], preferred_element_type=F32) + deltas[1]
        v_ref[pl.ds(row0, rows), :] = v.astype(BF)
    for copy in stores:
        copy.wait()


def project(
    tp, lens, table, gain, w_qkv, up, cos, sin, toks, downs, n_dp, cap, pool_dev, n_chunk
):
    n_tp = len(toks)
    sub = toks[0].shape[0] // n_chunk
    rows = toks[0].shape[0] * n_tp
    width = w_qkv.shape[2]
    smem = pl.BlockSpec(memory_space=pltpu.SMEM)
    vmem = pl.BlockSpec(memory_space=pltpu.VMEM)
    out = jax.ShapeDtypeStruct((rows, width), BF)
    return pl.pallas_call(
        functools.partial(project_kernel, n_tp, cap, pool_dev),
        out_shape=(
            out, out, out, jax.ShapeDtypeStruct((table.shape[1],), jnp.int32),
            jax.ShapeDtypeStruct((n_chunk, n_tp, sub, toks[0].shape[1]), BF),
        ),
        in_specs=[smem] * 3 + [pl.BlockSpec(memory_space=pltpu.HBM)] * (5 + 2 * n_tp),
        out_specs=(vmem, vmem, vmem, smem, pl.BlockSpec(memory_space=pltpu.HBM)),
        scratch_shapes=[
            pltpu.VMEM((n_tp,) + downs[0].shape, BF),
            pltpu.SMEM((n_dp,), jnp.int32),
        ]
        + [pltpu.VMEM(x.shape, x.dtype) for x in (gain, w_qkv, up, cos, sin)]
        + [
            pltpu.VMEM((n_tp,) + toks[0].shape, BF),
            pltpu.SemaphoreType.DMA((5 + 2 * n_tp,)),
            pltpu.SemaphoreType.DMA((n_tp, n_chunk)),
        ],
        compiler_params=pltpu.CompilerParams(vmem_limit_bytes=60 << 20),
        cost_estimate=LIGHT,
        name="project",
    )(tp, lens, table, gain, w_qkv, up, cos, sin, *toks, *downs)


def attend_kernel(
    group, per, n_chunk, lens_ref, counts_ref, pos_ref, bias_ref,
    q_ref, kn_ref, vn_ref, raw_ref, *rest
):
    out_refs = rest[:-9]
    kc, vc, knp, vnp, qbd, pairs, sbuf, wbuf, obuf = rest[-9:]
    page_len = kc.shape[1]
    width = q_ref.shape[1]
    rows = q_ref.shape[0]
    n_req = lens_ref.shape[1]
    back = knp.shape[0] - rows
    n_page = PAGES_REQ
    n_new = (back + TILE) // KCH

    row = lax.broadcasted_iota(jnp.int32, (2 * page_len, 2 * page_len), 0)
    col = lax.broadcasted_iota(jnp.int32, (2 * page_len, 2 * page_len), 1)
    src = jnp.where(row < page_len, 2 * row, 2 * row - (2 * page_len - 1))
    choose = (col == src).astype(F32).astype(BF)

    def unpack(slot):
        pages = [raw_ref[pos_ref[slot + i]] for i in range(BLK)]
        both = jnp.dot(
            choose, jnp.concatenate(pages, axis=1), preferred_element_type=F32
        ).astype(BF)
        for i in range(BLK):
            kc[slot + i] = both[:page_len, i * width : (i + 1) * width]
            vc[slot + i] = both[page_len:, i * width : (i + 1) * width]

    for slot in range(0, n_req * n_page, BLK):
        unpack(slot)

    knp[:back, :] = jnp.zeros((back, width), BF)
    vnp[:back, :] = jnp.zeros((back, width), BF)
    knp[back:, :] = kn_ref[...]
    vnp[back:, :] = vn_ref[...]

    lane = lax.broadcasted_iota(jnp.int32, (1, width), 1)
    lane_f = lax.broadcasted_iota(jnp.int32, (1, KCH), 1).astype(F32)
    delta = [bias_ref[0, group * per + a] - bias_ref[1, group * per + a] for a in range(per)]
    parts = [slice(a * TILE, (a + 1) * TILE) for a in range(per)]
    n_all = n_page + n_new

    for t in range(rows // TILE):
        qt = q_ref[t * TILE : (t + 1) * TILE, :].astype(F32)
        for a in range(per):
            mine = (lane >= a * HD) & (lane < (a + 1) * HD)
            qbd[t, parts[a], :] = jnp.where(mine, qt, 0.0).astype(BF)

    def list_pairs(r, carry):
        start, found = carry
        end = start + lens_ref[0, r]

        def add(t, found):
            pairs[0, found] = t
            pairs[1, found] = r
            pairs[2, found] = start
            return found + 1

        return end, lax.fori_loop(start // TILE, (end - 1) // TILE + 1, add, found)

    _, found = lax.fori_loop(0, n_req, list_pairs, (jnp.int32(0), jnp.int32(0)))

    def pair_body(i, carry):
        t, r, start = pairs[0, i], pairs[1, i], pairs[2, i]
        row0 = pl.multiple_of(t * TILE, TILE)
        live = counts_ref[0, r]
        end = start + lens_ref[0, r]
        offset = (live * page_len - start).astype(F32)
        start_f = start.astype(F32)
        row = (row0 + lax.broadcasted_iota(jnp.int32, (TILE, KCH), 0)).astype(F32)
        var_first = jnp.floor((row + offset + 0.5) * (1.0 / VARLEN)) * VARLEN

        def scores(keys):
            return lax.dot_general(
                qbd[t], keys, (((1,), (1,)), ((), ())), preferred_element_type=F32
            )

        first = r * n_page
        s_page = scores(kc[pl.ds(first, n_page)].reshape(n_page * page_len, width))
        s_new = scores(knp[pl.ds(row0, back + TILE), :])
        top = [None] * per
        for c in range(n_all):
            if c < n_page:
                dead = jnp.where(c < live, 0.0, NEG)
                same = var_first <= lane_f + c * page_len
            else:
                key_row = lane_f + (row0 - back + (c - n_page) * KCH).astype(F32)
                allowed = (key_row >= start_f) & (key_row <= row)
                same = var_first - offset <= key_row
            for a, p in enumerate(parts):
                if c < n_page:
                    v = s_page[p, c * KCH : (c + 1) * KCH]
                    v = v + jnp.where(same, delta[a] + dead, dead)
                else:
                    v = s_new[p, (c - n_page) * KCH : (c - n_page + 1) * KCH]
                    v = jnp.where(allowed, v + jnp.where(same, delta[a], 0.0), NEG)
                sbuf[c, p, :] = v
                top[a] = v if top[a] is None else jnp.maximum(top[a], v)
        peak = [jnp.broadcast_to(jnp.max(x, axis=1, keepdims=True), (TILE, KCH)) for x in top]
        total = [jnp.zeros((TILE, KCH), F32) for _ in parts]
        for c in range(n_all):
            for a, p in enumerate(parts):
                e = jnp.exp(sbuf[c, p, :] - peak[a])
                sbuf[c, p, :] = e
                total[a] = total[a] + e
        inverse = [
            jnp.broadcast_to(1.0 / jnp.sum(x, axis=1, keepdims=True), (TILE, KCH)) for x in total
        ]
        for c in range(n_all):
            for a, p in enumerate(parts):
                wbuf[p, c * KCH : (c + 1) * KCH] = (sbuf[c, p, :] * inverse[a]).astype(BF)
        o = jnp.dot(
            wbuf[:, : n_page * KCH],
            vc[pl.ds(first, n_page)].reshape(n_page * page_len, width),
            preferred_element_type=F32,
        ) + jnp.dot(
            wbuf[:, n_page * KCH :], vnp[pl.ds(row0, back + TILE), :],
            preferred_element_type=F32,
        )
        mixed = o[parts[0]]
        for a in range(1, per):
            mixed = jnp.where(lane >= a * HD, o[parts[a]], mixed)
        inside = (row >= start_f) & (row < end.astype(F32))
        obuf[t] = jnp.where(inside[:, :width], mixed, obuf[t])
        return carry

    lax.fori_loop(0, found, pair_body, 0)
    per_chunk = rows // n_chunk
    for t in range(rows // TILE):
        if n_chunk == 1:
            out_refs[0][t * TILE : (t + 1) * TILE, :] = obuf[t].astype(BF)
            continue
        sub = TILE // n_chunk
        for c in range(n_chunk):
            part = obuf[t, c * sub : (c + 1) * sub, :].astype(BF)
            if len(out_refs) == 1:
                base = c * per_chunk + t * sub
                out_refs[0][base : base + sub, :] = part
            else:
                out_refs[c][t * sub : (t + 1) * sub, :] = part


def attend(group, lanes, most, n_chunk, apart, lens, counts, pos, bias, q, kn, vn, raw):
    rows = q.shape[0]
    per = lanes // HD
    page_len = raw.shape[1] // 2
    slots = raw.shape[0]
    back = -(-most // KCH) * KCH
    n_all = PAGES_REQ + (back + TILE) // KCH
    n_out = n_chunk if apart else 1
    tiles = rows // TILE
    smem = pl.BlockSpec(memory_space=pltpu.SMEM)
    part = pl.BlockSpec((rows, lanes), lambda i: (0, group))
    return pl.pallas_call(
        functools.partial(attend_kernel, group, per, n_chunk),
        grid=(1,),
        out_shape=[jax.ShapeDtypeStruct((rows // n_out, lanes), BF)] * n_out,
        in_specs=[smem] * 4
        + [part] * 3
        + [pl.BlockSpec(raw.shape, lambda i: (0, 0, 0), pipeline_mode=pl.Buffered(1))],
        out_specs=[pl.BlockSpec((rows // n_out, lanes), lambda i: (0, 0))] * n_out,
        scratch_shapes=[
            pltpu.VMEM((slots, page_len, lanes), BF),
            pltpu.VMEM((slots, page_len, lanes), BF),
            pltpu.VMEM((back + rows, lanes), BF),
            pltpu.VMEM((back + rows, lanes), BF),
            pltpu.VMEM((tiles, per * TILE, lanes), BF),
            pltpu.SMEM((3, tiles + lens.shape[1]), jnp.int32),
            pltpu.VMEM((n_all, per * TILE, KCH), F32),
            pltpu.VMEM((per * TILE, n_all * KCH), BF),
            pltpu.VMEM((tiles, TILE, lanes), F32),
        ],
        compiler_params=pltpu.CompilerParams(vmem_limit_bytes=60 << 20),
        cost_estimate=LIGHT,
        name="attend",
    )(lens, counts, pos, bias, q, kn, vn, raw)


def shift(value, axis, n, k):
    return lax.ppermute(value, axis, [(i, (i + k) % n) for i in range(n)])


def whole_weight(own, halves, dp, n_dp, n_group):
    twins = lax.ppermute(jnp.stack(halves), "dp", [(i, i ^ 1) for i in range(n_dp)])
    first = dp % 2 == 0
    lower = [jnp.where(first, h, twins[k]) for k, h in enumerate(halves)]
    upper = [jnp.where(first, twins[k], h) for k, h in enumerate(halves)]
    if n_group == 2:
        own_parts = jnp.split(own, 2)
        return [
            jnp.concatenate([mine] + part, axis=0)
            for mine, part in zip(own_parts, (lower, upper))
        ]
    both = [x for pair in zip(lower, upper) for x in pair]
    whole = jnp.concatenate([own] + both, axis=0)
    width, d_model = own.shape
    parts = whole.reshape(len(halves) + 1, n_group, width // n_group, d_model)
    return [parts[:, a].reshape(-1, d_model) for a in range(n_group)]


def per_device(
    tokens,
    attn_gain,
    ffn_gain,
    w_qkv,
    w_out,
    w_gateup,
    w_down,
    variate_bias,
    adapter_down,
    adapter_up,
    owner_table,
    lengths,
    adapter_ids,
    page_counts,
    page_table,
    cache_pool,
):
    n_tp = lax.axis_size("tensor")
    n_dp = lax.axis_size("dp")
    tp = lax.axis_index("tensor")
    dp = lax.axis_index("dp")
    me = dp.astype(jnp.int32).reshape(1)
    tp_id = tp.astype(jnp.int32).reshape(1)
    row_count, d_model = tokens.shape
    tok_total = row_count * n_tp
    width = w_out.shape[0]
    page_len = cache_pool.shape[1]
    pool_dev = cache_pool.shape[0]
    cap = max(1, page_table.shape[1] // n_dp)
    far_first = [k for k in range(1, n_tp)]
    lanes = min(width, 2 * HD)
    n_group = width // lanes
    slots = n_dp * cap
    dd = d_model // n_tp
    n_loc, _, rank, _ = adapter_down.shape
    n_chunk = max(1, row_count // CHUNK)
    sub = row_count // n_chunk
    span = 2 * rank

    toks = [tokens] + [shift(tokens, "tensor", n_tp, k) for k in far_first]

    down_part = lax.dynamic_slice_in_dim(adapter_down, tp * dd, dd, 3).reshape(n_loc * span, dd)
    names = jnp.concatenate([page_table // pool_dev, page_table % pool_dev], axis=0).astype(BF)
    names = jnp.pad(names, ((0, 14), (0, dd - names.shape[1])))
    payload = jnp.concatenate([down_part, adapter_up.reshape(n_loc * span, width), names], axis=0)
    gathered = lax.all_gather(payload, "dp", axis=0)
    asked = gathered[:, 2 * n_loc * span : 2 * n_loc * span + 2, : page_table.shape[1]]
    picked = pick(me, asked.astype(jnp.int32), cache_pool, n_dp, cap, lanes)
    send = lax.optimization_barrier((picked[0], toks[1:-1]))[0]
    fetched = [lax.all_to_all(send, "dp", split_axis=0, concat_axis=0, tiled=True)]

    own_half = lax.dynamic_slice_in_dim(w_out, (dp % 2) * (width // 2), width // 2, 0)
    gathered, lengths_b = lax.optimization_barrier((gathered, lengths, send))[:2]
    down_named, up_named = named(owner_table, adapter_ids, gathered, n_loc, span)
    downs = [down_named] + [shift(down_named, "tensor", n_tp, k) for k in far_first]

    _, position = token_layout(lengths_b[0], page_counts[0], page_len, tok_total)
    index = jnp.arange(2 * HD, dtype=jnp.int32)
    frequency = 10000.0 ** (-2.0 * (index % (HD // 2)).astype(F32) / HD)
    angles = (position % VARLEN).astype(F32)[:, None] * frequency[None, :]
    sign = jnp.where(index % HD < HD // 2, -1.0, 1.0).astype(F32)
    query, new_keys, new_values, buffer_pos, all_tokens = project(
        tp_id, lengths, page_table, attn_gain.reshape(1, d_model), w_qkv, up_named,
        jnp.cos(angles), jnp.sin(angles) * sign[None, :], toks, downs, n_dp, cap, pool_dev, n_chunk,
    )
    own_half = lax.optimization_barrier((own_half, downs[1:]))[0]
    halves = [shift(own_half, "tensor", n_tp, k) for k in far_first]
    for a in range(1, n_group):
        send = lax.optimization_barrier((picked[a], fetched[-1], query, halves[:1]))[0]
        fetched.append(lax.all_to_all(send, "dp", split_axis=0, concat_axis=0, tiled=True))
    fetched = [f.reshape(slots, 2 * page_len, lanes) for f in fetched]


    def mixed(blocks, a):
        return jnp.dot(
            jnp.concatenate(blocks, axis=1), w_whole[a], preferred_element_type=F32
        )

    def attended(a, q, apart):
        return attend(
            a, lanes, 2 * TILE, n_chunk, apart, lengths, page_counts, buffer_pos, variate_bias,
            q, new_keys, new_values, fetched[a],
        )

    early = []
    w_whole = None
    for a in range(n_group - 1):
        mix = attended(a, query, False)[0]
        if w_whole is None:
            mix, halves = lax.optimization_barrier((mix, halves))
            w_whole = whole_weight(w_out, halves, dp, n_dp, n_group)
        blocks = [mix] + [shift(mix, "tensor", n_tp, k) for k in far_first]
        query, w_whole, blocks = lax.optimization_barrier((query, w_whole, blocks))
        early.append(blocks)
    if w_whole is None:
        w_whole = whole_weight(w_out, halves, dp, n_dp, n_group)
    last = attended(n_group - 1, query, True)
    early, last, w_whole = lax.optimization_barrier((early, last, w_whole))
    early = [[jnp.split(block, n_chunk) for block in blocks] for blocks in early]
    outs = []
    pieces = None
    bases = []
    late = []
    for c in range(n_chunk):
        own = last[c]
        if bases:
            own = lax.optimization_barrier((own, bases[-1]))[0]
        late.append([own] + [shift(own, "tensor", n_tp, k) for k in far_first])
        base = all_tokens[c].reshape(n_tp * sub, d_model).astype(F32)
        for a in range(n_group - 1):
            base = base + mixed([block[c] for block in early[a]], a)
        bases.append(base)
    for c in range(n_chunk):
        blocks = late[c]
        if pieces is not None:
            blocks = lax.optimization_barrier((blocks, pieces))[0]
        residual = bases[c] + mixed(blocks, n_group - 1)
        ffn_in = normalize(residual, ffn_gain).astype(BF)
        gate_up = jnp.einsum("td,kdf->ktf", ffn_in, w_gateup, preferred_element_type=F32)
        hidden = (jax.nn.silu(gate_up[0]) * gate_up[1]).astype(BF)
        down = jnp.dot(hidden, w_down, preferred_element_type=F32).reshape(n_tp, sub, d_model)
        total = lax.dynamic_index_in_dim(down, tp, 0, False)
        total = total + lax.dynamic_index_in_dim(
            residual.reshape(n_tp, sub, d_model), tp, 0, False
        )
        down = down.astype(BF)
        pieces = [lax.dynamic_index_in_dim(down, (tp + k) % n_tp, 0, False) for k in far_first]
        for k, piece in zip(far_first, pieces):
            total = total + shift(piece, "tensor", n_tp, k).astype(F32)
        outs.append(total.astype(BF))
    return jnp.concatenate(outs, axis=0)


def solution(mesh):
    return jax.shard_map(
        per_device,
        mesh=mesh,
        in_specs=(
            P(("dp", "tensor"), None),
            P(),
            P(),
            P(None, None, "tensor"),
            P("tensor", None),
            P(None, None, "tensor"),
            P("tensor", None),
            P(None, "tensor"),
            P("dp", None, None, None),
            P("dp", None, None, "tensor"),
            P(),
            P("dp", None),
            P("dp", None),
            P("dp", None),
            P("dp", None),
            P("dp", None, None, "tensor"),
        ),
        out_specs=P(("dp", "tensor"), None),
        check_vma=False,
    )
```

```python
import functools

import jax
import jax.numpy as jnp
from jax import lax
from jax.experimental import pallas as pl
from jax.experimental.pallas import tpu as pltpu
from jax.sharding import PartitionSpec as P

HD = 64
PAGES_REQ = 8
VARLEN = 160
TILE = 128
KCH = 128
BLK = 4
CHUNK = 64
BF = jnp.bfloat16
F32 = jnp.float32
NEG = -1e30
LIGHT = pl.CostEstimate(flops=1000, bytes_accessed=1000, transcendentals=0)


def normalize(values, gain):
    values = values.astype(F32)
    inv_scale = lax.rsqrt(jnp.mean(values * values, axis=-1, keepdims=True) + 1e-05)
    return values * inv_scale * gain.astype(F32)


def token_layout(req_lens, live_counts, page_len, tok_total):
    end_pos = jnp.cumsum(req_lens, dtype=jnp.int32)
    starts = end_pos - req_lens
    tok_index = jnp.arange(tok_total, dtype=jnp.int32)
    request = jnp.sum(
        (tok_index[:, None] >= end_pos[None, :]).astype(jnp.int32), axis=1, dtype=jnp.int32
    )
    onehot = request[:, None] == jnp.arange(req_lens.shape[0], dtype=jnp.int32)[None, :]
    first_pos = jnp.sum(jnp.where(onehot, starts[None, :], 0), axis=1, dtype=jnp.int32)
    cached = jnp.sum(jnp.where(onehot, live_counts[None, :], 0), axis=1, dtype=jnp.int32)
    return (onehot, cached * page_len + tok_index - first_pos)


def pick_kernel(n_dp, cap, me_ref, asked_ref, pool_ref, *rest):
    n_out = len(rest) - 3
    outs, (buf, sem_in, sem_out) = rest[:n_out], rest[n_out:]
    lanes = outs[0].shape[-1]
    me = me_ref[0]
    slots = asked_ref.shape[2]

    def find(g, carry):
        count = jnp.int32(0)
        for p in range(slots):
            hit = asked_ref[g, 0, p] == me

            @pl.when(hit)
            def _():
                pltpu.make_async_copy(
                    pool_ref.at[asked_ref[g, 1, p]], buf.at[g, count], sem_in.at[g]
                ).start()

            count = count + hit.astype(jnp.int32)
        return carry

    lax.fori_loop(0, n_dp, find, 0)
    done = []
    for g in range(n_dp):
        pltpu.make_async_copy(pool_ref.at[pl.ds(0, cap)], buf.at[g], sem_in.at[g]).wait()
        for a in range(n_out):
            copy = pltpu.make_async_copy(
                buf.at[g, :, :, :, pl.ds(a * lanes, lanes)], outs[a].at[g], sem_out.at[a, g]
            )
            copy.start()
            done.append(copy)
    for copy in done:
        copy.wait()


def pick(me, asked, pool, n_dp, cap, lanes):
    smem = pl.BlockSpec(memory_space=pltpu.SMEM)
    hbm = pl.BlockSpec(memory_space=pl.ANY)
    n_out = pool.shape[-1] // lanes
    shape = (n_dp, cap) + pool.shape[1:-1]
    return pl.pallas_call(
        functools.partial(pick_kernel, n_dp, cap),
        out_shape=[jax.ShapeDtypeStruct(shape + (lanes,), pool.dtype)] * n_out,
        in_specs=[smem, smem, hbm],
        out_specs=[hbm] * n_out,
        scratch_shapes=[
            pltpu.VMEM(shape + pool.shape[-1:], pool.dtype),
            pltpu.SemaphoreType.DMA((n_dp,)),
            pltpu.SemaphoreType.DMA((n_out, n_dp)),
        ],
        cost_estimate=LIGHT,
        name="pick_pages",
    )(me, asked, pool)


def named_kernel(n_loc, span, table_ref, ids_ref, all_ref, down_out, up_out, down_ref, up_ref, sem):
    copies = []
    for r in range(ids_ref.shape[1]):
        slot = table_ref[ids_ref[0, r]]
        home, inner = slot // n_loc, slot % n_loc
        for half, out in ((0, down_ref), (1, up_ref)):
            base = pl.multiple_of((half * n_loc + inner) * span, span)
            copy = pltpu.make_async_copy(
                all_ref.at[home, pl.ds(base, span)], out.at[pl.ds(r * span, span)], sem.at[r, half]
            )
            copy.start()
            copies.append(copy)
    for copy in copies:
        copy.wait()
    last = [
        pltpu.make_async_copy(down_ref, down_out, sem.at[0, 0]),
        pltpu.make_async_copy(up_ref, up_out, sem.at[0, 1]),
    ]
    for copy in last:
        copy.start()
    for copy in last:
        copy.wait()


def named(owner_table, adapter_ids, gathered, n_loc, span):
    n_req = adapter_ids.shape[1]
    smem = pl.BlockSpec(memory_space=pltpu.SMEM)
    hbm = pl.BlockSpec(memory_space=pltpu.HBM)
    out = jax.ShapeDtypeStruct((n_req * span, gathered.shape[-1]), BF)
    return pl.pallas_call(
        functools.partial(named_kernel, n_loc, span),
        out_shape=(out, out),
        in_specs=[smem, smem, hbm],
        out_specs=(hbm, hbm),
        scratch_shapes=[
            pltpu.VMEM(out.shape, BF),
            pltpu.VMEM(out.shape, BF),
            pltpu.SemaphoreType.DMA((n_req, 2)),
        ],
        cost_estimate=LIGHT,
        name="named_adapters",
    )(owner_table, adapter_ids, gathered)


def project_kernel(n_tp, cap, pool_dev, n_chunk, tp_ref, lens_ref, table_ref, *rest):
    hbm_refs, rest = rest[: 5 + 2 * n_tp], rest[5 + 2 * n_tp :]
    q_ref, k_ref, v_ref, pos_ref = rest[:4]
    all_refs = rest[4 : 4 + n_chunk]
    down, count, *held = rest[4 + n_chunk :]
    held, sem, sem_out = held[:-2], held[-2], held[-1]
    gain_ref, w_ref, up_ref, cos_ref, sin_ref, tok_ref = held
    tp = tp_ref[0]
    copies = []
    targets = list(held[:5]) + [tok_ref.at[k] for k in range(n_tp)]
    for k in range(n_tp):
        targets.append(down.at[lax.rem(tp - k + n_tp, n_tp)])
    for i in list(range(5, 5 + 2 * n_tp)) + list(range(5)):
        copy = pltpu.make_async_copy(hbm_refs[i], targets[i], sem.at[i])
        copy.start()
        copies.append(copy)
    _, rows, _ = tok_ref.shape
    width = q_ref.shape[1]
    n_low, dd = down.shape[1:]
    n_req = lens_ref.shape[1]
    rank = n_low // n_req // 2

    for g in range(count.shape[0]):
        count[g] = 0

    def place(p, carry):
        home = table_ref[0, p] // pool_dev
        seen = count[home]
        count[home] = seen + 1
        pos_ref[p] = home * cap + seen
        return carry

    lax.fori_loop(0, table_ref.shape[1], place, 0)

    for copy in copies:
        copy.wait()
    sub = all_refs[0].shape[1]
    stores = []
    for k in range(n_tp):
        for c in range(n_chunk):
            copy = pltpu.make_async_copy(
                tok_ref.at[k, pl.ds(c * sub, sub)],
                all_refs[c].at[lax.rem(tp - k + n_tp, n_tp)],
                sem_out.at[k, c],
            )
            copy.start()
            stores.append(copy)
    lane = lax.broadcasted_iota(jnp.int32, (1, 128), 1)
    first = jnp.bitwise_and(lane, HD - 1) < HD // 2

    def rope(u, cos, sin):
        parts = []
        for a in range(width // 128):
            part = u[:, a * 128 : (a + 1) * 128]
            other = jnp.where(
                first, pltpu.roll(part, 128 - HD // 2, 1), pltpu.roll(part, HD // 2, 1)
            )
            parts.append(part * cos + other * sin)
        return parts

    for k in range(n_tp):
        row0 = pl.multiple_of(lax.rem(tp - k + n_tp, n_tp) * rows, rows)
        x = tok_ref[k].astype(F32)
        inv = lax.rsqrt(jnp.mean(x * x, axis=1, keepdims=True) + 1e-05)
        normed = (x * inv * gain_ref[...].astype(F32)).astype(BF)
        low = jnp.zeros((rows, n_low), F32)
        for j in range(n_tp):
            low = low + lax.dot_general(
                normed[:, j * dd : (j + 1) * dd], down[j], (((1,), (1,)), ((), ())),
                preferred_element_type=F32,
            )
        row = row0 + lax.broadcasted_iota(jnp.int32, (rows, n_low), 0)
        col = lax.broadcasted_iota(jnp.int32, (rows, n_low), 1)
        request = jnp.zeros((rows, n_low), jnp.int32)
        end = jnp.int32(0)
        for r in range(n_req - 1):
            end = end + lens_ref[0, r]
            request = request + (row >= end).astype(jnp.int32)
        own = col // (2 * rank) == request
        kind = (col // rank) % 2
        deltas = []
        for kk in range(2):
            part = jnp.where(own & (kind == kk), low, 0.0).astype(BF)
            deltas.append(jnp.dot(part, up_ref[...], preferred_element_type=F32))
        cos = cos_ref[pl.ds(row0, rows), :]
        sin = sin_ref[pl.ds(row0, rows), :]
        q = jnp.dot(normed, w_ref[0], preferred_element_type=F32) + deltas[0]
        for a, part in enumerate(rope(q, cos, sin)):
            part = part.astype(BF).astype(F32) * (HD ** -0.5)
            q_ref[pl.ds(row0, rows), a * 128 : (a + 1) * 128] = part.astype(BF)
        kk = jnp.dot(normed, w_ref[1], preferred_element_type=F32)
        for a, part in enumerate(rope(kk, cos, sin)):
            k_ref[pl.ds(row0, rows), a * 128 : (a + 1) * 128] = part.astype(BF)
        v = jnp.dot(normed, w_ref[2], preferred_element_type=F32) + deltas[1]
        v_ref[pl.ds(row0, rows), :] = v.astype(BF)
    for copy in stores:
        copy.wait()


def project(
    tp, lens, table, gain, w_qkv, up, cos, sin, toks, downs, n_dp, cap, pool_dev, n_chunk
):
    n_tp = len(toks)
    sub = toks[0].shape[0] // n_chunk
    rows = toks[0].shape[0] * n_tp
    width = w_qkv.shape[2]
    smem = pl.BlockSpec(memory_space=pltpu.SMEM)
    vmem = pl.BlockSpec(memory_space=pltpu.VMEM)
    out = jax.ShapeDtypeStruct((rows, width), BF)
    return pl.pallas_call(
        functools.partial(project_kernel, n_tp, cap, pool_dev, n_chunk),
        out_shape=(
            out, out, out, jax.ShapeDtypeStruct((table.shape[1],), jnp.int32),
        )
        + (jax.ShapeDtypeStruct((n_tp, sub, toks[0].shape[1]), BF),) * n_chunk,
        in_specs=[smem] * 3 + [pl.BlockSpec(memory_space=pltpu.HBM)] * (5 + 2 * n_tp),
        out_specs=(vmem, vmem, vmem, smem) + (pl.BlockSpec(memory_space=pltpu.HBM),) * n_chunk,
        scratch_shapes=[
            pltpu.VMEM((n_tp,) + downs[0].shape, BF),
            pltpu.SMEM((n_dp,), jnp.int32),
        ]
        + [pltpu.VMEM(x.shape, x.dtype) for x in (gain, w_qkv, up, cos, sin)]
        + [
            pltpu.VMEM((n_tp,) + toks[0].shape, BF),
            pltpu.SemaphoreType.DMA((5 + 2 * n_tp,)),
            pltpu.SemaphoreType.DMA((n_tp, n_chunk)),
        ],
        compiler_params=pltpu.CompilerParams(vmem_limit_bytes=60 << 20),
        cost_estimate=LIGHT,
        name="project",
    )(tp, lens, table, gain, w_qkv, up, cos, sin, *toks, *downs)


def attend_kernel(
    group, per, n_chunk, lens_ref, counts_ref, pos_ref, bias_ref,
    q_ref, kn_ref, vn_ref, raw_ref, *rest
):
    out_refs = rest[:-9]
    kc, vc, knp, vnp, qbd, pairs, sbuf, wbuf, obuf = rest[-9:]
    page_len = kc.shape[1]
    width = q_ref.shape[1]
    rows = q_ref.shape[0]
    n_req = lens_ref.shape[1]
    back = knp.shape[0] - rows
    n_page = PAGES_REQ
    n_new = (back + TILE) // KCH

    row = lax.broadcasted_iota(jnp.int32, (2 * page_len, 2 * page_len), 0)
    col = lax.broadcasted_iota(jnp.int32, (2 * page_len, 2 * page_len), 1)
    src = jnp.where(row < page_len, 2 * row, 2 * row - (2 * page_len - 1))
    choose = (col == src).astype(F32).astype(BF)

    def unpack(slot):
        pages = [raw_ref[pos_ref[slot + i]] for i in range(BLK)]
        both = jnp.dot(
            choose, jnp.concatenate(pages, axis=1), preferred_element_type=F32
        ).astype(BF)
        for i in range(BLK):
            kc[slot + i] = both[:page_len, i * width : (i + 1) * width]
            vc[slot + i] = both[page_len:, i * width : (i + 1) * width]

    for slot in range(0, n_req * n_page, BLK):
        unpack(slot)

    knp[:back, :] = jnp.zeros((back, width), BF)
    vnp[:back, :] = jnp.zeros((back, width), BF)
    knp[back:, :] = kn_ref[...]
    vnp[back:, :] = vn_ref[...]

    lane = lax.broadcasted_iota(jnp.int32, (1, width), 1)
    lane_f = lax.broadcasted_iota(jnp.int32, (1, KCH), 1).astype(F32)
    delta = [bias_ref[0, group * per + a] - bias_ref[1, group * per + a] for a in range(per)]
    parts = [slice(a * TILE, (a + 1) * TILE) for a in range(per)]
    n_all = n_page + n_new

    for t in range(rows // TILE):
        qt = q_ref[t * TILE : (t + 1) * TILE, :].astype(F32)
        for a in range(per):
            mine = (lane >= a * HD) & (lane < (a + 1) * HD)
            qbd[t, parts[a], :] = jnp.where(mine, qt, 0.0).astype(BF)

    def list_pairs(r, carry):
        start, found = carry
        end = start + lens_ref[0, r]

        def add(t, found):
            pairs[0, found] = t
            pairs[1, found] = r
            pairs[2, found] = start
            return found + 1

        return end, lax.fori_loop(start // TILE, (end - 1) // TILE + 1, add, found)

    _, found = lax.fori_loop(0, n_req, list_pairs, (jnp.int32(0), jnp.int32(0)))

    def pair_body(i, carry):
        t, r, start = pairs[0, i], pairs[1, i], pairs[2, i]
        row0 = pl.multiple_of(t * TILE, TILE)
        live = counts_ref[0, r]
        end = start + lens_ref[0, r]
        offset = (live * page_len - start).astype(F32)
        start_f = start.astype(F32)
        row = (row0 + lax.broadcasted_iota(jnp.int32, (TILE, KCH), 0)).astype(F32)
        var_first = jnp.floor((row + offset + 0.5) * (1.0 / VARLEN)) * VARLEN

        def scores(keys):
            return lax.dot_general(
                qbd[t], keys, (((1,), (1,)), ((), ())), preferred_element_type=F32
            )

        first = r * n_page
        s_page = scores(kc[pl.ds(first, n_page)].reshape(n_page * page_len, width))
        s_new = scores(knp[pl.ds(row0, back + TILE), :])
        top = [None] * per
        for c in range(n_all):
            if c < n_page:
                dead = jnp.where(c < live, 0.0, NEG)
                same = var_first <= lane_f + c * page_len
            else:
                key_row = lane_f + (row0 - back + (c - n_page) * KCH).astype(F32)
                allowed = (key_row >= start_f) & (key_row <= row)
                same = var_first - offset <= key_row
            for a, p in enumerate(parts):
                if c < n_page:
                    v = s_page[p, c * KCH : (c + 1) * KCH]
                    v = v + jnp.where(same, delta[a] + dead, dead)
                else:
                    v = s_new[p, (c - n_page) * KCH : (c - n_page + 1) * KCH]
                    v = jnp.where(allowed, v + jnp.where(same, delta[a], 0.0), NEG)
                sbuf[c, p, :] = v
                top[a] = v if top[a] is None else jnp.maximum(top[a], v)
        peak = [jnp.broadcast_to(jnp.max(x, axis=1, keepdims=True), (TILE, KCH)) for x in top]
        total = [jnp.zeros((TILE, KCH), F32) for _ in parts]
        for c in range(n_all):
            for a, p in enumerate(parts):
                e = jnp.exp(sbuf[c, p, :] - peak[a])
                sbuf[c, p, :] = e
                total[a] = total[a] + e
        inverse = [
            jnp.broadcast_to(1.0 / jnp.sum(x, axis=1, keepdims=True), (TILE, KCH)) for x in total
        ]
        for c in range(n_all):
            for a, p in enumerate(parts):
                wbuf[p, c * KCH : (c + 1) * KCH] = (sbuf[c, p, :] * inverse[a]).astype(BF)
        o = jnp.dot(
            wbuf[:, : n_page * KCH],
            vc[pl.ds(first, n_page)].reshape(n_page * page_len, width),
            preferred_element_type=F32,
        ) + jnp.dot(
            wbuf[:, n_page * KCH :], vnp[pl.ds(row0, back + TILE), :],
            preferred_element_type=F32,
        )
        mixed = o[parts[0]]
        for a in range(1, per):
            mixed = jnp.where(lane >= a * HD, o[parts[a]], mixed)
        inside = (row >= start_f) & (row < end.astype(F32))
        obuf[t] = jnp.where(inside[:, :width], mixed, obuf[t])
        return carry

    lax.fori_loop(0, found, pair_body, 0)
    per_chunk = rows // n_chunk
    for t in range(rows // TILE):
        if n_chunk == 1:
            out_refs[0][t * TILE : (t + 1) * TILE, :] = obuf[t].astype(BF)
            continue
        sub = TILE // n_chunk
        for c in range(n_chunk):
            part = obuf[t, c * sub : (c + 1) * sub, :].astype(BF)
            if len(out_refs) == 1:
                base = c * per_chunk + t * sub
                out_refs[0][base : base + sub, :] = part
            else:
                out_refs[c][t * sub : (t + 1) * sub, :] = part


def attend(group, lanes, most, n_chunk, apart, lens, counts, pos, bias, q, kn, vn, raw):
    rows = q.shape[0]
    per = lanes // HD
    page_len = raw.shape[1] // 2
    slots = raw.shape[0]
    back = -(-most // KCH) * KCH
    n_all = PAGES_REQ + (back + TILE) // KCH
    n_out = n_chunk if apart else 1
    tiles = rows // TILE
    smem = pl.BlockSpec(memory_space=pltpu.SMEM)
    part = pl.BlockSpec((rows, lanes), lambda i: (0, group))
    return pl.pallas_call(
        functools.partial(attend_kernel, group, per, n_chunk),
        grid=(1,),
        out_shape=[jax.ShapeDtypeStruct((rows // n_out, lanes), BF)] * n_out,
        in_specs=[smem] * 4
        + [part] * 3
        + [pl.BlockSpec(raw.shape, lambda i: (0, 0, 0), pipeline_mode=pl.Buffered(1))],
        out_specs=[pl.BlockSpec((rows // n_out, lanes), lambda i: (0, 0))] * n_out,
        scratch_shapes=[
            pltpu.VMEM((slots, page_len, lanes), BF),
            pltpu.VMEM((slots, page_len, lanes), BF),
            pltpu.VMEM((back + rows, lanes), BF),
            pltpu.VMEM((back + rows, lanes), BF),
            pltpu.VMEM((tiles, per * TILE, lanes), BF),
            pltpu.SMEM((3, tiles + lens.shape[1]), jnp.int32),
            pltpu.VMEM((n_all, per * TILE, KCH), F32),
            pltpu.VMEM((per * TILE, n_all * KCH), BF),
            pltpu.VMEM((tiles, TILE, lanes), F32),
        ],
        compiler_params=pltpu.CompilerParams(vmem_limit_bytes=60 << 20),
        cost_estimate=LIGHT,
        name="attend",
    )(lens, counts, pos, bias, q, kn, vn, raw)


def shift(value, axis, n, k):
    return lax.ppermute(value, axis, [(i, (i + k) % n) for i in range(n)])


def whole_weight(own, halves, dp, n_dp, n_group):
    twins = lax.ppermute(jnp.stack(halves), "dp", [(i, i ^ 1) for i in range(n_dp)])
    first = dp % 2 == 0
    lower = [jnp.where(first, h, twins[k]) for k, h in enumerate(halves)]
    upper = [jnp.where(first, twins[k], h) for k, h in enumerate(halves)]
    if n_group == 2:
        own_parts = jnp.split(own, 2)
        return [
            jnp.concatenate([mine] + part, axis=0)
            for mine, part in zip(own_parts, (lower, upper))
        ]
    both = [x for pair in zip(lower, upper) for x in pair]
    whole = jnp.concatenate([own] + both, axis=0)
    width, d_model = own.shape
    parts = whole.reshape(len(halves) + 1, n_group, width // n_group, d_model)
    return [parts[:, a].reshape(-1, d_model) for a in range(n_group)]


def per_device(
    tokens,
    attn_gain,
    ffn_gain,
    w_qkv,
    w_out,
    w_gateup,
    w_down,
    variate_bias,
    adapter_down,
    adapter_up,
    owner_table,
    lengths,
    adapter_ids,
    page_counts,
    page_table,
    cache_pool,
):
    n_tp = lax.axis_size("tensor")
    n_dp = lax.axis_size("dp")
    tp = lax.axis_index("tensor")
    dp = lax.axis_index("dp")
    me = dp.astype(jnp.int32).reshape(1)
    tp_id = tp.astype(jnp.int32).reshape(1)
    row_count, d_model = tokens.shape
    tok_total = row_count * n_tp
    width = w_out.shape[0]
    page_len = cache_pool.shape[1]
    pool_dev = cache_pool.shape[0]
    cap = max(1, page_table.shape[1] // n_dp)
    far_first = [k for k in range(1, n_tp)]
    lanes = min(width, 2 * HD)
    n_group = width // lanes
    slots = n_dp * cap
    dd = d_model // n_tp
    n_loc, _, rank, _ = adapter_down.shape
    n_chunk = max(1, row_count // CHUNK)
    sub = row_count // n_chunk
    span = 2 * rank

    toks = [tokens] + [shift(tokens, "tensor", n_tp, k) for k in far_first]

    down_part = lax.dynamic_slice_in_dim(adapter_down, tp * dd, dd, 3).reshape(n_loc * span, dd)
    names = jnp.concatenate([page_table // pool_dev, page_table % pool_dev], axis=0).astype(BF)
    names = jnp.pad(names, ((0, 14), (0, dd - names.shape[1])))
    payload = jnp.concatenate([down_part, adapter_up.reshape(n_loc * span, width), names], axis=0)
    gathered = lax.all_gather(payload, "dp", axis=0)
    asked = gathered[:, 2 * n_loc * span : 2 * n_loc * span + 2, : page_table.shape[1]]
    picked = pick(me, asked.astype(jnp.int32), cache_pool, n_dp, cap, lanes)
    send = lax.optimization_barrier((picked[0], toks[1:-1]))[0]
    fetched = [lax.all_to_all(send, "dp", split_axis=0, concat_axis=0, tiled=True)]

    own_half = lax.dynamic_slice_in_dim(w_out, (dp % 2) * (width // 2), width // 2, 0)
    gathered, lengths_b = lax.optimization_barrier((gathered, lengths, send))[:2]
    down_named, up_named = named(owner_table, adapter_ids, gathered, n_loc, span)
    downs = [down_named] + [shift(down_named, "tensor", n_tp, k) for k in far_first]

    _, position = token_layout(lengths_b[0], page_counts[0], page_len, tok_total)
    index = jnp.arange(2 * HD, dtype=jnp.int32)
    frequency = 10000.0 ** (-2.0 * (index % (HD // 2)).astype(F32) / HD)
    angles = (position % VARLEN).astype(F32)[:, None] * frequency[None, :]
    sign = jnp.where(index % HD < HD // 2, -1.0, 1.0).astype(F32)
    query, new_keys, new_values, buffer_pos, *all_tokens = project(
        tp_id, lengths, page_table, attn_gain.reshape(1, d_model), w_qkv, up_named,
        jnp.cos(angles), jnp.sin(angles) * sign[None, :], toks, downs, n_dp, cap, pool_dev, n_chunk,
    )
    own_half = lax.optimization_barrier((own_half, downs[1:]))[0]
    halves = [shift(own_half, "tensor", n_tp, k) for k in far_first]
    for a in range(1, n_group):
        send = lax.optimization_barrier((picked[a], fetched[-1], query, halves[:1]))[0]
        fetched.append(lax.all_to_all(send, "dp", split_axis=0, concat_axis=0, tiled=True))
    fetched = [f.reshape(slots, 2 * page_len, lanes) for f in fetched]


    def mixed(blocks, a):
        return jnp.dot(
            jnp.concatenate(blocks, axis=1), w_whole[a], preferred_element_type=F32
        )

    def attended(a, q, apart):
        return attend(
            a, lanes, 2 * TILE, n_chunk, apart, lengths, page_counts, buffer_pos, variate_bias,
            q, new_keys, new_values, fetched[a],
        )

    early = []
    w_whole = None
    for a in range(n_group - 1):
        mix = attended(a, query, False)[0]
        if w_whole is None:
            mix, halves = lax.optimization_barrier((mix, halves))
            w_whole = whole_weight(w_out, halves, dp, n_dp, n_group)
        blocks = [mix] + [shift(mix, "tensor", n_tp, k) for k in far_first]
        query, w_whole = lax.optimization_barrier((query, w_whole))
        early.append(blocks)
    if w_whole is None:
        w_whole = whole_weight(w_out, halves, dp, n_dp, n_group)
    last = attended(n_group - 1, query, True)
    early, last, w_whole = lax.optimization_barrier((early, last, w_whole))
    early = [[jnp.split(block, n_chunk) for block in blocks] for blocks in early]
    outs = []
    pieces = None
    bases = []
    late = []
    for c in range(n_chunk):
        own = last[c]
        if bases:
            own = lax.optimization_barrier((own, bases[-1]))[0]
        late.append([own] + [shift(own, "tensor", n_tp, k) for k in far_first])
        base = all_tokens[c].reshape(n_tp * sub, d_model).astype(F32)
        for a in range(n_group - 1):
            base = base + mixed([block[c] for block in early[a]], a)
        bases.append(base)
    for c in range(n_chunk):
        blocks = late[c]
        if pieces is not None:
            blocks = lax.optimization_barrier((blocks, pieces))[0]
        residual = bases[c] + mixed(blocks, n_group - 1)
        ffn_in = normalize(residual, ffn_gain).astype(BF)
        gate_up = jnp.einsum("td,kdf->ktf", ffn_in, w_gateup, preferred_element_type=F32)
        hidden = (jax.nn.silu(gate_up[0]) * gate_up[1]).astype(BF)
        down = jnp.dot(hidden, w_down, preferred_element_type=F32).reshape(n_tp, sub, d_model)
        total = lax.dynamic_index_in_dim(down, tp, 0, False)
        total = total + lax.dynamic_index_in_dim(
            residual.reshape(n_tp, sub, d_model), tp, 0, False
        )
        down = down.astype(BF)
        pieces = [lax.dynamic_index_in_dim(down, (tp + k) % n_tp, 0, False) for k in far_first]
        for k, piece in zip(far_first, pieces):
            total = total + shift(piece, "tensor", n_tp, k).astype(F32)
        outs.append(total.astype(BF))
    return jnp.concatenate(outs, axis=0)


def solution(mesh):
    return jax.shard_map(
        per_device,
        mesh=mesh,
        in_specs=(
            P(("dp", "tensor"), None),
            P(),
            P(),
            P(None, None, "tensor"),
            P("tensor", None),
            P(None, None, "tensor"),
            P("tensor", None),
            P(None, "tensor"),
            P("dp", None, None, None),
            P("dp", None, None, "tensor"),
            P(),
            P("dp", None),
            P("dp", None),
            P("dp", None),
            P("dp", None),
            P("dp", None, None, "tensor"),
        ),
        out_specs=P(("dp", "tensor"), None),
        check_vma=False,
    )
```

```python
import functools

import jax
import jax.numpy as jnp
from jax import lax
from jax.experimental import pallas as pl
from jax.experimental.pallas import tpu as pltpu
from jax.sharding import PartitionSpec as P

HD = 64
PAGES_REQ = 8
VARLEN = 160
TILE = 128
KCH = 128
BLK = 4
CHUNK = 64
BF = jnp.bfloat16
F32 = jnp.float32
NEG = -1e30
LIGHT = pl.CostEstimate(flops=1000, bytes_accessed=1000, transcendentals=0)


def normalize(values, gain):
    values = values.astype(F32)
    inv_scale = lax.rsqrt(jnp.mean(values * values, axis=-1, keepdims=True) + 1e-05)
    return values * inv_scale * gain.astype(F32)


def token_layout(req_lens, live_counts, page_len, tok_total):
    end_pos = jnp.cumsum(req_lens, dtype=jnp.int32)
    starts = end_pos - req_lens
    tok_index = jnp.arange(tok_total, dtype=jnp.int32)
    request = jnp.sum(
        (tok_index[:, None] >= end_pos[None, :]).astype(jnp.int32), axis=1, dtype=jnp.int32
    )
    onehot = request[:, None] == jnp.arange(req_lens.shape[0], dtype=jnp.int32)[None, :]
    first_pos = jnp.sum(jnp.where(onehot, starts[None, :], 0), axis=1, dtype=jnp.int32)
    cached = jnp.sum(jnp.where(onehot, live_counts[None, :], 0), axis=1, dtype=jnp.int32)
    return (onehot, cached * page_len + tok_index - first_pos)


def pick_kernel(n_dp, cap, me_ref, asked_ref, pool_ref, *rest):
    n_out = len(rest) - 3
    outs, (buf, sem_in, sem_out) = rest[:n_out], rest[n_out:]
    lanes = outs[0].shape[-1]
    me = me_ref[0]
    slots = asked_ref.shape[2]

    def find(g, carry):
        count = jnp.int32(0)
        for p in range(slots):
            hit = asked_ref[g, 0, p] == me

            @pl.when(hit)
            def _():
                pltpu.make_async_copy(
                    pool_ref.at[asked_ref[g, 1, p]], buf.at[g, count], sem_in.at[g]
                ).start()

            count = count + hit.astype(jnp.int32)
        return carry

    lax.fori_loop(0, n_dp, find, 0)
    done = []
    for g in range(n_dp):
        pltpu.make_async_copy(pool_ref.at[pl.ds(0, cap)], buf.at[g], sem_in.at[g]).wait()
        for a in range(n_out):
            copy = pltpu.make_async_copy(
                buf.at[g, :, :, :, pl.ds(a * lanes, lanes)], outs[a].at[g], sem_out.at[a, g]
            )
            copy.start()
            done.append(copy)
    for copy in done:
        copy.wait()


def pick(me, asked, pool, n_dp, cap, lanes):
    smem = pl.BlockSpec(memory_space=pltpu.SMEM)
    hbm = pl.BlockSpec(memory_space=pl.ANY)
    n_out = pool.shape[-1] // lanes
    shape = (n_dp, cap) + pool.shape[1:-1]
    return pl.pallas_call(
        functools.partial(pick_kernel, n_dp, cap),
        out_shape=[jax.ShapeDtypeStruct(shape + (lanes,), pool.dtype)] * n_out,
        in_specs=[smem, smem, hbm],
        out_specs=[hbm] * n_out,
        scratch_shapes=[
            pltpu.VMEM(shape + pool.shape[-1:], pool.dtype),
            pltpu.SemaphoreType.DMA((n_dp,)),
            pltpu.SemaphoreType.DMA((n_out, n_dp)),
        ],
        cost_estimate=LIGHT,
        name="pick_pages",
    )(me, asked, pool)


def named_kernel(n_loc, span, table_ref, ids_ref, all_ref, down_out, up_out, down_ref, up_ref, sem):
    copies = []
    for r in range(ids_ref.shape[1]):
        slot = table_ref[ids_ref[0, r]]
        home, inner = slot // n_loc, slot % n_loc
        for half, out in ((0, down_ref), (1, up_ref)):
            base = pl.multiple_of((half * n_loc + inner) * span, span)
            copy = pltpu.make_async_copy(
                all_ref.at[home, pl.ds(base, span)], out.at[pl.ds(r * span, span)], sem.at[r, half]
            )
            copy.start()
            copies.append(copy)
    for copy in copies:
        copy.wait()
    last = [
        pltpu.make_async_copy(down_ref, down_out, sem.at[0, 0]),
        pltpu.make_async_copy(up_ref, up_out, sem.at[0, 1]),
    ]
    for copy in last:
        copy.start()
    for copy in last:
        copy.wait()


def named(owner_table, adapter_ids, gathered, n_loc, span):
    n_req = adapter_ids.shape[1]
    smem = pl.BlockSpec(memory_space=pltpu.SMEM)
    hbm = pl.BlockSpec(memory_space=pltpu.HBM)
    out = jax.ShapeDtypeStruct((n_req * span, gathered.shape[-1]), BF)
    return pl.pallas_call(
        functools.partial(named_kernel, n_loc, span),
        out_shape=(out, out),
        in_specs=[smem, smem, hbm],
        out_specs=(hbm, hbm),
        scratch_shapes=[
            pltpu.VMEM(out.shape, BF),
            pltpu.VMEM(out.shape, BF),
            pltpu.SemaphoreType.DMA((n_req, 2)),
        ],
        cost_estimate=LIGHT,
        name="named_adapters",
    )(owner_table, adapter_ids, gathered)


def project_kernel(n_tp, cap, pool_dev, n_chunk, tp_ref, lens_ref, table_ref, *rest):
    hbm_refs, rest = rest[: 5 + 2 * n_tp], rest[5 + 2 * n_tp :]
    q_ref, k_ref, v_ref, pos_ref = rest[:4]
    all_refs = rest[4 : 4 + n_chunk]
    down, count, *held = rest[4 + n_chunk :]
    held, sem, sem_out = held[:-2], held[-2], held[-1]
    gain_ref, w_ref, up_ref, cos_ref, sin_ref, tok_ref = held
    tp = tp_ref[0]
    copies = []
    targets = list(held[:5]) + [tok_ref.at[k] for k in range(n_tp)]
    for k in range(n_tp):
        targets.append(down.at[lax.rem(tp - k + n_tp, n_tp)])
    for i in list(range(5, 5 + 2 * n_tp)) + list(range(5)):
        copy = pltpu.make_async_copy(hbm_refs[i], targets[i], sem.at[i])
        copy.start()
        copies.append(copy)
    _, rows, _ = tok_ref.shape
    width = q_ref.shape[1]
    n_low, dd = down.shape[1:]
    n_req = lens_ref.shape[1]
    rank = n_low // n_req // 2

    for g in range(count.shape[0]):
        count[g] = 0

    def place(p, carry):
        home = table_ref[0, p] // pool_dev
        seen = count[home]
        count[home] = seen + 1
        pos_ref[p] = home * cap + seen
        return carry

    lax.fori_loop(0, table_ref.shape[1], place, 0)

    for copy in copies:
        copy.wait()
    sub = all_refs[0].shape[1]
    stores = []
    for k in range(n_tp):
        for c in range(n_chunk):
            copy = pltpu.make_async_copy(
                tok_ref.at[k, pl.ds(c * sub, sub)],
                all_refs[c].at[lax.rem(tp - k + n_tp, n_tp)],
                sem_out.at[k, c],
            )
            copy.start()
            stores.append(copy)
    lane = lax.broadcasted_iota(jnp.int32, (1, 128), 1)
    first = jnp.bitwise_and(lane, HD - 1) < HD // 2

    def rope(u, cos, sin):
        parts = []
        for a in range(width // 128):
            part = u[:, a * 128 : (a + 1) * 128]
            other = jnp.where(
                first, pltpu.roll(part, 128 - HD // 2, 1), pltpu.roll(part, HD // 2, 1)
            )
            parts.append(part * cos + other * sin)
        return parts

    for k in range(n_tp):
        row0 = pl.multiple_of(lax.rem(tp - k + n_tp, n_tp) * rows, rows)
        x = tok_ref[k].astype(F32)
        inv = lax.rsqrt(jnp.mean(x * x, axis=1, keepdims=True) + 1e-05)
        normed = (x * inv * gain_ref[...].astype(F32)).astype(BF)
        low = jnp.zeros((rows, n_low), F32)
        for j in range(n_tp):
            low = low + lax.dot_general(
                normed[:, j * dd : (j + 1) * dd], down[j], (((1,), (1,)), ((), ())),
                preferred_element_type=F32,
            )
        row = row0 + lax.broadcasted_iota(jnp.int32, (rows, n_low), 0)
        col = lax.broadcasted_iota(jnp.int32, (rows, n_low), 1)
        request = jnp.zeros((rows, n_low), jnp.int32)
        end = jnp.int32(0)
        for r in range(n_req - 1):
            end = end + lens_ref[0, r]
            request = request + (row >= end).astype(jnp.int32)
        own = col // (2 * rank) == request
        kind = (col // rank) % 2
        deltas = []
        for kk in range(2):
            part = jnp.where(own & (kind == kk), low, 0.0).astype(BF)
            deltas.append(jnp.dot(part, up_ref[...], preferred_element_type=F32))
        cos = cos_ref[pl.ds(row0, rows), :]
        sin = sin_ref[pl.ds(row0, rows), :]
        q = jnp.dot(normed, w_ref[0], preferred_element_type=F32) + deltas[0]
        for a, part in enumerate(rope(q, cos, sin)):
            part = part.astype(BF).astype(F32) * (HD ** -0.5)
            q_ref[pl.ds(row0, rows), a * 128 : (a + 1) * 128] = part.astype(BF)
        kk = jnp.dot(normed, w_ref[1], preferred_element_type=F32)
        for a, part in enumerate(rope(kk, cos, sin)):
            k_ref[pl.ds(row0, rows), a * 128 : (a + 1) * 128] = part.astype(BF)
        v = jnp.dot(normed, w_ref[2], preferred_element_type=F32) + deltas[1]
        v_ref[pl.ds(row0, rows), :] = v.astype(BF)
    for copy in stores:
        copy.wait()


def project(
    tp, lens, table, gain, w_qkv, up, cos, sin, toks, downs, n_dp, cap, pool_dev, n_chunk
):
    n_tp = len(toks)
    sub = toks[0].shape[0] // n_chunk
    rows = toks[0].shape[0] * n_tp
    width = w_qkv.shape[2]
    smem = pl.BlockSpec(memory_space=pltpu.SMEM)
    vmem = pl.BlockSpec(memory_space=pltpu.VMEM)
    out = jax.ShapeDtypeStruct((rows, width), BF)
    return pl.pallas_call(
        functools.partial(project_kernel, n_tp, cap, pool_dev, n_chunk),
        out_shape=(
            out, out, out, jax.ShapeDtypeStruct((table.shape[1],), jnp.int32),
        )
        + (jax.ShapeDtypeStruct((n_tp, sub, toks[0].shape[1]), BF),) * n_chunk,
        in_specs=[smem] * 3 + [pl.BlockSpec(memory_space=pltpu.HBM)] * (5 + 2 * n_tp),
        out_specs=(vmem, vmem, vmem, smem) + (pl.BlockSpec(memory_space=pltpu.HBM),) * n_chunk,
        scratch_shapes=[
            pltpu.VMEM((n_tp,) + downs[0].shape, BF),
            pltpu.SMEM((n_dp,), jnp.int32),
        ]
        + [pltpu.VMEM(x.shape, x.dtype) for x in (gain, w_qkv, up, cos, sin)]
        + [
            pltpu.VMEM((n_tp,) + toks[0].shape, BF),
            pltpu.SemaphoreType.DMA((5 + 2 * n_tp,)),
            pltpu.SemaphoreType.DMA((n_tp, n_chunk)),
        ],
        compiler_params=pltpu.CompilerParams(vmem_limit_bytes=60 << 20),
        cost_estimate=LIGHT,
        name="project",
    )(tp, lens, table, gain, w_qkv, up, cos, sin, *toks, *downs)


def attend_kernel(
    group, per, n_chunk, lens_ref, counts_ref, pos_ref, bias_ref,
    q_ref, kn_ref, vn_ref, raw_ref, *rest
):
    out_refs = rest[:-9]
    kc, vc, knp, vnp, qbd, pairs, sbuf, wbuf, obuf = rest[-9:]
    page_len = kc.shape[1]
    width = q_ref.shape[1]
    rows = q_ref.shape[0]
    n_req = lens_ref.shape[1]
    back = knp.shape[0] - rows
    n_page = PAGES_REQ
    n_new = (back + TILE) // KCH

    row = lax.broadcasted_iota(jnp.int32, (2 * page_len, 2 * page_len), 0)
    col = lax.broadcasted_iota(jnp.int32, (2 * page_len, 2 * page_len), 1)
    src = jnp.where(row < page_len, 2 * row, 2 * row - (2 * page_len - 1))
    choose = (col == src).astype(F32).astype(BF)

    def unpack(slot):
        pages = [raw_ref[pos_ref[slot + i]] for i in range(BLK)]
        both = jnp.dot(
            choose, jnp.concatenate(pages, axis=1), preferred_element_type=F32
        ).astype(BF)
        for i in range(BLK):
            kc[slot + i] = both[:page_len, i * width : (i + 1) * width]
            vc[slot + i] = both[page_len:, i * width : (i + 1) * width]

    for slot in range(0, n_req * n_page, BLK):
        unpack(slot)

    knp[:back, :] = jnp.zeros((back, width), BF)
    vnp[:back, :] = jnp.zeros((back, width), BF)
    knp[back:, :] = kn_ref[...]
    vnp[back:, :] = vn_ref[...]

    lane = lax.broadcasted_iota(jnp.int32, (1, width), 1)
    lane_f = lax.broadcasted_iota(jnp.int32, (1, KCH), 1).astype(F32)
    delta = [bias_ref[0, group * per + a] - bias_ref[1, group * per + a] for a in range(per)]
    parts = [slice(a * TILE, (a + 1) * TILE) for a in range(per)]
    n_all = n_page + n_new

    for t in range(rows // TILE):
        qt = q_ref[t * TILE : (t + 1) * TILE, :].astype(F32)
        for a in range(per):
            mine = (lane >= a * HD) & (lane < (a + 1) * HD)
            qbd[t, parts[a], :] = jnp.where(mine, qt, 0.0).astype(BF)

    def list_pairs(r, carry):
        start, found = carry
        end = start + lens_ref[0, r]

        def add(t, found):
            pairs[0, found] = t
            pairs[1, found] = r
            pairs[2, found] = start
            return found + 1

        return end, lax.fori_loop(start // TILE, (end - 1) // TILE + 1, add, found)

    _, found = lax.fori_loop(0, n_req, list_pairs, (jnp.int32(0), jnp.int32(0)))

    def one_pair(i, sbuf, wbuf):
        t, r, start = pairs[0, i], pairs[1, i], pairs[2, i]
        row0 = pl.multiple_of(t * TILE, TILE)
        live = counts_ref[0, r]
        end = start + lens_ref[0, r]
        offset = (live * page_len - start).astype(F32)
        start_f = start.astype(F32)
        row = (row0 + lax.broadcasted_iota(jnp.int32, (TILE, KCH), 0)).astype(F32)
        var_first = jnp.floor((row + offset + 0.5) * (1.0 / VARLEN)) * VARLEN

        def scores(keys):
            return lax.dot_general(
                qbd[t], keys, (((1,), (1,)), ((), ())), preferred_element_type=F32
            )

        first = r * n_page
        s_page = scores(kc[pl.ds(first, n_page)].reshape(n_page * page_len, width))
        s_new = scores(knp[pl.ds(row0, back + TILE), :])
        top = [None] * per
        for c in range(n_all):
            if c < n_page:
                dead = jnp.where(c < live, 0.0, NEG)
                same = var_first <= lane_f + c * page_len
            else:
                key_row = lane_f + (row0 - back + (c - n_page) * KCH).astype(F32)
                allowed = (key_row >= start_f) & (key_row <= row)
                same = var_first - offset <= key_row
            for a, p in enumerate(parts):
                if c < n_page:
                    v = s_page[p, c * KCH : (c + 1) * KCH]
                    v = v + jnp.where(same, delta[a] + dead, dead)
                else:
                    v = s_new[p, (c - n_page) * KCH : (c - n_page + 1) * KCH]
                    v = jnp.where(allowed, v + jnp.where(same, delta[a], 0.0), NEG)
                sbuf[c, p, :] = v
                top[a] = v if top[a] is None else jnp.maximum(top[a], v)
        peak = [jnp.broadcast_to(jnp.max(x, axis=1, keepdims=True), (TILE, KCH)) for x in top]
        total = [jnp.zeros((TILE, KCH), F32) for _ in parts]
        for c in range(n_all):
            for a, p in enumerate(parts):
                e = jnp.exp(sbuf[c, p, :] - peak[a])
                sbuf[c, p, :] = e
                total[a] = total[a] + e
        inverse = [
            jnp.broadcast_to(1.0 / jnp.sum(x, axis=1, keepdims=True), (TILE, KCH)) for x in total
        ]
        for c in range(n_all):
            for a, p in enumerate(parts):
                wbuf[p, c * KCH : (c + 1) * KCH] = (sbuf[c, p, :] * inverse[a]).astype(BF)
        o = jnp.dot(
            wbuf[:, : n_page * KCH],
            vc[pl.ds(first, n_page)].reshape(n_page * page_len, width),
            preferred_element_type=F32,
        ) + jnp.dot(
            wbuf[:, n_page * KCH :], vnp[pl.ds(row0, back + TILE), :],
            preferred_element_type=F32,
        )
        mixed = o[parts[0]]
        for a in range(1, per):
            mixed = jnp.where(lane >= a * HD, o[parts[a]], mixed)
        inside = (row >= start_f) & (row < end.astype(F32))
        obuf[t] = jnp.where(inside[:, :width], mixed, obuf[t])

    def pair_body(i, carry):
        one_pair(2 * i, sbuf.at[0], wbuf.at[0])
        one_pair(jnp.minimum(2 * i + 1, found - 1), sbuf.at[1], wbuf.at[1])
        return carry

    lax.fori_loop(0, (found + 1) // 2, pair_body, 0)
    per_chunk = rows // n_chunk
    for t in range(rows // TILE):
        if n_chunk == 1:
            out_refs[0][t * TILE : (t + 1) * TILE, :] = obuf[t].astype(BF)
            continue
        sub = TILE // n_chunk
        for c in range(n_chunk):
            part = obuf[t, c * sub : (c + 1) * sub, :].astype(BF)
            if len(out_refs) == 1:
                base = c * per_chunk + t * sub
                out_refs[0][base : base + sub, :] = part
            else:
                out_refs[c][t * sub : (t + 1) * sub, :] = part


def attend(group, lanes, most, n_chunk, apart, lens, counts, pos, bias, q, kn, vn, raw):
    rows = q.shape[0]
    per = lanes // HD
    page_len = raw.shape[1] // 2
    slots = raw.shape[0]
    back = -(-most // KCH) * KCH
    n_all = PAGES_REQ + (back + TILE) // KCH
    n_out = n_chunk if apart else 1
    tiles = rows // TILE
    smem = pl.BlockSpec(memory_space=pltpu.SMEM)
    part = pl.BlockSpec((rows, lanes), lambda i: (0, group))
    return pl.pallas_call(
        functools.partial(attend_kernel, group, per, n_chunk),
        grid=(1,),
        out_shape=[jax.ShapeDtypeStruct((rows // n_out, lanes), BF)] * n_out,
        in_specs=[smem] * 4
        + [part] * 3
        + [pl.BlockSpec(raw.shape, lambda i: (0, 0, 0), pipeline_mode=pl.Buffered(1))],
        out_specs=[pl.BlockSpec((rows // n_out, lanes), lambda i: (0, 0))] * n_out,
        scratch_shapes=[
            pltpu.VMEM((slots, page_len, lanes), BF),
            pltpu.VMEM((slots, page_len, lanes), BF),
            pltpu.VMEM((back + rows, lanes), BF),
            pltpu.VMEM((back + rows, lanes), BF),
            pltpu.VMEM((tiles, per * TILE, lanes), BF),
            pltpu.SMEM((3, tiles + lens.shape[1]), jnp.int32),
            pltpu.VMEM((2, n_all, per * TILE, KCH), F32),
            pltpu.VMEM((2, per * TILE, n_all * KCH), BF),
            pltpu.VMEM((tiles, TILE, lanes), F32),
        ],
        compiler_params=pltpu.CompilerParams(vmem_limit_bytes=60 << 20),
        cost_estimate=LIGHT,
        name="attend",
    )(lens, counts, pos, bias, q, kn, vn, raw)


def shift(value, axis, n, k):
    return lax.ppermute(value, axis, [(i, (i + k) % n) for i in range(n)])


def whole_weight(own, halves, dp, n_dp, n_group):
    twins = lax.ppermute(jnp.stack(halves), "dp", [(i, i ^ 1) for i in range(n_dp)])
    first = dp % 2 == 0
    lower = [jnp.where(first, h, twins[k]) for k, h in enumerate(halves)]
    upper = [jnp.where(first, twins[k], h) for k, h in enumerate(halves)]
    if n_group == 2:
        own_parts = jnp.split(own, 2)
        return [
            jnp.concatenate([mine] + part, axis=0)
            for mine, part in zip(own_parts, (lower, upper))
        ]
    both = [x for pair in zip(lower, upper) for x in pair]
    whole = jnp.concatenate([own] + both, axis=0)
    width, d_model = own.shape
    parts = whole.reshape(len(halves) + 1, n_group, width // n_group, d_model)
    return [parts[:, a].reshape(-1, d_model) for a in range(n_group)]


def per_device(
    tokens,
    attn_gain,
    ffn_gain,
    w_qkv,
    w_out,
    w_gateup,
    w_down,
    variate_bias,
    adapter_down,
    adapter_up,
    owner_table,
    lengths,
    adapter_ids,
    page_counts,
    page_table,
    cache_pool,
):
    n_tp = lax.axis_size("tensor")
    n_dp = lax.axis_size("dp")
    tp = lax.axis_index("tensor")
    dp = lax.axis_index("dp")
    me = dp.astype(jnp.int32).reshape(1)
    tp_id = tp.astype(jnp.int32).reshape(1)
    row_count, d_model = tokens.shape
    tok_total = row_count * n_tp
    width = w_out.shape[0]
    page_len = cache_pool.shape[1]
    pool_dev = cache_pool.shape[0]
    cap = max(1, page_table.shape[1] // n_dp)
    far_first = [k for k in range(1, n_tp)]
    lanes = min(width, 2 * HD)
    n_group = width // lanes
    slots = n_dp * cap
    dd = d_model // n_tp
    n_loc, _, rank, _ = adapter_down.shape
    n_chunk = max(1, row_count // CHUNK)
    sub = row_count // n_chunk
    span = 2 * rank

    toks = [tokens] + [shift(tokens, "tensor", n_tp, k) for k in far_first]

    down_part = lax.dynamic_slice_in_dim(adapter_down, tp * dd, dd, 3).reshape(n_loc * span, dd)
    names = jnp.concatenate([page_table // pool_dev, page_table % pool_dev], axis=0).astype(BF)
    names = jnp.pad(names, ((0, 14), (0, dd - names.shape[1])))
    payload = jnp.concatenate([down_part, adapter_up.reshape(n_loc * span, width), names], axis=0)
    gathered = lax.all_gather(payload, "dp", axis=0)
    asked = gathered[:, 2 * n_loc * span : 2 * n_loc * span + 2, : page_table.shape[1]]
    picked = pick(me, asked.astype(jnp.int32), cache_pool, n_dp, cap, lanes)
    send = lax.optimization_barrier((picked[0], toks[1:-1]))[0]
    fetched = [lax.all_to_all(send, "dp", split_axis=0, concat_axis=0, tiled=True)]

    own_half = lax.dynamic_slice_in_dim(w_out, (dp % 2) * (width // 2), width // 2, 0)
    gathered, lengths_b = lax.optimization_barrier((gathered, lengths, send))[:2]
    down_named, up_named = named(owner_table, adapter_ids, gathered, n_loc, span)
    downs = [down_named] + [shift(down_named, "tensor", n_tp, k) for k in far_first]

    _, position = token_layout(lengths_b[0], page_counts[0], page_len, tok_total)
    index = jnp.arange(2 * HD, dtype=jnp.int32)
    frequency = 10000.0 ** (-2.0 * (index % (HD // 2)).astype(F32) / HD)
    angles = (position % VARLEN).astype(F32)[:, None] * frequency[None, :]
    sign = jnp.where(index % HD < HD // 2, -1.0, 1.0).astype(F32)
    query, new_keys, new_values, buffer_pos, *all_tokens = project(
        tp_id, lengths, page_table, attn_gain.reshape(1, d_model), w_qkv, up_named,
        jnp.cos(angles), jnp.sin(angles) * sign[None, :], toks, downs, n_dp, cap, pool_dev, n_chunk,
    )
    own_half = lax.optimization_barrier((own_half, downs[1:]))[0]
    halves = [shift(own_half, "tensor", n_tp, k) for k in far_first]
    for a in range(1, n_group):
        send = lax.optimization_barrier((picked[a], fetched[-1], query, halves[:1]))[0]
        fetched.append(lax.all_to_all(send, "dp", split_axis=0, concat_axis=0, tiled=True))
    fetched = [f.reshape(slots, 2 * page_len, lanes) for f in fetched]


    def mixed(blocks, a):
        return jnp.dot(
            jnp.concatenate(blocks, axis=1), w_whole[a], preferred_element_type=F32
        )

    def attended(a, q, apart):
        return attend(
            a, lanes, 2 * TILE, n_chunk, apart, lengths, page_counts, buffer_pos, variate_bias,
            q, new_keys, new_values, fetched[a],
        )

    early = []
    w_whole = None
    for a in range(n_group - 1):
        mix = attended(a, query, False)[0]
        if w_whole is None:
            mix, halves = lax.optimization_barrier((mix, halves))
            w_whole = whole_weight(w_out, halves, dp, n_dp, n_group)
        blocks = [mix] + [shift(mix, "tensor", n_tp, k) for k in far_first]
        query, w_whole = lax.optimization_barrier((query, w_whole))
        early.append(blocks)
    if w_whole is None:
        w_whole = whole_weight(w_out, halves, dp, n_dp, n_group)
    last = attended(n_group - 1, query, False)[0]
    early, last, w_whole = lax.optimization_barrier((early, last, w_whole))
    last = [last] + [shift(last, "tensor", n_tp, k) for k in far_first]
    outs = []
    pieces = None
    base = jnp.concatenate(all_tokens, axis=0).reshape(tok_total, d_model).astype(F32)
    for a in range(n_group - 1):
        base = base + mixed(early[a], a)
    last = lax.optimization_barrier((last, base))[0]
    everything = base + mixed(last, n_group - 1)
    for c in range(n_chunk):
        residual = everything[c * n_tp * sub : (c + 1) * n_tp * sub]
        if pieces is not None:
            residual = lax.optimization_barrier((residual, pieces))[0]
        ffn_in = normalize(residual, ffn_gain).astype(BF)
        gate_up = jnp.einsum("td,kdf->ktf", ffn_in, w_gateup, preferred_element_type=F32)
        hidden = (jax.nn.silu(gate_up[0]) * gate_up[1]).astype(BF)
        down = jnp.dot(hidden, w_down, preferred_element_type=F32).reshape(n_tp, sub, d_model)
        total = lax.dynamic_index_in_dim(down, tp, 0, False)
        total = total + lax.dynamic_index_in_dim(
            residual.reshape(n_tp, sub, d_model), tp, 0, False
        )
        down = down.astype(BF)
        pieces = [lax.dynamic_index_in_dim(down, (tp + k) % n_tp, 0, False) for k in far_first]
        for k, piece in zip(far_first, pieces):
            total = total + shift(piece, "tensor", n_tp, k).astype(F32)
        outs.append(total.astype(BF))
    return jnp.concatenate(outs, axis=0)


def solution(mesh):
    return jax.shard_map(
        per_device,
        mesh=mesh,
        in_specs=(
            P(("dp", "tensor"), None),
            P(),
            P(),
            P(None, None, "tensor"),
            P("tensor", None),
            P(None, None, "tensor"),
            P("tensor", None),
            P(None, "tensor"),
            P("dp", None, None, None),
            P("dp", None, None, "tensor"),
            P(),
            P("dp", None),
            P("dp", None),
            P("dp", None),
            P("dp", None),
            P("dp", None, None, "tensor"),
        ),
        out_specs=P(("dp", "tensor"), None),
        check_vma=False,
    )
```

```python
import functools

import jax
import jax.numpy as jnp
from jax import lax
from jax.experimental import pallas as pl
from jax.experimental.pallas import tpu as pltpu
from jax.sharding import PartitionSpec as P

HD = 64
PAGES_REQ = 8
VARLEN = 160
TILE = 128
KCH = 128
BLK = 4
CHUNK = 64
BF = jnp.bfloat16
F32 = jnp.float32
NEG = -1e30
LIGHT = pl.CostEstimate(flops=1000, bytes_accessed=1000, transcendentals=0)


def normalize(values, gain):
    values = values.astype(F32)
    inv_scale = lax.rsqrt(jnp.mean(values * values, axis=-1, keepdims=True) + 1e-05)
    return values * inv_scale * gain.astype(F32)


def token_layout(req_lens, live_counts, page_len, tok_total):
    end_pos = jnp.cumsum(req_lens, dtype=jnp.int32)
    starts = end_pos - req_lens
    tok_index = jnp.arange(tok_total, dtype=jnp.int32)
    request = jnp.sum(
        (tok_index[:, None] >= end_pos[None, :]).astype(jnp.int32), axis=1, dtype=jnp.int32
    )
    onehot = request[:, None] == jnp.arange(req_lens.shape[0], dtype=jnp.int32)[None, :]
    first_pos = jnp.sum(jnp.where(onehot, starts[None, :], 0), axis=1, dtype=jnp.int32)
    cached = jnp.sum(jnp.where(onehot, live_counts[None, :], 0), axis=1, dtype=jnp.int32)
    return (onehot, cached * page_len + tok_index - first_pos)


def pick_kernel(n_dp, cap, me_ref, asked_ref, pool_ref, *rest):
    n_out = len(rest) - 3
    outs, (buf, sem_in, sem_out) = rest[:n_out], rest[n_out:]
    lanes = outs[0].shape[-1]
    me = me_ref[0]
    slots = asked_ref.shape[2]

    def find(g, carry):
        count = jnp.int32(0)
        for p in range(slots):
            hit = asked_ref[g, 0, p] == me

            @pl.when(hit)
            def _():
                pltpu.make_async_copy(
                    pool_ref.at[asked_ref[g, 1, p]], buf.at[g, count], sem_in.at[g]
                ).start()

            count = count + hit.astype(jnp.int32)
        return carry

    lax.fori_loop(0, n_dp, find, 0)
    done = []
    for g in range(n_dp):
        pltpu.make_async_copy(pool_ref.at[pl.ds(0, cap)], buf.at[g], sem_in.at[g]).wait()
        for a in range(n_out):
            copy = pltpu.make_async_copy(
                buf.at[g, :, :, :, pl.ds(a * lanes, lanes)], outs[a].at[g], sem_out.at[a, g]
            )
            copy.start()
            done.append(copy)
    for copy in done:
        copy.wait()


def pick(me, asked, pool, n_dp, cap, lanes):
    smem = pl.BlockSpec(memory_space=pltpu.SMEM)
    hbm = pl.BlockSpec(memory_space=pl.ANY)
    n_out = pool.shape[-1] // lanes
    shape = (n_dp, cap) + pool.shape[1:-1]
    return pl.pallas_call(
        functools.partial(pick_kernel, n_dp, cap),
        out_shape=[jax.ShapeDtypeStruct(shape + (lanes,), pool.dtype)] * n_out,
        in_specs=[smem, smem, hbm],
        out_specs=[hbm] * n_out,
        scratch_shapes=[
            pltpu.VMEM(shape + pool.shape[-1:], pool.dtype),
            pltpu.SemaphoreType.DMA((n_dp,)),
            pltpu.SemaphoreType.DMA((n_out, n_dp)),
        ],
        cost_estimate=LIGHT,
        name="pick_pages",
    )(me, asked, pool)


def named_kernel(n_loc, span, table_ref, ids_ref, all_ref, down_out, up_out, down_ref, up_ref, sem):
    copies = []
    for r in range(ids_ref.shape[1]):
        slot = table_ref[ids_ref[0, r]]
        home, inner = slot // n_loc, slot % n_loc
        for half, out in ((0, down_ref), (1, up_ref)):
            base = pl.multiple_of((half * n_loc + inner) * span, span)
            copy = pltpu.make_async_copy(
                all_ref.at[home, pl.ds(base, span)], out.at[pl.ds(r * span, span)], sem.at[r, half]
            )
            copy.start()
            copies.append(copy)
    for copy in copies:
        copy.wait()
    last = [
        pltpu.make_async_copy(down_ref, down_out, sem.at[0, 0]),
        pltpu.make_async_copy(up_ref, up_out, sem.at[0, 1]),
    ]
    for copy in last:
        copy.start()
    for copy in last:
        copy.wait()


def named(owner_table, adapter_ids, gathered, n_loc, span):
    n_req = adapter_ids.shape[1]
    smem = pl.BlockSpec(memory_space=pltpu.SMEM)
    hbm = pl.BlockSpec(memory_space=pltpu.HBM)
    out = jax.ShapeDtypeStruct((n_req * span, gathered.shape[-1]), BF)
    return pl.pallas_call(
        functools.partial(named_kernel, n_loc, span),
        out_shape=(out, out),
        in_specs=[smem, smem, hbm],
        out_specs=(hbm, hbm),
        scratch_shapes=[
            pltpu.VMEM(out.shape, BF),
            pltpu.VMEM(out.shape, BF),
            pltpu.SemaphoreType.DMA((n_req, 2)),
        ],
        cost_estimate=LIGHT,
        name="named_adapters",
    )(owner_table, adapter_ids, gathered)


def project_kernel(n_tp, cap, pool_dev, n_chunk, tp_ref, lens_ref, table_ref, *rest):
    hbm_refs, rest = rest[: 5 + 2 * n_tp], rest[5 + 2 * n_tp :]
    q_ref, k_ref, v_ref, pos_ref = rest[:4]
    all_refs = rest[4 : 4 + n_chunk]
    down, count, *held = rest[4 + n_chunk :]
    held, sem, sem_out = held[:-2], held[-2], held[-1]
    gain_ref, w_ref, up_ref, cos_ref, sin_ref, tok_ref = held
    tp = tp_ref[0]
    copies = []
    targets = list(held[:5]) + [tok_ref.at[k] for k in range(n_tp)]
    for k in range(n_tp):
        targets.append(down.at[lax.rem(tp - k + n_tp, n_tp)])
    for i in list(range(5, 5 + 2 * n_tp)) + list(range(5)):
        copy = pltpu.make_async_copy(hbm_refs[i], targets[i], sem.at[i])
        copy.start()
        copies.append(copy)
    _, rows, _ = tok_ref.shape
    width = q_ref.shape[1]
    n_low, dd = down.shape[1:]
    n_req = lens_ref.shape[1]
    rank = n_low // n_req // 2

    for g in range(count.shape[0]):
        count[g] = 0

    def place(p, carry):
        home = table_ref[0, p] // pool_dev
        seen = count[home]
        count[home] = seen + 1
        pos_ref[p] = home * cap + seen
        return carry

    lax.fori_loop(0, table_ref.shape[1], place, 0)

    for copy in copies:
        copy.wait()
    sub = all_refs[0].shape[1]
    stores = []
    for k in range(n_tp):
        for c in range(n_chunk):
            copy = pltpu.make_async_copy(
                tok_ref.at[k, pl.ds(c * sub, sub)],
                all_refs[c].at[lax.rem(tp - k + n_tp, n_tp)],
                sem_out.at[k, c],
            )
            copy.start()
            stores.append(copy)
    lane = lax.broadcasted_iota(jnp.int32, (1, 128), 1)
    first = jnp.bitwise_and(lane, HD - 1) < HD // 2

    def rope(u, cos, sin):
        parts = []
        for a in range(width // 128):
            part = u[:, a * 128 : (a + 1) * 128]
            other = jnp.where(
                first, pltpu.roll(part, 128 - HD // 2, 1), pltpu.roll(part, HD // 2, 1)
            )
            parts.append(part * cos + other * sin)
        return parts

    for k in range(n_tp):
        row0 = pl.multiple_of(lax.rem(tp - k + n_tp, n_tp) * rows, rows)
        x = tok_ref[k].astype(F32)
        inv = lax.rsqrt(jnp.mean(x * x, axis=1, keepdims=True) + 1e-05)
        normed = (x * inv * gain_ref[...].astype(F32)).astype(BF)
        low = jnp.zeros((rows, n_low), F32)
        for j in range(n_tp):
            low = low + lax.dot_general(
                normed[:, j * dd : (j + 1) * dd], down[j], (((1,), (1,)), ((), ())),
                preferred_element_type=F32,
            )
        row = row0 + lax.broadcasted_iota(jnp.int32, (rows, n_low), 0)
        col = lax.broadcasted_iota(jnp.int32, (rows, n_low), 1)
        request = jnp.zeros((rows, n_low), jnp.int32)
        end = jnp.int32(0)
        for r in range(n_req - 1):
            end = end + lens_ref[0, r]
            request = request + (row >= end).astype(jnp.int32)
        own = col // (2 * rank) == request
        kind = (col // rank) % 2
        deltas = []
        for kk in range(2):
            part = jnp.where(own & (kind == kk), low, 0.0).astype(BF)
            deltas.append(jnp.dot(part, up_ref[...], preferred_element_type=F32))
        cos = cos_ref[pl.ds(row0, rows), :]
        sin = sin_ref[pl.ds(row0, rows), :]
        q = jnp.dot(normed, w_ref[0], preferred_element_type=F32) + deltas[0]
        for a, part in enumerate(rope(q, cos, sin)):
            part = part.astype(BF).astype(F32) * (HD ** -0.5)
            q_ref[pl.ds(row0, rows), a * 128 : (a + 1) * 128] = part.astype(BF)
        kk = jnp.dot(normed, w_ref[1], preferred_element_type=F32)
        for a, part in enumerate(rope(kk, cos, sin)):
            k_ref[pl.ds(row0, rows), a * 128 : (a + 1) * 128] = part.astype(BF)
        v = jnp.dot(normed, w_ref[2], preferred_element_type=F32) + deltas[1]
        v_ref[pl.ds(row0, rows), :] = v.astype(BF)
    for copy in stores:
        copy.wait()


def project(
    tp, lens, table, gain, w_qkv, up, cos, sin, toks, downs, n_dp, cap, pool_dev, n_chunk
):
    n_tp = len(toks)
    sub = toks[0].shape[0] // n_chunk
    rows = toks[0].shape[0] * n_tp
    width = w_qkv.shape[2]
    smem = pl.BlockSpec(memory_space=pltpu.SMEM)
    vmem = pl.BlockSpec(memory_space=pltpu.VMEM)
    out = jax.ShapeDtypeStruct((rows, width), BF)
    return pl.pallas_call(
        functools.partial(project_kernel, n_tp, cap, pool_dev, n_chunk),
        out_shape=(
            out, out, out, jax.ShapeDtypeStruct((table.shape[1],), jnp.int32),
        )
        + (jax.ShapeDtypeStruct((n_tp, sub, toks[0].shape[1]), BF),) * n_chunk,
        in_specs=[smem] * 3 + [pl.BlockSpec(memory_space=pltpu.HBM)] * (5 + 2 * n_tp),
        out_specs=(vmem, vmem, vmem, smem) + (pl.BlockSpec(memory_space=pltpu.HBM),) * n_chunk,
        scratch_shapes=[
            pltpu.VMEM((n_tp,) + downs[0].shape, BF),
            pltpu.SMEM((n_dp,), jnp.int32),
        ]
        + [pltpu.VMEM(x.shape, x.dtype) for x in (gain, w_qkv, up, cos, sin)]
        + [
            pltpu.VMEM((n_tp,) + toks[0].shape, BF),
            pltpu.SemaphoreType.DMA((5 + 2 * n_tp,)),
            pltpu.SemaphoreType.DMA((n_tp, n_chunk)),
        ],
        compiler_params=pltpu.CompilerParams(vmem_limit_bytes=60 << 20),
        cost_estimate=LIGHT,
        name="project",
    )(tp, lens, table, gain, w_qkv, up, cos, sin, *toks, *downs)


def attend_kernel(
    group, per, n_chunk, lens_ref, counts_ref, pos_ref, bias_ref,
    q_ref, kn_ref, vn_ref, raw_ref, *rest
):
    out_refs = rest[:-9]
    kc, vc, knp, vnp, qbd, pairs, sbuf, wbuf, obuf = rest[-9:]
    page_len = kc.shape[1]
    width = q_ref.shape[1]
    rows = q_ref.shape[0]
    n_req = lens_ref.shape[1]
    back = knp.shape[0] - rows
    n_page = PAGES_REQ
    n_new = (back + TILE) // KCH

    row = lax.broadcasted_iota(jnp.int32, (2 * page_len, 2 * page_len), 0)
    col = lax.broadcasted_iota(jnp.int32, (2 * page_len, 2 * page_len), 1)
    src = jnp.where(row < page_len, 2 * row, 2 * row - (2 * page_len - 1))
    choose = (col == src).astype(F32).astype(BF)

    def unpack(slot):
        pages = [raw_ref[pos_ref[slot + i]] for i in range(BLK)]
        both = jnp.dot(
            choose, jnp.concatenate(pages, axis=1), preferred_element_type=F32
        ).astype(BF)
        for i in range(BLK):
            kc[slot + i] = both[:page_len, i * width : (i + 1) * width]
            vc[slot + i] = both[page_len:, i * width : (i + 1) * width]

    for slot in range(0, n_req * n_page, BLK):
        unpack(slot)

    knp[:back, :] = jnp.zeros((back, width), BF)
    vnp[:back, :] = jnp.zeros((back, width), BF)
    knp[back:, :] = kn_ref[...]
    vnp[back:, :] = vn_ref[...]

    lane = lax.broadcasted_iota(jnp.int32, (1, width), 1)
    lane_f = lax.broadcasted_iota(jnp.int32, (1, KCH), 1).astype(F32)
    delta = [bias_ref[0, group * per + a] - bias_ref[1, group * per + a] for a in range(per)]
    parts = [slice(a * TILE, (a + 1) * TILE) for a in range(per)]
    n_all = n_page + n_new

    for t in range(rows // TILE):
        qt = q_ref[t * TILE : (t + 1) * TILE, :].astype(F32)
        for a in range(per):
            mine = (lane >= a * HD) & (lane < (a + 1) * HD)
            qbd[t, parts[a], :] = jnp.where(mine, qt, 0.0).astype(BF)

    def list_pairs(r, carry):
        start, found = carry
        end = start + lens_ref[0, r]

        def add(t, found):
            pairs[0, found] = t
            pairs[1, found] = r
            pairs[2, found] = start
            return found + 1

        return end, lax.fori_loop(start // TILE, (end - 1) // TILE + 1, add, found)

    _, found = lax.fori_loop(0, n_req, list_pairs, (jnp.int32(0), jnp.int32(0)))

    def pair_body(i, carry):
        t, r, start = pairs[0, i], pairs[1, i], pairs[2, i]
        row0 = pl.multiple_of(t * TILE, TILE)
        live = counts_ref[0, r]
        end = start + lens_ref[0, r]
        offset = (live * page_len - start).astype(F32)
        start_f = start.astype(F32)
        row = (row0 + lax.broadcasted_iota(jnp.int32, (TILE, KCH), 0)).astype(F32)
        var_first = jnp.floor((row + offset + 0.5) * (1.0 / VARLEN)) * VARLEN

        def scores(keys):
            return lax.dot_general(
                qbd[t], keys, (((1,), (1,)), ((), ())), preferred_element_type=F32
            )

        first = r * n_page
        s_page = scores(kc[pl.ds(first, n_page)].reshape(n_page * page_len, width))
        s_new = scores(knp[pl.ds(row0, back + TILE), :])
        top = [None] * per
        for c in range(n_all):
            if c < n_page:
                dead = jnp.where(c < live, 0.0, NEG)
                same = var_first <= lane_f + c * page_len
            else:
                key_row = lane_f + (row0 - back + (c - n_page) * KCH).astype(F32)
                allowed = (key_row >= start_f) & (key_row <= row)
                same = var_first - offset <= key_row
            for a, p in enumerate(parts):
                if c < n_page:
                    v = s_page[p, c * KCH : (c + 1) * KCH]
                    v = v + jnp.where(same, delta[a] + dead, dead)
                else:
                    v = s_new[p, (c - n_page) * KCH : (c - n_page + 1) * KCH]
                    v = jnp.where(allowed, v + jnp.where(same, delta[a], 0.0), NEG)
                sbuf[c, p, :] = v
                top[a] = v if top[a] is None else jnp.maximum(top[a], v)
        peak = [jnp.broadcast_to(jnp.max(x, axis=1, keepdims=True), (TILE, KCH)) for x in top]
        total = [jnp.zeros((TILE, KCH), F32) for _ in parts]
        for c in range(n_all):
            for a, p in enumerate(parts):
                e = jnp.exp(sbuf[c, p, :] - peak[a])
                sbuf[c, p, :] = e
                total[a] = total[a] + e
        inverse = [
            jnp.broadcast_to(1.0 / jnp.sum(x, axis=1, keepdims=True), (TILE, KCH)) for x in total
        ]
        for c in range(n_all):
            for a, p in enumerate(parts):
                wbuf[p, c * KCH : (c + 1) * KCH] = (sbuf[c, p, :] * inverse[a]).astype(BF)
        o = jnp.dot(
            wbuf[:, : n_page * KCH],
            vc[pl.ds(first, n_page)].reshape(n_page * page_len, width),
            preferred_element_type=F32,
        ) + jnp.dot(
            wbuf[:, n_page * KCH :], vnp[pl.ds(row0, back + TILE), :],
            preferred_element_type=F32,
        )
        mixed = o[parts[0]]
        for a in range(1, per):
            mixed = jnp.where(lane >= a * HD, o[parts[a]], mixed)
        inside = (row >= start_f) & (row < end.astype(F32))
        obuf[t] = jnp.where(inside[:, :width], mixed, obuf[t])
        return carry

    lax.fori_loop(0, found, pair_body, 0)
    per_chunk = rows // n_chunk
    for t in range(rows // TILE):
        if n_chunk == 1:
            out_refs[0][t * TILE : (t + 1) * TILE, :] = obuf[t].astype(BF)
            continue
        sub = TILE // n_chunk
        for c in range(n_chunk):
            part = obuf[t, c * sub : (c + 1) * sub, :].astype(BF)
            if len(out_refs) == 1:
                base = c * per_chunk + t * sub
                out_refs[0][base : base + sub, :] = part
            else:
                out_refs[c][t * sub : (t + 1) * sub, :] = part


def attend(group, lanes, most, n_chunk, apart, lens, counts, pos, bias, q, kn, vn, raw):
    rows = q.shape[0]
    per = lanes // HD
    page_len = raw.shape[1] // 2
    slots = raw.shape[0]
    back = -(-most // KCH) * KCH
    n_all = PAGES_REQ + (back + TILE) // KCH
    n_out = n_chunk if apart else 1
    tiles = rows // TILE
    smem = pl.BlockSpec(memory_space=pltpu.SMEM)
    part = pl.BlockSpec((rows, lanes), lambda i: (0, group))
    return pl.pallas_call(
        functools.partial(attend_kernel, group, per, n_chunk),
        grid=(1,),
        out_shape=[jax.ShapeDtypeStruct((rows // n_out, lanes), BF)] * n_out,
        in_specs=[smem] * 4
        + [part] * 3
        + [pl.BlockSpec(raw.shape, lambda i: (0, 0, 0), pipeline_mode=pl.Buffered(1))],
        out_specs=[pl.BlockSpec((rows // n_out, lanes), lambda i: (0, 0))] * n_out,
        scratch_shapes=[
            pltpu.VMEM((slots, page_len, lanes), BF),
            pltpu.VMEM((slots, page_len, lanes), BF),
            pltpu.VMEM((back + rows, lanes), BF),
            pltpu.VMEM((back + rows, lanes), BF),
            pltpu.VMEM((tiles, per * TILE, lanes), BF),
            pltpu.SMEM((3, tiles + lens.shape[1]), jnp.int32),
            pltpu.VMEM((n_all, per * TILE, KCH), F32),
            pltpu.VMEM((per * TILE, n_all * KCH), BF),
            pltpu.VMEM((tiles, TILE, lanes), F32),
        ],
        compiler_params=pltpu.CompilerParams(vmem_limit_bytes=60 << 20),
        cost_estimate=LIGHT,
        name="attend",
    )(lens, counts, pos, bias, q, kn, vn, raw)


def partial_kernel(n_chunk, n_block, *refs):
    toks, refs = refs[:n_chunk], refs[n_chunk:]
    blocks, refs = refs[:n_block], refs[n_block:]
    w_ref, outs = refs[0], refs[1:]
    rows = outs[0].shape[0]
    for c in range(n_chunk):
        part = jnp.concatenate([b[c * rows : (c + 1) * rows, :] for b in blocks], axis=1)
        outs[c][...] = toks[c][...].astype(F32) + jnp.dot(
            part, w_ref[...], preferred_element_type=F32
        )


def partial(toks, blocks, weight):
    n_chunk = len(toks)
    vmem = pl.BlockSpec(memory_space=pltpu.VMEM)
    out = jax.ShapeDtypeStruct(toks[0].shape, F32)
    return pl.pallas_call(
        functools.partial(partial_kernel, n_chunk, len(blocks)),
        out_shape=[out] * n_chunk,
        in_specs=[vmem] * (n_chunk + len(blocks) + 1),
        out_specs=[vmem] * n_chunk,
        compiler_params=pltpu.CompilerParams(vmem_limit_bytes=24 << 20),
        cost_estimate=LIGHT,
        name="partial",
    )(*toks, *blocks, weight)


def shift(value, axis, n, k):
    return lax.ppermute(value, axis, [(i, (i + k) % n) for i in range(n)])


def whole_weight(own, halves, dp, n_dp, n_group):
    twins = lax.ppermute(jnp.stack(halves), "dp", [(i, i ^ 1) for i in range(n_dp)])
    first = dp % 2 == 0
    lower = [jnp.where(first, h, twins[k]) for k, h in enumerate(halves)]
    upper = [jnp.where(first, twins[k], h) for k, h in enumerate(halves)]
    if n_group == 2:
        own_parts = jnp.split(own, 2)
        return [
            jnp.concatenate([mine] + part, axis=0)
            for mine, part in zip(own_parts, (lower, upper))
        ]
    both = [x for pair in zip(lower, upper) for x in pair]
    whole = jnp.concatenate([own] + both, axis=0)
    width, d_model = own.shape
    parts = whole.reshape(len(halves) + 1, n_group, width // n_group, d_model)
    return [parts[:, a].reshape(-1, d_model) for a in range(n_group)]


def per_device(
    tokens,
    attn_gain,
    ffn_gain,
    w_qkv,
    w_out,
    w_gateup,
    w_down,
    variate_bias,
    adapter_down,
    adapter_up,
    owner_table,
    lengths,
    adapter_ids,
    page_counts,
    page_table,
    cache_pool,
):
    n_tp = lax.axis_size("tensor")
    n_dp = lax.axis_size("dp")
    tp = lax.axis_index("tensor")
    dp = lax.axis_index("dp")
    me = dp.astype(jnp.int32).reshape(1)
    tp_id = tp.astype(jnp.int32).reshape(1)
    row_count, d_model = tokens.shape
    tok_total = row_count * n_tp
    width = w_out.shape[0]
    page_len = cache_pool.shape[1]
    pool_dev = cache_pool.shape[0]
    cap = max(1, page_table.shape[1] // n_dp)
    far_first = [k for k in range(1, n_tp)]
    lanes = min(width, 2 * HD)
    n_group = width // lanes
    slots = n_dp * cap
    dd = d_model // n_tp
    n_loc, _, rank, _ = adapter_down.shape
    n_chunk = max(1, row_count // CHUNK)
    sub = row_count // n_chunk
    span = 2 * rank

    toks = [tokens] + [shift(tokens, "tensor", n_tp, k) for k in far_first]

    down_part = lax.dynamic_slice_in_dim(adapter_down, tp * dd, dd, 3).reshape(n_loc * span, dd)
    names = jnp.concatenate([page_table // pool_dev, page_table % pool_dev], axis=0).astype(BF)
    names = jnp.pad(names, ((0, 14), (0, dd - names.shape[1])))
    payload = jnp.concatenate([down_part, adapter_up.reshape(n_loc * span, width), names], axis=0)
    gathered = lax.all_gather(payload, "dp", axis=0)
    asked = gathered[:, 2 * n_loc * span : 2 * n_loc * span + 2, : page_table.shape[1]]
    picked = pick(me, asked.astype(jnp.int32), cache_pool, n_dp, cap, lanes)
    send = lax.optimization_barrier((picked[0], toks[1:-1]))[0]
    fetched = [lax.all_to_all(send, "dp", split_axis=0, concat_axis=0, tiled=True)]

    own_half = lax.dynamic_slice_in_dim(w_out, (dp % 2) * (width // 2), width // 2, 0)
    gathered, lengths_b = lax.optimization_barrier((gathered, lengths, send))[:2]
    down_named, up_named = named(owner_table, adapter_ids, gathered, n_loc, span)
    downs = [down_named] + [shift(down_named, "tensor", n_tp, k) for k in far_first]

    _, position = token_layout(lengths_b[0], page_counts[0], page_len, tok_total)
    index = jnp.arange(2 * HD, dtype=jnp.int32)
    frequency = 10000.0 ** (-2.0 * (index % (HD // 2)).astype(F32) / HD)
    angles = (position % VARLEN).astype(F32)[:, None] * frequency[None, :]
    sign = jnp.where(index % HD < HD // 2, -1.0, 1.0).astype(F32)
    query, new_keys, new_values, buffer_pos, *all_tokens = project(
        tp_id, lengths, page_table, attn_gain.reshape(1, d_model), w_qkv, up_named,
        jnp.cos(angles), jnp.sin(angles) * sign[None, :], toks, downs, n_dp, cap, pool_dev, n_chunk,
    )
    own_half = lax.optimization_barrier((own_half, downs[1:]))[0]
    halves = [shift(own_half, "tensor", n_tp, k) for k in far_first]
    for a in range(1, n_group):
        send = lax.optimization_barrier((picked[a], fetched[-1], query, halves[:1]))[0]
        fetched.append(lax.all_to_all(send, "dp", split_axis=0, concat_axis=0, tiled=True))
    fetched = [f.reshape(slots, 2 * page_len, lanes) for f in fetched]


    def mixed(blocks, a):
        return jnp.dot(
            jnp.concatenate(blocks, axis=1), w_whole[a], preferred_element_type=F32
        )

    def attended(a, q, apart):
        return attend(
            a, lanes, 2 * TILE, n_chunk, apart, lengths, page_counts, buffer_pos, variate_bias,
            q, new_keys, new_values, fetched[a],
        )

    early = []
    w_whole = None
    for a in range(n_group - 1):
        mix = attended(a, query, False)[0]
        if w_whole is None:
            mix, halves = lax.optimization_barrier((mix, halves))
            w_whole = whole_weight(w_out, halves, dp, n_dp, n_group)
        blocks = [mix] + [shift(mix, "tensor", n_tp, k) for k in far_first]
        query, w_whole = lax.optimization_barrier((query, w_whole))
        early.append(blocks)
    if w_whole is None:
        w_whole = whole_weight(w_out, halves, dp, n_dp, n_group)
    last = attended(n_group - 1, query, True)
    early, last, w_whole = lax.optimization_barrier((early, last, w_whole))
    bases = [tok.reshape(n_tp * sub, d_model) for tok in all_tokens]
    for a in range(n_group - 1):
        bases = partial(bases, early[a], w_whole[a])
    outs = []
    pieces = None
    late = []
    for c in range(n_chunk):
        own = last[c]
        if late:
            own = lax.optimization_barrier((own, bases))[0]
        late.append([own] + [shift(own, "tensor", n_tp, k) for k in far_first])
    for c in range(n_chunk):
        blocks = late[c]
        if pieces is not None:
            blocks = lax.optimization_barrier((blocks, pieces))[0]
        residual = bases[c].astype(F32) + mixed(blocks, n_group - 1)
        ffn_in = normalize(residual, ffn_gain).astype(BF)
        gate_up = jnp.einsum("td,kdf->ktf", ffn_in, w_gateup, preferred_element_type=F32)
        hidden = (jax.nn.silu(gate_up[0]) * gate_up[1]).astype(BF)
        down = jnp.dot(hidden, w_down, preferred_element_type=F32).reshape(n_tp, sub, d_model)
        total = lax.dynamic_index_in_dim(down, tp, 0, False)
        total = total + lax.dynamic_index_in_dim(
            residual.reshape(n_tp, sub, d_model), tp, 0, False
        )
        down = down.astype(BF)
        pieces = [lax.dynamic_index_in_dim(down, (tp + k) % n_tp, 0, False) for k in far_first]
        for k, piece in zip(far_first, pieces):
            total = total + shift(piece, "tensor", n_tp, k).astype(F32)
        outs.append(total.astype(BF))
    return jnp.concatenate(outs, axis=0)


def solution(mesh):
    return jax.shard_map(
        per_device,
        mesh=mesh,
        in_specs=(
            P(("dp", "tensor"), None),
            P(),
            P(),
            P(None, None, "tensor"),
            P("tensor", None),
            P(None, None, "tensor"),
            P("tensor", None),
            P(None, "tensor"),
            P("dp", None, None, None),
            P("dp", None, None, "tensor"),
            P(),
            P("dp", None),
            P("dp", None),
            P("dp", None),
            P("dp", None),
            P("dp", None, None, "tensor"),
        ),
        out_specs=P(("dp", "tensor"), None),
        check_vma=False,
    )
```

```python
import functools

import jax
import jax.numpy as jnp
from jax import lax
from jax.experimental import pallas as pl
from jax.experimental.pallas import tpu as pltpu
from jax.sharding import PartitionSpec as P

HD = 64
PAGES_REQ = 8
VARLEN = 160
TILE = 128
KCH = 128
BLK = 4
CHUNK = 64
BF = jnp.bfloat16
F32 = jnp.float32
NEG = -1e30
COPY = pl.CostEstimate(flops=1000, bytes_accessed=8 << 20, transcendentals=0)
LIGHT = pl.CostEstimate(flops=1000, bytes_accessed=1000, transcendentals=0)


def normalize(values, gain):
    values = values.astype(F32)
    inv_scale = lax.rsqrt(jnp.mean(values * values, axis=-1, keepdims=True) + 1e-05)
    return values * inv_scale * gain.astype(F32)


def token_layout(req_lens, live_counts, page_len, tok_total):
    end_pos = jnp.cumsum(req_lens, dtype=jnp.int32)
    starts = end_pos - req_lens
    tok_index = jnp.arange(tok_total, dtype=jnp.int32)
    request = jnp.sum(
        (tok_index[:, None] >= end_pos[None, :]).astype(jnp.int32), axis=1, dtype=jnp.int32
    )
    onehot = request[:, None] == jnp.arange(req_lens.shape[0], dtype=jnp.int32)[None, :]
    first_pos = jnp.sum(jnp.where(onehot, starts[None, :], 0), axis=1, dtype=jnp.int32)
    cached = jnp.sum(jnp.where(onehot, live_counts[None, :], 0), axis=1, dtype=jnp.int32)
    return (onehot, cached * page_len + tok_index - first_pos)


def pick_kernel(n_dp, cap, group, me_ref, asked_ref, pool_ref, out, buf, sem_in, sem_out):
    part = pl.ds(group * out.shape[-1], out.shape[-1])
    me = me_ref[0]
    slots = asked_ref.shape[2]

    def find(g, carry):
        count = jnp.int32(0)
        for p in range(slots):
            hit = asked_ref[g, 0, p] == me

            @pl.when(hit)
            def _():
                pltpu.make_async_copy(
                    pool_ref.at[asked_ref[g, 1, p], :, :, part], buf.at[g, count], sem_in.at[g]
                ).start()

            count = count + hit.astype(jnp.int32)
        return carry

    lax.fori_loop(0, n_dp, find, 0)
    done = []
    for g in range(n_dp):
        pltpu.make_async_copy(
            pool_ref.at[pl.ds(0, cap), :, :, part], buf.at[g], sem_in.at[g]
        ).wait()
        copy = pltpu.make_async_copy(buf.at[g], out.at[g], sem_out.at[g])
        copy.start()
        done.append(copy)
    for copy in done:
        copy.wait()


def pick(group, me, asked, pool, n_dp, cap, lanes):
    smem = pl.BlockSpec(memory_space=pltpu.SMEM)
    hbm = pl.BlockSpec(memory_space=pl.ANY)
    shape = (n_dp, cap) + pool.shape[1:-1] + (lanes,)
    return pl.pallas_call(
        functools.partial(pick_kernel, n_dp, cap, group),
        out_shape=jax.ShapeDtypeStruct(shape, pool.dtype),
        in_specs=[smem, smem, hbm],
        out_specs=hbm,
        scratch_shapes=[
            pltpu.VMEM(shape, pool.dtype),
            pltpu.SemaphoreType.DMA((n_dp,)),
            pltpu.SemaphoreType.DMA((n_dp,)),
        ],
        cost_estimate=LIGHT if group == 0 else COPY,
        name="pick_pages",
    )(me, asked, pool)


def named_kernel(n_loc, span, table_ref, ids_ref, all_ref, down_out, up_out, down_ref, up_ref, sem):
    copies = []
    for r in range(ids_ref.shape[1]):
        slot = table_ref[ids_ref[0, r]]
        home, inner = slot // n_loc, slot % n_loc
        for half, out in ((0, down_ref), (1, up_ref)):
            base = pl.multiple_of((half * n_loc + inner) * span, span)
            copy = pltpu.make_async_copy(
                all_ref.at[home, pl.ds(base, span)], out.at[pl.ds(r * span, span)], sem.at[r, half]
            )
            copy.start()
            copies.append(copy)
    for copy in copies:
        copy.wait()
    last = [
        pltpu.make_async_copy(down_ref, down_out, sem.at[0, 0]),
        pltpu.make_async_copy(up_ref, up_out, sem.at[0, 1]),
    ]
    for copy in last:
        copy.start()
    for copy in last:
        copy.wait()


def named(owner_table, adapter_ids, gathered, n_loc, span):
    n_req = adapter_ids.shape[1]
    smem = pl.BlockSpec(memory_space=pltpu.SMEM)
    hbm = pl.BlockSpec(memory_space=pltpu.HBM)
    out = jax.ShapeDtypeStruct((n_req * span, gathered.shape[-1]), BF)
    return pl.pallas_call(
        functools.partial(named_kernel, n_loc, span),
        out_shape=(out, out),
        in_specs=[smem, smem, hbm],
        out_specs=(hbm, hbm),
        scratch_shapes=[
            pltpu.VMEM(out.shape, BF),
            pltpu.VMEM(out.shape, BF),
            pltpu.SemaphoreType.DMA((n_req, 2)),
        ],
        cost_estimate=LIGHT,
        name="named_adapters",
    )(owner_table, adapter_ids, gathered)


def project_kernel(n_tp, cap, pool_dev, n_chunk, tp_ref, lens_ref, table_ref, *rest):
    hbm_refs, rest = rest[: 5 + 2 * n_tp], rest[5 + 2 * n_tp :]
    q_ref, k_ref, v_ref, pos_ref = rest[:4]
    all_refs = rest[4 : 4 + n_chunk]
    down, count, *held = rest[4 + n_chunk :]
    held, sem, sem_out = held[:-2], held[-2], held[-1]
    gain_ref, w_ref, up_ref, cos_ref, sin_ref, tok_ref = held
    tp = tp_ref[0]
    copies = []
    targets = list(held[:5]) + [tok_ref.at[k] for k in range(n_tp)]
    for k in range(n_tp):
        targets.append(down.at[lax.rem(tp - k + n_tp, n_tp)])
    for i in list(range(5, 5 + 2 * n_tp)) + list(range(5)):
        copy = pltpu.make_async_copy(hbm_refs[i], targets[i], sem.at[i])
        copy.start()
        copies.append(copy)
    _, rows, _ = tok_ref.shape
    width = q_ref.shape[1]
    n_low, dd = down.shape[1:]
    n_req = lens_ref.shape[1]
    rank = n_low // n_req // 2

    for g in range(count.shape[0]):
        count[g] = 0

    def place(p, carry):
        home = table_ref[0, p] // pool_dev
        seen = count[home]
        count[home] = seen + 1
        pos_ref[p] = home * cap + seen
        return carry

    lax.fori_loop(0, table_ref.shape[1], place, 0)

    for copy in copies:
        copy.wait()
    sub = all_refs[0].shape[1]
    stores = []
    for k in range(n_tp):
        for c in range(n_chunk):
            copy = pltpu.make_async_copy(
                tok_ref.at[k, pl.ds(c * sub, sub)],
                all_refs[c].at[lax.rem(tp - k + n_tp, n_tp)],
                sem_out.at[k, c],
            )
            copy.start()
            stores.append(copy)
    lane = lax.broadcasted_iota(jnp.int32, (1, 128), 1)
    first = jnp.bitwise_and(lane, HD - 1) < HD // 2

    def rope(u, cos, sin):
        parts = []
        for a in range(width // 128):
            part = u[:, a * 128 : (a + 1) * 128]
            other = jnp.where(
                first, pltpu.roll(part, 128 - HD // 2, 1), pltpu.roll(part, HD // 2, 1)
            )
            parts.append(part * cos + other * sin)
        return parts

    for k in range(n_tp):
        row0 = pl.multiple_of(lax.rem(tp - k + n_tp, n_tp) * rows, rows)
        x = tok_ref[k].astype(F32)
        inv = lax.rsqrt(jnp.mean(x * x, axis=1, keepdims=True) + 1e-05)
        normed = (x * inv * gain_ref[...].astype(F32)).astype(BF)
        low = jnp.zeros((rows, n_low), F32)
        for j in range(n_tp):
            low = low + lax.dot_general(
                normed[:, j * dd : (j + 1) * dd], down[j], (((1,), (1,)), ((), ())),
                preferred_element_type=F32,
            )
        row = row0 + lax.broadcasted_iota(jnp.int32, (rows, n_low), 0)
        col = lax.broadcasted_iota(jnp.int32, (rows, n_low), 1)
        request = jnp.zeros((rows, n_low), jnp.int32)
        end = jnp.int32(0)
        for r in range(n_req - 1):
            end = end + lens_ref[0, r]
            request = request + (row >= end).astype(jnp.int32)
        own = col // (2 * rank) == request
        kind = (col // rank) % 2
        deltas = []
        for kk in range(2):
            part = jnp.where(own & (kind == kk), low, 0.0).astype(BF)
            deltas.append(jnp.dot(part, up_ref[...], preferred_element_type=F32))
        cos = cos_ref[pl.ds(row0, rows), :]
        sin = sin_ref[pl.ds(row0, rows), :]
        q = jnp.dot(normed, w_ref[0], preferred_element_type=F32) + deltas[0]
        for a, part in enumerate(rope(q, cos, sin)):
            part = part.astype(BF).astype(F32) * (HD ** -0.5)
            q_ref[pl.ds(row0, rows), a * 128 : (a + 1) * 128] = part.astype(BF)
        kk = jnp.dot(normed, w_ref[1], preferred_element_type=F32)
        for a, part in enumerate(rope(kk, cos, sin)):
            k_ref[pl.ds(row0, rows), a * 128 : (a + 1) * 128] = part.astype(BF)
        v = jnp.dot(normed, w_ref[2], preferred_element_type=F32) + deltas[1]
        v_ref[pl.ds(row0, rows), :] = v.astype(BF)
    for copy in stores:
        copy.wait()


def project(
    tp, lens, table, gain, w_qkv, up, cos, sin, toks, downs, n_dp, cap, pool_dev, n_chunk
):
    n_tp = len(toks)
    sub = toks[0].shape[0] // n_chunk
    rows = toks[0].shape[0] * n_tp
    width = w_qkv.shape[2]
    smem = pl.BlockSpec(memory_space=pltpu.SMEM)
    vmem = pl.BlockSpec(memory_space=pltpu.VMEM)
    out = jax.ShapeDtypeStruct((rows, width), BF)
    return pl.pallas_call(
        functools.partial(project_kernel, n_tp, cap, pool_dev, n_chunk),
        out_shape=(
            out, out, out, jax.ShapeDtypeStruct((table.shape[1],), jnp.int32),
        )
        + (jax.ShapeDtypeStruct((n_tp, sub, toks[0].shape[1]), BF),) * n_chunk,
        in_specs=[smem] * 3 + [pl.BlockSpec(memory_space=pltpu.HBM)] * (5 + 2 * n_tp),
        out_specs=(vmem, vmem, vmem, smem) + (pl.BlockSpec(memory_space=pltpu.HBM),) * n_chunk,
        scratch_shapes=[
            pltpu.VMEM((n_tp,) + downs[0].shape, BF),
            pltpu.SMEM((n_dp,), jnp.int32),
        ]
        + [pltpu.VMEM(x.shape, x.dtype) for x in (gain, w_qkv, up, cos, sin)]
        + [
            pltpu.VMEM((n_tp,) + toks[0].shape, BF),
            pltpu.SemaphoreType.DMA((5 + 2 * n_tp,)),
            pltpu.SemaphoreType.DMA((n_tp, n_chunk)),
        ],
        compiler_params=pltpu.CompilerParams(vmem_limit_bytes=60 << 20),
        cost_estimate=LIGHT,
        name="project",
    )(tp, lens, table, gain, w_qkv, up, cos, sin, *toks, *downs)


def attend_kernel(
    group, per, n_chunk, lens_ref, counts_ref, pos_ref, bias_ref,
    q_ref, kn_ref, vn_ref, raw_ref, *rest
):
    out_refs = rest[:-9]
    kc, vc, knp, vnp, qbd, pairs, sbuf, wbuf, obuf = rest[-9:]
    page_len = kc.shape[1]
    width = q_ref.shape[1]
    rows = q_ref.shape[0]
    n_req = lens_ref.shape[1]
    back = knp.shape[0] - rows
    n_page = PAGES_REQ
    n_new = (back + TILE) // KCH

    row = lax.broadcasted_iota(jnp.int32, (2 * page_len, 2 * page_len), 0)
    col = lax.broadcasted_iota(jnp.int32, (2 * page_len, 2 * page_len), 1)
    src = jnp.where(row < page_len, 2 * row, 2 * row - (2 * page_len - 1))
    choose = (col == src).astype(F32).astype(BF)

    def unpack(slot):
        pages = [raw_ref[pos_ref[slot + i]] for i in range(BLK)]
        both = jnp.dot(
            choose, jnp.concatenate(pages, axis=1), preferred_element_type=F32
        ).astype(BF)
        for i in range(BLK):
            kc[slot + i] = both[:page_len, i * width : (i + 1) * width]
            vc[slot + i] = both[page_len:, i * width : (i + 1) * width]

    for slot in range(0, n_req * n_page, BLK):
        unpack(slot)

    knp[:back, :] = jnp.zeros((back, width), BF)
    vnp[:back, :] = jnp.zeros((back, width), BF)
    knp[back:, :] = kn_ref[...]
    vnp[back:, :] = vn_ref[...]

    lane = lax.broadcasted_iota(jnp.int32, (1, width), 1)
    lane_f = lax.broadcasted_iota(jnp.int32, (1, KCH), 1).astype(F32)
    delta = [bias_ref[0, group * per + a] - bias_ref[1, group * per + a] for a in range(per)]
    parts = [slice(a * TILE, (a + 1) * TILE) for a in range(per)]
    n_all = n_page + n_new

    for t in range(rows // TILE):
        qt = q_ref[t * TILE : (t + 1) * TILE, :].astype(F32)
        for a in range(per):
            mine = (lane >= a * HD) & (lane < (a + 1) * HD)
            qbd[t, parts[a], :] = jnp.where(mine, qt, 0.0).astype(BF)

    def list_pairs(r, carry):
        start, found = carry
        end = start + lens_ref[0, r]

        def add(t, found):
            pairs[0, found] = t
            pairs[1, found] = r
            pairs[2, found] = start
            return found + 1

        return end, lax.fori_loop(start // TILE, (end - 1) // TILE + 1, add, found)

    _, found = lax.fori_loop(0, n_req, list_pairs, (jnp.int32(0), jnp.int32(0)))

    def pair_body(i, carry):
        t, r, start = pairs[0, i], pairs[1, i], pairs[2, i]
        row0 = pl.multiple_of(t * TILE, TILE)
        live = counts_ref[0, r]
        end = start + lens_ref[0, r]
        offset = (live * page_len - start).astype(F32)
        start_f = start.astype(F32)
        row = (row0 + lax.broadcasted_iota(jnp.int32, (TILE, KCH), 0)).astype(F32)
        var_first = jnp.floor((row + offset + 0.5) * (1.0 / VARLEN)) * VARLEN

        def scores(keys):
            return lax.dot_general(
                qbd[t], keys, (((1,), (1,)), ((), ())), preferred_element_type=F32
            )

        first = r * n_page
        s_page = scores(kc[pl.ds(first, n_page)].reshape(n_page * page_len, width))
        s_new = scores(knp[pl.ds(row0, back + TILE), :])
        top = [None] * per
        for c in range(n_all):
            if c < n_page:
                dead = jnp.where(c < live, 0.0, NEG)
                same = var_first <= lane_f + c * page_len
            else:
                key_row = lane_f + (row0 - back + (c - n_page) * KCH).astype(F32)
                allowed = (key_row >= start_f) & (key_row <= row)
                same = var_first - offset <= key_row
            for a, p in enumerate(parts):
                if c < n_page:
                    v = s_page[p, c * KCH : (c + 1) * KCH]
                    v = v + jnp.where(same, delta[a] + dead, dead)
                else:
                    v = s_new[p, (c - n_page) * KCH : (c - n_page + 1) * KCH]
                    v = jnp.where(allowed, v + jnp.where(same, delta[a], 0.0), NEG)
                sbuf[c, p, :] = v
                top[a] = v if top[a] is None else jnp.maximum(top[a], v)
        peak = [jnp.broadcast_to(jnp.max(x, axis=1, keepdims=True), (TILE, KCH)) for x in top]
        total = [jnp.zeros((TILE, KCH), F32) for _ in parts]
        for c in range(n_all):
            for a, p in enumerate(parts):
                e = jnp.exp(sbuf[c, p, :] - peak[a])
                sbuf[c, p, :] = e
                total[a] = total[a] + e
        inverse = [
            jnp.broadcast_to(1.0 / jnp.sum(x, axis=1, keepdims=True), (TILE, KCH)) for x in total
        ]
        for c in range(n_all):
            for a, p in enumerate(parts):
                wbuf[p, c * KCH : (c + 1) * KCH] = (sbuf[c, p, :] * inverse[a]).astype(BF)
        o = jnp.dot(
            wbuf[:, : n_page * KCH],
            vc[pl.ds(first, n_page)].reshape(n_page * page_len, width),
            preferred_element_type=F32,
        ) + jnp.dot(
            wbuf[:, n_page * KCH :], vnp[pl.ds(row0, back + TILE), :],
            preferred_element_type=F32,
        )
        mixed = o[parts[0]]
        for a in range(1, per):
            mixed = jnp.where(lane >= a * HD, o[parts[a]], mixed)
        inside = (row >= start_f) & (row < end.astype(F32))
        obuf[t] = jnp.where(inside[:, :width], mixed, obuf[t])
        return carry

    lax.fori_loop(0, found, pair_body, 0)
    per_chunk = rows // n_chunk
    for t in range(rows // TILE):
        if n_chunk == 1:
            out_refs[0][t * TILE : (t + 1) * TILE, :] = obuf[t].astype(BF)
            continue
        sub = TILE // n_chunk
        for c in range(n_chunk):
            part = obuf[t, c * sub : (c + 1) * sub, :].astype(BF)
            if len(out_refs) == 1:
                base = c * per_chunk + t * sub
                out_refs[0][base : base + sub, :] = part
            else:
                out_refs[c][t * sub : (t + 1) * sub, :] = part


def attend(group, lanes, most, n_chunk, apart, lens, counts, pos, bias, q, kn, vn, raw):
    rows = q.shape[0]
    per = lanes // HD
    page_len = raw.shape[1] // 2
    slots = raw.shape[0]
    back = -(-most // KCH) * KCH
    n_all = PAGES_REQ + (back + TILE) // KCH
    n_out = n_chunk if apart else 1
    tiles = rows // TILE
    smem = pl.BlockSpec(memory_space=pltpu.SMEM)
    part = pl.BlockSpec((rows, lanes), lambda i: (0, group))
    return pl.pallas_call(
        functools.partial(attend_kernel, group, per, n_chunk),
        grid=(1,),
        out_shape=[jax.ShapeDtypeStruct((rows // n_out, lanes), BF)] * n_out,
        in_specs=[smem] * 4
        + [part] * 3
        + [pl.BlockSpec(raw.shape, lambda i: (0, 0, 0), pipeline_mode=pl.Buffered(1))],
        out_specs=[pl.BlockSpec((rows // n_out, lanes), lambda i: (0, 0))] * n_out,
        scratch_shapes=[
            pltpu.VMEM((slots, page_len, lanes), BF),
            pltpu.VMEM((slots, page_len, lanes), BF),
            pltpu.VMEM((back + rows, lanes), BF),
            pltpu.VMEM((back + rows, lanes), BF),
            pltpu.VMEM((tiles, per * TILE, lanes), BF),
            pltpu.SMEM((3, tiles + lens.shape[1]), jnp.int32),
            pltpu.VMEM((n_all, per * TILE, KCH), F32),
            pltpu.VMEM((per * TILE, n_all * KCH), BF),
            pltpu.VMEM((tiles, TILE, lanes), F32),
        ],
        compiler_params=pltpu.CompilerParams(vmem_limit_bytes=60 << 20),
        cost_estimate=LIGHT,
        name="attend",
    )(lens, counts, pos, bias, q, kn, vn, raw)


def partial_kernel(n_chunk, n_block, *refs):
    blocks, refs = refs[:n_block], refs[n_block:]
    w_ref, outs = refs[0], refs[1:]
    rows = outs[0].shape[0]
    for c in range(n_chunk):
        part = jnp.concatenate([b[c * rows : (c + 1) * rows, :] for b in blocks], axis=1)
        outs[c][...] = jnp.dot(part, w_ref[...], preferred_element_type=F32)


def partial(n_chunk, blocks, weight):
    vmem = pl.BlockSpec(memory_space=pltpu.VMEM)
    out = jax.ShapeDtypeStruct((blocks[0].shape[0] // n_chunk, weight.shape[1]), F32)
    return pl.pallas_call(
        functools.partial(partial_kernel, n_chunk, len(blocks)),
        out_shape=[out] * n_chunk,
        in_specs=[vmem] * (len(blocks) + 1),
        out_specs=[vmem] * n_chunk,
        compiler_params=pltpu.CompilerParams(vmem_limit_bytes=24 << 20),
        cost_estimate=LIGHT,
        name="partial",
    )(*blocks, weight)


def shift(value, axis, n, k):
    return lax.ppermute(value, axis, [(i, (i + k) % n) for i in range(n)])


def whole_weight(own, halves, dp, n_dp, n_group):
    twins = lax.ppermute(jnp.stack(halves), "dp", [(i, i ^ 1) for i in range(n_dp)])
    first = dp % 2 == 0
    lower = [jnp.where(first, h, twins[k]) for k, h in enumerate(halves)]
    upper = [jnp.where(first, twins[k], h) for k, h in enumerate(halves)]
    if n_group == 2:
        own_parts = jnp.split(own, 2)
        return [
            jnp.concatenate([mine] + part, axis=0)
            for mine, part in zip(own_parts, (lower, upper))
        ]
    both = [x for pair in zip(lower, upper) for x in pair]
    whole = jnp.concatenate([own] + both, axis=0)
    width, d_model = own.shape
    parts = whole.reshape(len(halves) + 1, n_group, width // n_group, d_model)
    return [parts[:, a].reshape(-1, d_model) for a in range(n_group)]


def per_device(
    tokens,
    attn_gain,
    ffn_gain,
    w_qkv,
    w_out,
    w_gateup,
    w_down,
    variate_bias,
    adapter_down,
    adapter_up,
    owner_table,
    lengths,
    adapter_ids,
    page_counts,
    page_table,
    cache_pool,
):
    n_tp = lax.axis_size("tensor")
    n_dp = lax.axis_size("dp")
    tp = lax.axis_index("tensor")
    dp = lax.axis_index("dp")
    me = dp.astype(jnp.int32).reshape(1)
    tp_id = tp.astype(jnp.int32).reshape(1)
    row_count, d_model = tokens.shape
    tok_total = row_count * n_tp
    width = w_out.shape[0]
    page_len = cache_pool.shape[1]
    pool_dev = cache_pool.shape[0]
    cap = max(1, page_table.shape[1] // n_dp)
    far_first = [k for k in range(1, n_tp)]
    lanes = min(width, 2 * HD)
    n_group = width // lanes
    slots = n_dp * cap
    dd = d_model // n_tp
    n_loc, _, rank, _ = adapter_down.shape
    n_chunk = max(1, row_count // CHUNK)
    sub = row_count // n_chunk
    span = 2 * rank

    toks = [tokens] + [shift(tokens, "tensor", n_tp, k) for k in far_first]

    down_part = lax.dynamic_slice_in_dim(adapter_down, tp * dd, dd, 3).reshape(n_loc * span, dd)
    names = jnp.concatenate([page_table // pool_dev, page_table % pool_dev], axis=0).astype(BF)
    names = jnp.pad(names, ((0, 14), (0, dd - names.shape[1])))
    payload = jnp.concatenate([down_part, adapter_up.reshape(n_loc * span, width), names], axis=0)
    gathered = lax.all_gather(payload, "dp", axis=0)
    asked = gathered[:, 2 * n_loc * span : 2 * n_loc * span + 2, : page_table.shape[1]]
    asked = asked.astype(jnp.int32)
    send = pick(0, me, asked, cache_pool, n_dp, cap, lanes)
    send = lax.optimization_barrier((send, toks[1:-1]))[0]
    fetched = [lax.all_to_all(send, "dp", split_axis=0, concat_axis=0, tiled=True)]

    own_half = lax.dynamic_slice_in_dim(w_out, (dp % 2) * (width // 2), width // 2, 0)
    gathered, lengths_b = lax.optimization_barrier((gathered, lengths, send))[:2]
    down_named, up_named = named(owner_table, adapter_ids, gathered, n_loc, span)
    later = lax.optimization_barrier((asked, down_named))[0]
    downs = [down_named] + [shift(down_named, "tensor", n_tp, k) for k in far_first]

    _, position = token_layout(lengths_b[0], page_counts[0], page_len, tok_total)
    index = jnp.arange(2 * HD, dtype=jnp.int32)
    frequency = 10000.0 ** (-2.0 * (index % (HD // 2)).astype(F32) / HD)
    angles = (position % VARLEN).astype(F32)[:, None] * frequency[None, :]
    sign = jnp.where(index % HD < HD // 2, -1.0, 1.0).astype(F32)
    query, new_keys, new_values, buffer_pos, *all_tokens = project(
        tp_id, lengths, page_table, attn_gain.reshape(1, d_model), w_qkv, up_named,
        jnp.cos(angles), jnp.sin(angles) * sign[None, :], toks, downs, n_dp, cap, pool_dev, n_chunk,
    )
    own_half = lax.optimization_barrier((own_half, downs[1:]))[0]
    halves = [shift(own_half, "tensor", n_tp, k) for k in far_first]
    for a in range(1, n_group):
        send = pick(a, me, later, cache_pool, n_dp, cap, lanes)
        send = lax.optimization_barrier((send, fetched[-1], query, halves[:1]))[0]
        fetched.append(lax.all_to_all(send, "dp", split_axis=0, concat_axis=0, tiled=True))
    fetched = [f.reshape(slots, 2 * page_len, lanes) for f in fetched]


    def mixed(blocks, a):
        return jnp.dot(
            jnp.concatenate(blocks, axis=1), w_whole[a], preferred_element_type=F32
        )

    def attended(a, q, apart):
        return attend(
            a, lanes, 2 * TILE, n_chunk, apart, lengths, page_counts, buffer_pos, variate_bias,
            q, new_keys, new_values, fetched[a],
        )

    early = []
    w_whole = None
    for a in range(n_group - 1):
        mix = attended(a, query, False)[0]
        if w_whole is None:
            mix, halves = lax.optimization_barrier((mix, halves))
            w_whole = whole_weight(w_out, halves, dp, n_dp, n_group)
        blocks = [mix] + [shift(mix, "tensor", n_tp, k) for k in far_first]
        query, w_whole = lax.optimization_barrier((query, w_whole))
        early.append(blocks)
    if w_whole is None:
        w_whole = whole_weight(w_out, halves, dp, n_dp, n_group)
    last = attended(n_group - 1, query, True)
    early, last, w_whole = lax.optimization_barrier((early, last, w_whole))
    bases = [partial(n_chunk, early[a], w_whole[a]) for a in range(n_group - 1)]
    outs = []
    pieces = None
    late = []
    for c in range(n_chunk):
        own = last[c]
        if late:
            own = lax.optimization_barrier((own, bases))[0]
        late.append([own] + [shift(own, "tensor", n_tp, k) for k in far_first])
    for c in range(n_chunk):
        blocks = late[c]
        if pieces is not None:
            blocks = lax.optimization_barrier((blocks, pieces))[0]
        residual = all_tokens[c].reshape(n_tp * sub, d_model).astype(F32)
        for part in bases:
            residual = residual + part[c]
        residual = residual + mixed(blocks, n_group - 1)
        ffn_in = normalize(residual, ffn_gain).astype(BF)
        gate_up = jnp.einsum("td,kdf->ktf", ffn_in, w_gateup, preferred_element_type=F32)
        hidden = (jax.nn.silu(gate_up[0]) * gate_up[1]).astype(BF)
        down = jnp.dot(hidden, w_down, preferred_element_type=F32).reshape(n_tp, sub, d_model)
        total = lax.dynamic_index_in_dim(down, tp, 0, False)
        total = total + lax.dynamic_index_in_dim(
            residual.reshape(n_tp, sub, d_model), tp, 0, False
        )
        down = down.astype(BF)
        pieces = [lax.dynamic_index_in_dim(down, (tp + k) % n_tp, 0, False) for k in far_first]
        for k, piece in zip(far_first, pieces):
            total = total + shift(piece, "tensor", n_tp, k).astype(F32)
        outs.append(total.astype(BF))
    return jnp.concatenate(outs, axis=0)


def solution(mesh):
    return jax.shard_map(
        per_device,
        mesh=mesh,
        in_specs=(
            P(("dp", "tensor"), None),
            P(),
            P(),
            P(None, None, "tensor"),
            P("tensor", None),
            P(None, None, "tensor"),
            P("tensor", None),
            P(None, "tensor"),
            P("dp", None, None, None),
            P("dp", None, None, "tensor"),
            P(),
            P("dp", None),
            P("dp", None),
            P("dp", None),
            P("dp", None),
            P("dp", None, None, "tensor"),
        ),
        out_specs=P(("dp", "tensor"), None),
        check_vma=False,
    )
```

```python
import functools

import jax
import jax.numpy as jnp
from jax import lax
from jax.experimental import pallas as pl
from jax.experimental.pallas import tpu as pltpu
from jax.sharding import PartitionSpec as P

HD = 64
PAGES_REQ = 8
VARLEN = 160
TILE = 128
KCH = 128
BLK = 4
CHUNK = 64
BF = jnp.bfloat16
F32 = jnp.float32
NEG = -1e30
LIGHT = pl.CostEstimate(flops=1000, bytes_accessed=1000, transcendentals=0)


def normalize(values, gain):
    values = values.astype(F32)
    inv_scale = lax.rsqrt(jnp.mean(values * values, axis=-1, keepdims=True) + 1e-05)
    return values * inv_scale * gain.astype(F32)


def token_layout(req_lens, live_counts, page_len, tok_total):
    end_pos = jnp.cumsum(req_lens, dtype=jnp.int32)
    starts = end_pos - req_lens
    tok_index = jnp.arange(tok_total, dtype=jnp.int32)
    request = jnp.sum(
        (tok_index[:, None] >= end_pos[None, :]).astype(jnp.int32), axis=1, dtype=jnp.int32
    )
    onehot = request[:, None] == jnp.arange(req_lens.shape[0], dtype=jnp.int32)[None, :]
    first_pos = jnp.sum(jnp.where(onehot, starts[None, :], 0), axis=1, dtype=jnp.int32)
    cached = jnp.sum(jnp.where(onehot, live_counts[None, :], 0), axis=1, dtype=jnp.int32)
    return (onehot, cached * page_len + tok_index - first_pos)


def pick_kernel(n_dp, cap, me_ref, asked_ref, pool_ref, *rest):
    n_out = len(rest) - 3
    outs, (buf, sem_in, sem_out) = rest[:n_out], rest[n_out:]
    lanes = outs[0].shape[-1]
    me = me_ref[0]
    slots = asked_ref.shape[2]

    def find(g, carry):
        count = jnp.int32(0)
        for p in range(slots):
            hit = asked_ref[g, 0, p] == me

            @pl.when(hit)
            def _():
                pltpu.make_async_copy(
                    pool_ref.at[asked_ref[g, 1, p]], buf.at[g, count], sem_in.at[g]
                ).start()

            count = count + hit.astype(jnp.int32)
        return carry

    lax.fori_loop(0, n_dp, find, 0)
    done = []
    for g in range(n_dp):
        pltpu.make_async_copy(pool_ref.at[pl.ds(0, cap)], buf.at[g], sem_in.at[g]).wait()
        for a in range(n_out):
            copy = pltpu.make_async_copy(
                buf.at[g, :, :, :, pl.ds(a * lanes, lanes)], outs[a].at[g], sem_out.at[a, g]
            )
            copy.start()
            done.append(copy)
    for copy in done:
        copy.wait()


def pick(me, asked, pool, n_dp, cap, lanes):
    smem = pl.BlockSpec(memory_space=pltpu.SMEM)
    hbm = pl.BlockSpec(memory_space=pl.ANY)
    n_out = pool.shape[-1] // lanes
    shape = (n_dp, cap) + pool.shape[1:-1]
    return pl.pallas_call(
        functools.partial(pick_kernel, n_dp, cap),
        out_shape=[jax.ShapeDtypeStruct(shape + (lanes,), pool.dtype)] * n_out,
        in_specs=[smem, smem, hbm],
        out_specs=[hbm] * n_out,
        scratch_shapes=[
            pltpu.VMEM(shape + pool.shape[-1:], pool.dtype),
            pltpu.SemaphoreType.DMA((n_dp,)),
            pltpu.SemaphoreType.DMA((n_out, n_dp)),
        ],
        cost_estimate=LIGHT,
        name="pick_pages",
    )(me, asked, pool)


def named_kernel(n_loc, span, table_ref, ids_ref, all_ref, down_out, up_out, down_ref, up_ref, sem):
    copies = []
    for r in range(ids_ref.shape[1]):
        slot = table_ref[ids_ref[0, r]]
        home, inner = slot // n_loc, slot % n_loc
        for half, out in ((0, down_ref), (1, up_ref)):
            base = pl.multiple_of((half * n_loc + inner) * span, span)
            copy = pltpu.make_async_copy(
                all_ref.at[home, pl.ds(base, span)], out.at[pl.ds(r * span, span)], sem.at[r, half]
            )
            copy.start()
            copies.append(copy)
    for copy in copies:
        copy.wait()
    last = [
        pltpu.make_async_copy(down_ref, down_out, sem.at[0, 0]),
        pltpu.make_async_copy(up_ref, up_out, sem.at[0, 1]),
    ]
    for copy in last:
        copy.start()
    for copy in last:
        copy.wait()


def named(owner_table, adapter_ids, gathered, n_loc, span):
    n_req = adapter_ids.shape[1]
    smem = pl.BlockSpec(memory_space=pltpu.SMEM)
    hbm = pl.BlockSpec(memory_space=pltpu.HBM)
    out = jax.ShapeDtypeStruct((n_req * span, gathered.shape[-1]), BF)
    return pl.pallas_call(
        functools.partial(named_kernel, n_loc, span),
        out_shape=(out, out),
        in_specs=[smem, smem, hbm],
        out_specs=(hbm, hbm),
        scratch_shapes=[
            pltpu.VMEM(out.shape, BF),
            pltpu.VMEM(out.shape, BF),
            pltpu.SemaphoreType.DMA((n_req, 2)),
        ],
        cost_estimate=LIGHT,
        name="named_adapters",
    )(owner_table, adapter_ids, gathered)


def project_kernel(n_tp, cap, pool_dev, n_chunk, tp_ref, lens_ref, table_ref, *rest):
    hbm_refs, rest = rest[: 5 + 2 * n_tp], rest[5 + 2 * n_tp :]
    q_ref, k_ref, v_ref, pos_ref = rest[:4]
    all_refs = rest[4 : 4 + n_chunk]
    down, count, *held = rest[4 + n_chunk :]
    held, sem, sem_out = held[:-2], held[-2], held[-1]
    gain_ref, w_ref, up_ref, cos_ref, sin_ref, tok_ref = held
    tp = tp_ref[0]
    copies = []
    targets = list(held[:5]) + [tok_ref.at[k] for k in range(n_tp)]
    for k in range(n_tp):
        targets.append(down.at[lax.rem(tp - k + n_tp, n_tp)])
    for i in list(range(5, 5 + 2 * n_tp)) + list(range(5)):
        copy = pltpu.make_async_copy(hbm_refs[i], targets[i], sem.at[i])
        copy.start()
        copies.append(copy)
    _, rows, _ = tok_ref.shape
    width = q_ref.shape[1]
    n_low, dd = down.shape[1:]
    n_req = lens_ref.shape[1]
    rank = n_low // n_req // 2

    for g in range(count.shape[0]):
        count[g] = 0

    def place(p, carry):
        home = table_ref[0, p] // pool_dev
        seen = count[home]
        count[home] = seen + 1
        pos_ref[p] = home * cap + seen
        return carry

    lax.fori_loop(0, table_ref.shape[1], place, 0)

    for copy in copies:
        copy.wait()
    sub = all_refs[0].shape[1]
    stores = []
    for k in range(n_tp):
        for c in range(n_chunk):
            copy = pltpu.make_async_copy(
                tok_ref.at[k, pl.ds(c * sub, sub)],
                all_refs[c].at[lax.rem(tp - k + n_tp, n_tp)],
                sem_out.at[k, c],
            )
            copy.start()
            stores.append(copy)
    lane = lax.broadcasted_iota(jnp.int32, (1, 128), 1)
    first = jnp.bitwise_and(lane, HD - 1) < HD // 2

    def rope(u, cos, sin):
        parts = []
        for a in range(width // 128):
            part = u[:, a * 128 : (a + 1) * 128]
            other = jnp.where(
                first, pltpu.roll(part, 128 - HD // 2, 1), pltpu.roll(part, HD // 2, 1)
            )
            parts.append(part * cos + other * sin)
        return parts

    for k in range(n_tp):
        row0 = pl.multiple_of(lax.rem(tp - k + n_tp, n_tp) * rows, rows)
        x = tok_ref[k].astype(F32)
        inv = lax.rsqrt(jnp.mean(x * x, axis=1, keepdims=True) + 1e-05)
        normed = (x * inv * gain_ref[...].astype(F32)).astype(BF)
        low = jnp.zeros((rows, n_low), F32)
        for j in range(n_tp):
            low = low + lax.dot_general(
                normed[:, j * dd : (j + 1) * dd], down[j], (((1,), (1,)), ((), ())),
                preferred_element_type=F32,
            )
        row = row0 + lax.broadcasted_iota(jnp.int32, (rows, n_low), 0)
        col = lax.broadcasted_iota(jnp.int32, (rows, n_low), 1)
        request = jnp.zeros((rows, n_low), jnp.int32)
        end = jnp.int32(0)
        for r in range(n_req - 1):
            end = end + lens_ref[0, r]
            request = request + (row >= end).astype(jnp.int32)
        own = col // (2 * rank) == request
        kind = (col // rank) % 2
        deltas = []
        for kk in range(2):
            part = jnp.where(own & (kind == kk), low, 0.0).astype(BF)
            deltas.append(jnp.dot(part, up_ref[...], preferred_element_type=F32))
        cos = cos_ref[pl.ds(row0, rows), :]
        sin = sin_ref[pl.ds(row0, rows), :]
        q = jnp.dot(normed, w_ref[0], preferred_element_type=F32) + deltas[0]
        for a, part in enumerate(rope(q, cos, sin)):
            part = part.astype(BF).astype(F32) * (HD ** -0.5)
            q_ref[pl.ds(row0, rows), a * 128 : (a + 1) * 128] = part.astype(BF)
        kk = jnp.dot(normed, w_ref[1], preferred_element_type=F32)
        for a, part in enumerate(rope(kk, cos, sin)):
            k_ref[pl.ds(row0, rows), a * 128 : (a + 1) * 128] = part.astype(BF)
        v = jnp.dot(normed, w_ref[2], preferred_element_type=F32) + deltas[1]
        v_ref[pl.ds(row0, rows), :] = v.astype(BF)
    for copy in stores:
        copy.wait()


def project(
    tp, lens, table, gain, w_qkv, up, cos, sin, toks, downs, n_dp, cap, pool_dev, n_chunk
):
    n_tp = len(toks)
    sub = toks[0].shape[0] // n_chunk
    rows = toks[0].shape[0] * n_tp
    width = w_qkv.shape[2]
    smem = pl.BlockSpec(memory_space=pltpu.SMEM)
    vmem = pl.BlockSpec(memory_space=pltpu.VMEM)
    out = jax.ShapeDtypeStruct((rows, width), BF)
    return pl.pallas_call(
        functools.partial(project_kernel, n_tp, cap, pool_dev, n_chunk),
        out_shape=(
            out, out, out, jax.ShapeDtypeStruct((table.shape[1],), jnp.int32),
        )
        + (jax.ShapeDtypeStruct((n_tp, sub, toks[0].shape[1]), BF),) * n_chunk,
        in_specs=[smem] * 3 + [pl.BlockSpec(memory_space=pltpu.HBM)] * (5 + 2 * n_tp),
        out_specs=(vmem, vmem, vmem, smem) + (pl.BlockSpec(memory_space=pltpu.HBM),) * n_chunk,
        scratch_shapes=[
            pltpu.VMEM((n_tp,) + downs[0].shape, BF),
            pltpu.SMEM((n_dp,), jnp.int32),
        ]
        + [pltpu.VMEM(x.shape, x.dtype) for x in (gain, w_qkv, up, cos, sin)]
        + [
            pltpu.VMEM((n_tp,) + toks[0].shape, BF),
            pltpu.SemaphoreType.DMA((5 + 2 * n_tp,)),
            pltpu.SemaphoreType.DMA((n_tp, n_chunk)),
        ],
        compiler_params=pltpu.CompilerParams(vmem_limit_bytes=60 << 20),
        cost_estimate=LIGHT,
        name="project",
    )(tp, lens, table, gain, w_qkv, up, cos, sin, *toks, *downs)


def attend_kernel(
    group, per, n_chunk, lens_ref, counts_ref, pos_ref, bias_ref,
    q_ref, kn_ref, vn_ref, raw_ref, *rest
):
    out_refs = rest[:-9]
    kc, vc, knp, vnp, qbd, pairs, sbuf, wbuf, obuf = rest[-9:]
    page_len = kc.shape[1]
    width = q_ref.shape[1]
    rows = q_ref.shape[0]
    n_req = lens_ref.shape[1]
    back = knp.shape[0] - rows
    n_page = PAGES_REQ
    n_new = (back + TILE) // KCH

    row = lax.broadcasted_iota(jnp.int32, (2 * page_len, 2 * page_len), 0)
    col = lax.broadcasted_iota(jnp.int32, (2 * page_len, 2 * page_len), 1)
    src = jnp.where(row < page_len, 2 * row, 2 * row - (2 * page_len - 1))
    choose = (col == src).astype(F32).astype(BF)

    def unpack(slot):
        pages = [raw_ref[pos_ref[slot + i]] for i in range(BLK)]
        both = jnp.dot(
            choose, jnp.concatenate(pages, axis=1), preferred_element_type=F32
        ).astype(BF)
        for i in range(BLK):
            kc[slot + i] = both[:page_len, i * width : (i + 1) * width]
            vc[slot + i] = both[page_len:, i * width : (i + 1) * width]

    for slot in range(0, n_req * n_page, BLK):
        unpack(slot)

    knp[:back, :] = jnp.zeros((back, width), BF)
    vnp[:back, :] = jnp.zeros((back, width), BF)
    knp[back:, :] = kn_ref[...]
    vnp[back:, :] = vn_ref[...]

    lane = lax.broadcasted_iota(jnp.int32, (1, width), 1)
    lane_f = lax.broadcasted_iota(jnp.int32, (1, KCH), 1).astype(F32)
    delta = [bias_ref[0, group * per + a] - bias_ref[1, group * per + a] for a in range(per)]
    parts = [slice(a * TILE, (a + 1) * TILE) for a in range(per)]
    n_all = n_page + n_new

    for t in range(rows // TILE):
        qt = q_ref[t * TILE : (t + 1) * TILE, :].astype(F32)
        for a in range(per):
            mine = (lane >= a * HD) & (lane < (a + 1) * HD)
            qbd[t, parts[a], :] = jnp.where(mine, qt, 0.0).astype(BF)

    def list_pairs(r, carry):
        start, found = carry
        end = start + lens_ref[0, r]

        def add(t, found):
            pairs[0, found] = t
            pairs[1, found] = r
            pairs[2, found] = start
            return found + 1

        return end, lax.fori_loop(start // TILE, (end - 1) // TILE + 1, add, found)

    _, found = lax.fori_loop(0, n_req, list_pairs, (jnp.int32(0), jnp.int32(0)))

    def pair_body(i, carry):
        t, r, start = pairs[0, i], pairs[1, i], pairs[2, i]
        row0 = pl.multiple_of(t * TILE, TILE)
        live = counts_ref[0, r]
        end = start + lens_ref[0, r]
        offset = (live * page_len - start).astype(F32)
        start_f = start.astype(F32)
        row = (row0 + lax.broadcasted_iota(jnp.int32, (TILE, KCH), 0)).astype(F32)
        var_first = jnp.floor((row + offset + 0.5) * (1.0 / VARLEN)) * VARLEN

        def scores(keys):
            return lax.dot_general(
                qbd[t], keys, (((1,), (1,)), ((), ())), preferred_element_type=F32
            )

        first = r * n_page
        s_page = scores(kc[pl.ds(first, n_page)].reshape(n_page * page_len, width))
        s_new = scores(knp[pl.ds(row0, back + TILE), :])
        top = [None] * per
        for c in range(n_all):
            if c < n_page:
                dead = jnp.where(c < live, 0.0, NEG)
                same = var_first <= lane_f + c * page_len
            else:
                key_row = lane_f + (row0 - back + (c - n_page) * KCH).astype(F32)
                allowed = (key_row >= start_f) & (key_row <= row)
                same = var_first - offset <= key_row
            for a, p in enumerate(parts):
                if c < n_page:
                    v = s_page[p, c * KCH : (c + 1) * KCH]
                    v = v + jnp.where(same, delta[a] + dead, dead)
                else:
                    v = s_new[p, (c - n_page) * KCH : (c - n_page + 1) * KCH]
                    v = jnp.where(allowed, v + jnp.where(same, delta[a], 0.0), NEG)
                sbuf[c, p, :] = v
                top[a] = v if top[a] is None else jnp.maximum(top[a], v)
        peak = [jnp.broadcast_to(jnp.max(x, axis=1, keepdims=True), (TILE, KCH)) for x in top]
        total = [jnp.zeros((TILE, KCH), F32) for _ in parts]
        for c in range(n_all):
            for a, p in enumerate(parts):
                e = jnp.exp(sbuf[c, p, :] - peak[a])
                sbuf[c, p, :] = e
                total[a] = total[a] + e
        inverse = [
            jnp.broadcast_to(1.0 / jnp.sum(x, axis=1, keepdims=True), (TILE, KCH)) for x in total
        ]
        for c in range(n_all):
            for a, p in enumerate(parts):
                wbuf[p, c * KCH : (c + 1) * KCH] = (sbuf[c, p, :] * inverse[a]).astype(BF)
        o = jnp.dot(
            wbuf[:, : n_page * KCH],
            vc[pl.ds(first, n_page)].reshape(n_page * page_len, width),
            preferred_element_type=F32,
        ) + jnp.dot(
            wbuf[:, n_page * KCH :], vnp[pl.ds(row0, back + TILE), :],
            preferred_element_type=F32,
        )
        mixed = o[parts[0]]
        for a in range(1, per):
            mixed = jnp.where(lane >= a * HD, o[parts[a]], mixed)
        inside = (row >= start_f) & (row < end.astype(F32))
        obuf[t] = jnp.where(inside[:, :width], mixed, obuf[t])
        return carry

    lax.fori_loop(0, found, pair_body, 0)
    per_chunk = rows // n_chunk
    for t in range(rows // TILE):
        if n_chunk == 1:
            out_refs[0][t * TILE : (t + 1) * TILE, :] = obuf[t].astype(BF)
            continue
        sub = TILE // n_chunk
        for c in range(n_chunk):
            part = obuf[t, c * sub : (c + 1) * sub, :].astype(BF)
            if len(out_refs) == 1:
                base = c * per_chunk + t * sub
                out_refs[0][base : base + sub, :] = part
            else:
                out_refs[c][t * sub : (t + 1) * sub, :] = part


def attend(group, lanes, most, n_chunk, apart, lens, counts, pos, bias, q, kn, vn, raw):
    rows = q.shape[0]
    per = lanes // HD
    page_len = raw.shape[1] // 2
    slots = raw.shape[0]
    back = -(-most // KCH) * KCH
    n_all = PAGES_REQ + (back + TILE) // KCH
    n_out = n_chunk if apart else 1
    tiles = rows // TILE
    smem = pl.BlockSpec(memory_space=pltpu.SMEM)
    part = pl.BlockSpec((rows, lanes), lambda i: (0, group))
    return pl.pallas_call(
        functools.partial(attend_kernel, group, per, n_chunk),
        grid=(1,),
        out_shape=[jax.ShapeDtypeStruct((rows // n_out, lanes), BF)] * n_out,
        in_specs=[smem] * 4
        + [part] * 3
        + [pl.BlockSpec(raw.shape, lambda i: (0, 0, 0), pipeline_mode=pl.Buffered(1))],
        out_specs=[pl.BlockSpec((rows // n_out, lanes), lambda i: (0, 0))] * n_out,
        scratch_shapes=[
            pltpu.VMEM((slots, page_len, lanes), BF),
            pltpu.VMEM((slots, page_len, lanes), BF),
            pltpu.VMEM((back + rows, lanes), BF),
            pltpu.VMEM((back + rows, lanes), BF),
            pltpu.VMEM((tiles, per * TILE, lanes), BF),
            pltpu.SMEM((3, tiles + lens.shape[1]), jnp.int32),
            pltpu.VMEM((n_all, per * TILE, KCH), F32),
            pltpu.VMEM((per * TILE, n_all * KCH), BF),
            pltpu.VMEM((tiles, TILE, lanes), F32),
        ],
        compiler_params=pltpu.CompilerParams(vmem_limit_bytes=60 << 20),
        cost_estimate=LIGHT,
        name="attend",
    )(lens, counts, pos, bias, q, kn, vn, raw)


def partial_kernel(n_chunk, n_block, *refs):
    blocks, refs = refs[:n_block], refs[n_block:]
    w_ref, outs = refs[0], refs[1:]
    rows = outs[0].shape[0]
    for c in range(n_chunk):
        part = jnp.concatenate([b[c * rows : (c + 1) * rows, :] for b in blocks], axis=1)
        outs[c][...] = jnp.dot(part, w_ref[...], preferred_element_type=F32)


def partial(n_chunk, blocks, weight):
    vmem = pl.BlockSpec(memory_space=pltpu.VMEM)
    out = jax.ShapeDtypeStruct((blocks[0].shape[0] // n_chunk, weight.shape[1]), F32)
    return pl.pallas_call(
        functools.partial(partial_kernel, n_chunk, len(blocks)),
        out_shape=[out] * n_chunk,
        in_specs=[vmem] * (len(blocks) + 1),
        out_specs=[vmem] * n_chunk,
        compiler_params=pltpu.CompilerParams(vmem_limit_bytes=24 << 20),
        cost_estimate=LIGHT,
        name="partial",
    )(*blocks, weight)


def shift(value, axis, n, k):
    return lax.ppermute(value, axis, [(i, (i + k) % n) for i in range(n)])


def whole_weight(own, halves, dp, n_dp, n_group):
    twins = lax.ppermute(jnp.stack(halves), "dp", [(i, i ^ 1) for i in range(n_dp)])
    first = dp % 2 == 0
    lower = [jnp.where(first, h, twins[k]) for k, h in enumerate(halves)]
    upper = [jnp.where(first, twins[k], h) for k, h in enumerate(halves)]
    if n_group == 2:
        own_parts = jnp.split(own, 2)
        return [
            jnp.concatenate([mine] + part, axis=0)
            for mine, part in zip(own_parts, (lower, upper))
        ]
    both = [x for pair in zip(lower, upper) for x in pair]
    whole = jnp.concatenate([own] + both, axis=0)
    width, d_model = own.shape
    parts = whole.reshape(len(halves) + 1, n_group, width // n_group, d_model)
    return [parts[:, a].reshape(-1, d_model) for a in range(n_group)]


def per_device(
    tokens,
    attn_gain,
    ffn_gain,
    w_qkv,
    w_out,
    w_gateup,
    w_down,
    variate_bias,
    adapter_down,
    adapter_up,
    owner_table,
    lengths,
    adapter_ids,
    page_counts,
    page_table,
    cache_pool,
):
    n_tp = lax.axis_size("tensor")
    n_dp = lax.axis_size("dp")
    tp = lax.axis_index("tensor")
    dp = lax.axis_index("dp")
    me = dp.astype(jnp.int32).reshape(1)
    tp_id = tp.astype(jnp.int32).reshape(1)
    row_count, d_model = tokens.shape
    tok_total = row_count * n_tp
    width = w_out.shape[0]
    page_len = cache_pool.shape[1]
    pool_dev = cache_pool.shape[0]
    cap = max(1, page_table.shape[1] // n_dp)
    far_first = [k for k in range(1, n_tp)]
    lanes = min(width, 2 * HD)
    n_group = width // lanes
    slots = n_dp * cap
    dd = d_model // n_tp
    n_loc, _, rank, _ = adapter_down.shape
    n_chunk = max(1, row_count // CHUNK)
    sub = row_count // n_chunk
    span = 2 * rank

    toks = [tokens] + [shift(tokens, "tensor", n_tp, k) for k in far_first]

    down_part = lax.dynamic_slice_in_dim(adapter_down, tp * dd, dd, 3).reshape(n_loc * span, dd)
    names = jnp.concatenate([page_table // pool_dev, page_table % pool_dev], axis=0).astype(BF)
    names = jnp.pad(names, ((0, 14), (0, dd - names.shape[1])))
    payload = jnp.concatenate([down_part, adapter_up.reshape(n_loc * span, width), names], axis=0)
    gathered = lax.all_gather(payload, "dp", axis=0)
    asked = gathered[:, 2 * n_loc * span : 2 * n_loc * span + 2, : page_table.shape[1]]
    picked = pick(me, asked.astype(jnp.int32), cache_pool, n_dp, cap, lanes)
    send = lax.optimization_barrier((picked[0], toks[1:-1]))[0]
    fetched = [lax.all_to_all(send, "dp", split_axis=0, concat_axis=0, tiled=True)]

    own_half = lax.dynamic_slice_in_dim(w_out, (dp % 2) * (width // 2), width // 2, 0)
    gathered, lengths_b = lax.optimization_barrier((gathered, lengths, send))[:2]
    down_named, up_named = named(owner_table, adapter_ids, gathered, n_loc, span)
    downs = [down_named] + [shift(down_named, "tensor", n_tp, k) for k in far_first]

    _, position = token_layout(lengths_b[0], page_counts[0], page_len, tok_total)
    index = jnp.arange(2 * HD, dtype=jnp.int32)
    frequency = 10000.0 ** (-2.0 * (index % (HD // 2)).astype(F32) / HD)
    angles = (position % VARLEN).astype(F32)[:, None] * frequency[None, :]
    sign = jnp.where(index % HD < HD // 2, -1.0, 1.0).astype(F32)
    query, new_keys, new_values, buffer_pos, *all_tokens = project(
        tp_id, lengths, page_table, attn_gain.reshape(1, d_model), w_qkv, up_named,
        jnp.cos(angles), jnp.sin(angles) * sign[None, :], toks, downs, n_dp, cap, pool_dev, n_chunk,
    )
    own_half = lax.optimization_barrier((own_half, downs[1:]))[0]
    halves = [shift(own_half, "tensor", n_tp, k) for k in far_first]
    for a in range(1, n_group):
        send = lax.optimization_barrier((picked[a], fetched[-1], query, halves[:1]))[0]
        fetched.append(lax.all_to_all(send, "dp", split_axis=0, concat_axis=0, tiled=True))
    fetched = [f.reshape(slots, 2 * page_len, lanes) for f in fetched]


    def mixed(blocks, a):
        return jnp.dot(
            jnp.concatenate(blocks, axis=1), w_whole[a], preferred_element_type=F32
        )

    def attended(a, q, apart):
        return attend(
            a, lanes, 2 * TILE, n_chunk, apart, lengths, page_counts, buffer_pos, variate_bias,
            q, new_keys, new_values, fetched[a],
        )

    early = []
    w_whole = None
    for a in range(n_group - 1):
        mix = attended(a, query, False)[0]
        if w_whole is None:
            mix, halves = lax.optimization_barrier((mix, halves))
            w_whole = whole_weight(w_out, halves, dp, n_dp, n_group)
        blocks = [mix] + [shift(mix, "tensor", n_tp, k) for k in far_first]
        query, w_whole = lax.optimization_barrier((query, w_whole))
        early.append(blocks)
    if w_whole is None:
        w_whole = whole_weight(w_out, halves, dp, n_dp, n_group)
    last = attended(n_group - 1, query, True)
    early, last, w_whole = lax.optimization_barrier((early, last, w_whole))
    bases = [partial(n_chunk, early[a], w_whole[a]) for a in range(n_group - 1)]
    outs = []
    pieces = None
    late = []
    for c in range(n_chunk):
        own = last[c]
        if late:
            own = lax.optimization_barrier((own, bases))[0]
        late.append([own] + [shift(own, "tensor", n_tp, k) for k in far_first])
    for c in range(n_chunk):
        blocks = late[c]
        if pieces is not None:
            blocks = lax.optimization_barrier((blocks, pieces))[0]
        residual = all_tokens[c].reshape(n_tp * sub, d_model).astype(F32)
        for part in bases:
            residual = residual + part[c]
        residual = residual + mixed(blocks, n_group - 1)
        ffn_in = normalize(residual, ffn_gain).astype(BF)
        gate_up = jnp.einsum("td,kdf->ktf", ffn_in, w_gateup, preferred_element_type=F32)
        hidden = (jax.nn.silu(gate_up[0]) * gate_up[1]).astype(BF)
        down = jnp.dot(hidden, w_down, preferred_element_type=F32).reshape(n_tp, sub, d_model)
        total = lax.dynamic_index_in_dim(down, tp, 0, False)
        total = total + lax.dynamic_index_in_dim(
            residual.reshape(n_tp, sub, d_model), tp, 0, False
        )
        down = down.astype(BF)
        pieces = [lax.dynamic_index_in_dim(down, (tp + k) % n_tp, 0, False) for k in far_first]
        for k, piece in zip(far_first, pieces):
            total = total + shift(piece, "tensor", n_tp, k).astype(F32)
        outs.append(total.astype(BF))
    return jnp.concatenate(outs, axis=0)


def solution(mesh):
    return jax.shard_map(
        per_device,
        mesh=mesh,
        in_specs=(
            P(("dp", "tensor"), None),
            P(),
            P(),
            P(None, None, "tensor"),
            P("tensor", None),
            P(None, None, "tensor"),
            P("tensor", None),
            P(None, "tensor"),
            P("dp", None, None, None),
            P("dp", None, None, "tensor"),
            P(),
            P("dp", None),
            P("dp", None),
            P("dp", None),
            P("dp", None),
            P("dp", None, None, "tensor"),
        ),
        out_specs=P(("dp", "tensor"), None),
        check_vma=False,
    )
```
